32 devices in a mesh: ctx: 16 (over z, y, core), fsdp: 2 (over x).
Axes of the slice: x: 2, y: 2, z: 4, core: 2. Of those that a mesh axis runs over, the one named last changes fastest.
Arguments:
- enc_input: float32 [4096, 1472], P(('ctx', 'fsdp')), may hold values from -6 to 6
- dec_input: float32 [4096, 1472], P(('ctx', 'fsdp')), may hold values from -6 to 6
- teacher: float32 [4096, 1472], P(('ctx', 'fsdp')), may hold values from -6 to 6
- valid_mask: int32 [4096], P(('ctx', 'fsdp')), may hold values from 0 to 1, as said below
- doc_lengths: int32 [16], replicated, may hold values from 1 to 1024, 4096 in all
- enc_buckets: int32 [2048], replicated, may hold values from 0 to 31
- dec_buckets: int32 [2048], replicated, may hold values from 0 to 31
- enc_norm_attn: float32 [1472], replicated, may hold values from 0.5 to 1.5
- enc_query: bfloat16 [1472, 384], P(None, 'fsdp'), may hold values from -0.01953125 to 0.01953125
- enc_key: bfloat16 [1472, 384], P(None, 'fsdp'), may hold values from -0.15625 to 0.15625
- enc_value: bfloat16 [1472, 384], P(None, 'fsdp'), may hold values from -0.15625 to 0.15625
- enc_out_proj: bfloat16 [384, 1472], P('fsdp'), may hold values from -1.25 to 1.25
- enc_norm_ff: float32 [1472], replicated, may hold values from 0.5 to 1.5
- enc_gate: bfloat16 [1472, 3584], P(None, 'fsdp'), may hold values from -0.15625 to 0.15625
- enc_up: bfloat16 [1472, 3584], P(None, 'fsdp'), may hold values from -0.15625 to 0.15625
- enc_down: bfloat16 [3584, 1472], P('fsdp'), may hold values from -0.09375 to 0.09375
- enc_rel_bias: float32 [32, 6], replicated, may hold values from -4 to 4
- dec_norm_self: float32 [1472], replicated, may hold values from 0.5 to 1.5
- dec_query: bfloat16 [1472, 384], P(None, 'fsdp'), may hold values from -0.01953125 to 0.01953125
- dec_key: bfloat16 [1472, 384], P(None, 'fsdp'), may hold values from -0.15625 to 0.15625
- dec_value: bfloat16 [1472, 384], P(None, 'fsdp'), may hold values from -0.15625 to 0.15625
- dec_out_proj: bfloat16 [384, 1472], P('fsdp'), may hold values from -1.25 to 1.25
- dec_norm_cross: float32 [1472], replicated, may hold values from 0.5 to 1.5
- cross_query: bfloat16 [1472, 384], P(None, 'fsdp'), may hold values from -0.01953125 to 0.01953125
- cross_key: bfloat16 [1472, 384], P(None, 'fsdp'), may hold values from -0.15625 to 0.15625
- cross_value: bfloat16 [1472, 384], P(None, 'fsdp'), may hold values from -0.15625 to 0.15625
- cross_out_proj: bfloat16 [384, 1472], P('fsdp'), may hold values from -1.25 to 1.25
- dec_norm_ff: float32 [1472], replicated, may hold values from 0.5 to 1.5
- dec_gate: bfloat16 [1472, 3584], P(None, 'fsdp'), may hold values from -0.15625 to 0.15625
- dec_up: bfloat16 [1472, 3584], P(None, 'fsdp'), may hold values from -0.15625 to 0.15625
- dec_down: bfloat16 [3584, 1472], P('fsdp'), may hold values from -0.09375 to 0.09375
- dec_rel_bias: float32 [32, 6], replicated, may hold values from -4 to 4
Outputs:
- teacher_loss: float32 [], replicated
- dec_output: float32 [4096, 1472], P(('ctx', 'fsdp'))
- grad_enc_input: float32 [4096, 1472], P(('ctx', 'fsdp'))
- grad_dec_input: float32 [4096, 1472], P(('ctx', 'fsdp'))
- grad_enc_norm_attn: float32 [1472], replicated
- grad_enc_query: float32 [1472, 384], P(None, ('ctx', 'fsdp'))
- grad_enc_key: float32 [1472, 384], P(None, ('ctx', 'fsdp'))
- grad_enc_value: float32 [1472, 384], P(None, ('ctx', 'fsdp'))
- grad_enc_out_proj: float32 [384, 1472], P(('ctx', 'fsdp'))
- grad_enc_norm_ff: float32 [1472], replicated
- grad_enc_gate: float32 [1472, 3584], P(None, ('ctx', 'fsdp'))
- grad_enc_up: float32 [1472, 3584], P(None, ('ctx', 'fsdp'))
- grad_enc_down: float32 [3584, 1472], P(('ctx', 'fsdp'))
- grad_enc_rel_bias: float32 [32, 6], replicated
- grad_dec_norm_self: float32 [1472], replicated
- grad_dec_query: float32 [1472, 384], P(None, ('ctx', 'fsdp'))
- grad_dec_key: float32 [1472, 384], P(None, ('ctx', 'fsdp'))
- grad_dec_value: float32 [1472, 384], P(None, ('ctx', 'fsdp'))
- grad_dec_out_proj: float32 [384, 1472], P(('ctx', 'fsdp'))
- grad_dec_norm_cross: float32 [1472], replicated
- grad_cross_query: float32 [1472, 384], P(None, ('ctx', 'fsdp'))
- grad_cross_key: float32 [1472, 384], P(None, ('ctx', 'fsdp'))
- grad_cross_value: float32 [1472, 384], P(None, ('ctx', 'fsdp'))
- grad_cross_out_proj: float32 [384, 1472], P(('ctx', 'fsdp'))
- grad_dec_norm_ff: float32 [1472], replicated
- grad_dec_gate: float32 [1472, 3584], P(None, ('ctx', 'fsdp'))
- grad_dec_up: float32 [1472, 3584], P(None, ('ctx', 'fsdp'))
- grad_dec_down: float32 [3584, 1472], P(('ctx', 'fsdp'))
- grad_dec_rel_bias: float32 [32, 6], replicated
The draws below stay inside these ranges and needn't reach their ends.
Inputs may be any that keep to these rules, and one draw needn't show every extreme that they name: `doc_lengths`: the lengths sum to 4096; the documents lie end to end from position 0, and one has exactly 1024 tokens. `valid_mask`: each block of 128 tokens begins with a 1.
All inputs are finite; a program needn't handle non-finite values.
Results may differ from the reference program's by a relative error of at most 0.04.
Values may be sent and summed in bfloat16 or wider, within the bound.
A program may use at most 448 MiB of HBM per device.

```python
import math
import jax
import jax.numpy as jnp
import numpy as np
from jax import lax

D = 1472
H = 6
DH = 64
INNER = 384
FF = 3584
NB = 32
TOK_DEV = 128
DOC_MAX = 1024
REACH = 8
TOKENS = 4096
NDOC = 16


def draw_valid_mask(key, part):
    positions = jnp.arange(TOKENS, dtype=jnp.int32)
    threshold = 256 + 512 * positions // TOKENS
    drawn = jax.random.randint(key, (TOKENS,), 0, 1024, dtype=jnp.int32)
    chosen = (drawn < threshold).astype(jnp.int32)
    return jnp.where(positions % TOK_DEV == 0, 1, chosen).astype(jnp.int32)


def set_ends(array, stream_key, smallest, high):
    extent = array.shape
    index_at = [jax.random.randint(jax.random.fold_in(stream_key, axis), (), 0, extent[axis]) for axis in range(len(extent))]
    array = array.at[tuple(index_at)].set(smallest)
    longest = extent.index(max(extent))
    index_at[longest] = (index_at[longest] + 1) % extent[longest]
    return array.at[tuple(index_at)].set(high)


def block_levels(key, shape, split, least, top_value):
    def one(dim, shards_of):
        steps = jax.random.uniform(jax.random.fold_in(jax.random.fold_in(key, 6), dim), (shards_of,), jnp.float32, least / len(split), top_value / len(split))
        return jnp.repeat(jnp.exp(steps), shape[dim] // shards_of).reshape((-1,) + (1,) * (len(shape) - dim - 1))

    factor_of = one(*split[0])
    for cut in split[1:]:
        factor_of = factor_of * one(*cut)
    return factor_of


def length_profile(number_of, total, limit, slope):
    portions = [(1 << 20) // math.isqrt(standing ** slope) + 1 for standing in range(2, number_of + 1)]
    surplus, given = total - limit - (number_of - 1), [1] * (number_of - 1)
    while surplus > 0:
        candidates = [i for i in range(number_of - 1) if given[i] < limit]
        pool, left = sum([portions[i] for i in candidates]), surplus
        for i in candidates:
            extra = min(limit - given[i], max(1, left * portions[i] // pool), surplus)
            given[i] = given[i] + extra
            surplus = surplus - extra
    return np.array([limit] + given)


def ragged(own_key, amount, total, reach, slope):
    if amount == 2:
        one = jax.random.randint(own_key, (), max(1, total - reach), min(reach, total - 1) + 1)
        return jnp.stack([one, total - one])
    sizes = jnp.asarray(length_profile(amount, total, reach, slope), jnp.int32)
    pairs = (amount - 1) // 2
    donor, taker = sizes[1:1 + 2 * pairs:2], sizes[2:2 + 2 * pairs:2]
    room = jnp.minimum(donor - 1, reach - taker)
    shifted = jax.random.randint(jax.random.fold_in(own_key, 1), (pairs,), 0, 1 << 20) % (room + 1)
    sizes = sizes.at[1:1 + 2 * pairs:2].set(donor - shifted).at[2:2 + 2 * pairs:2].set(taker + shifted)
    return sizes[jax.random.permutation(jax.random.fold_in(own_key, 2), amount)]


def scatter_about(key, extent, spread, limit, cuts=(), held_as=jnp.bfloat16):
    values = jax.random.normal(key, extent, jnp.float32) * spread
    if len(cuts) > 0:
        values = block_levels(key, extent, cuts, -0.22, 0.18) * values
    return jnp.clip(values, min=-limit, max=limit).astype(held_as)


def setup_inputs(seed: int = 0) -> dict:
    seeds = jax.random.split(jax.random.key(seed), 33)
    enc_input = scatter_about(seeds[0], (TOKENS, D), 1.0, 6.0, ((0, 32),), jnp.float32)
    dec_input = scatter_about(seeds[1], (TOKENS, D), 1.0, 6.0, ((0, 32),), jnp.float32)
    teacher = scatter_about(seeds[2], (TOKENS, D), 1.0, 6.0, ((0, 32),), jnp.float32)
    valid_mask = draw_valid_mask(jax.random.fold_in(seeds[32], 71), 0)
    doc_lengths = ragged(seeds[4], NDOC, TOKENS, DOC_MAX, 2).astype(jnp.int32)
    enc_buckets = set_ends(jax.random.randint(seeds[5], (2 * DOC_MAX,), 0, NB), jax.random.fold_in(seeds[5], 1), 0, NB - 1).astype(jnp.int32)
    dec_buckets = set_ends(jax.random.randint(seeds[6], (2 * DOC_MAX,), 0, NB), jax.random.fold_in(seeds[6], 1), 0, NB - 1).astype(jnp.int32)
    enc_norm_attn = jnp.clip(1.0 + 0.1 * jax.random.normal(seeds[7], (D,), jnp.float32), 0.5, 1.5)
    enc_query = scatter_about(seeds[8], (D, INNER), (D * DH) ** -0.5, 0.01953125, ((1, 2),))
    enc_key = scatter_about(seeds[9], (D, INNER), D ** -0.5, 0.15625, ((1, 2),))
    enc_value = scatter_about(seeds[10], (D, INNER), D ** -0.5, 0.15625, ((1, 2),))
    enc_out_proj = scatter_about(seeds[11], (INNER, D), (INNER // 16) ** -0.5, 1.25, ((0, 2),))
    enc_norm_ff = jnp.clip(1.0 + 0.1 * jax.random.normal(seeds[12], (D,), jnp.float32), 0.5, 1.5)
    enc_gate = scatter_about(seeds[13], (D, FF), D ** -0.5, 0.15625, ((1, 2),))
    enc_up = scatter_about(seeds[14], (D, FF), D ** -0.5, 0.15625, ((1, 2),))
    enc_down = scatter_about(seeds[15], (FF, D), FF ** -0.5, 0.09375, ((0, 2),))
    enc_rel_bias = scatter_about(seeds[16], (NB, H), 1.0, 4.0, (), jnp.float32)
    dec_norm_self = jnp.clip(1.0 + 0.1 * jax.random.normal(seeds[17], (D,), jnp.float32), 0.5, 1.5)
    dec_query = scatter_about(seeds[18], (D, INNER), (D * DH) ** -0.5, 0.01953125, ((1, 2),))
    dec_key = scatter_about(seeds[19], (D, INNER), D ** -0.5, 0.15625, ((1, 2),))
    dec_value = scatter_about(seeds[20], (D, INNER), D ** -0.5, 0.15625, ((1, 2),))
    dec_out_proj = scatter_about(seeds[21], (INNER, D), (INNER // 16) ** -0.5, 1.25, ((0, 2),))
    dec_norm_cross = jnp.clip(1.0 + 0.1 * jax.random.normal(seeds[22], (D,), jnp.float32), 0.5, 1.5)
    cross_query = scatter_about(seeds[23], (D, INNER), (D * DH) ** -0.5, 0.01953125, ((1, 2),))
    cross_key = scatter_about(seeds[24], (D, INNER), D ** -0.5, 0.15625, ((1, 2),))
    cross_value = scatter_about(seeds[25], (D, INNER), D ** -0.5, 0.15625, ((1, 2),))
    cross_out_proj = scatter_about(seeds[26], (INNER, D), (INNER // 16) ** -0.5, 1.25, ((0, 2),))
    dec_norm_ff = jnp.clip(1.0 + 0.1 * jax.random.normal(seeds[27], (D,), jnp.float32), 0.5, 1.5)
    dec_gate = scatter_about(seeds[28], (D, FF), D ** -0.5, 0.15625, ((1, 2),))
    dec_up = scatter_about(seeds[29], (D, FF), D ** -0.5, 0.15625, ((1, 2),))
    dec_down = scatter_about(seeds[30], (FF, D), FF ** -0.5, 0.09375, ((0, 2),))
    dec_rel_bias = scatter_about(seeds[31], (NB, H), 1.0, 4.0, (), jnp.float32)
    return {"enc_input": enc_input, "dec_input": dec_input, "teacher": teacher, "valid_mask": valid_mask, "doc_lengths": doc_lengths, "enc_buckets": enc_buckets, "dec_buckets": dec_buckets, "enc_norm_attn": enc_norm_attn, "enc_query": enc_query, "enc_key": enc_key, "enc_value": enc_value, "enc_out_proj": enc_out_proj, "enc_norm_ff": enc_norm_ff, "enc_gate": enc_gate, "enc_up": enc_up, "enc_down": enc_down, "enc_rel_bias": enc_rel_bias, "dec_norm_self": dec_norm_self, "dec_query": dec_query, "dec_key": dec_key, "dec_value": dec_value, "dec_out_proj": dec_out_proj, "dec_norm_cross": dec_norm_cross, "cross_query": cross_query, "cross_key": cross_key, "cross_value": cross_value, "cross_out_proj": cross_out_proj, "dec_norm_ff": dec_norm_ff, "dec_gate": dec_gate, "dec_up": dec_up, "dec_down": dec_down, "dec_rel_bias": dec_rel_bias}


epsilon = 1e-06
highest = lax.Precision.HIGHEST

@jax.custom_vjp
def low(v):
    return lax.optimization_barrier(v.astype(jnp.bfloat16)).astype(jnp.float32)

@jax.custom_vjp
def low_back(v):
    return v

def low_keep(v):
    return (low(v), None)

def low_pass(kept, grad):
    return (grad,)

def back_keep(v):
    return (v, None)

def back_low(kept, grad):
    return (low(grad),)
low.defvjp(low_keep, low_pass)
low_back.defvjp(back_keep, back_low)

def matmul(left, right):
    return jnp.dot(left, right, precision=highest, preferred_element_type=jnp.float32)

def root_norm(inputs, gain):
    return inputs * lax.rsqrt(lax.optimization_barrier(jnp.mean(inputs * inputs, axis=-1, keepdims=True)) + epsilon) * gain

def attention(queries, keys, values, doc_ids, bias_line, causal):
    margin = REACH * TOK_DEV
    window = (2 * REACH + 1) * TOK_DEV
    head_size = queries.shape[1] // H
    padded_keys = jnp.pad(keys, ((margin, margin), (0, 0)))
    padded_values = jnp.pad(values, ((margin, margin), (0, 0)))
    padded_docs = jnp.pad(doc_ids, (margin, margin), constant_values=-1)

    def one_block(offset):
        query_rows = lax.dynamic_slice_in_dim(queries, offset, TOK_DEV, 0).reshape(TOK_DEV, H, head_size)
        key_rows = lax.dynamic_slice_in_dim(padded_keys, offset, window, 0).reshape(window, H, head_size)
        value_rows = lax.dynamic_slice_in_dim(padded_values, offset, window, 0).reshape(window, H, head_size)
        query_doc = lax.dynamic_slice_in_dim(doc_ids, offset, TOK_DEV, 0)
        key_doc = lax.dynamic_slice_in_dim(padded_docs, offset, window, 0)
        query_pos = offset + jnp.arange(TOK_DEV, dtype=jnp.int32)
        key_pos = offset - margin + jnp.arange(window, dtype=jnp.int32)
        scores = jnp.einsum('qhd,khd->hqk', query_rows, key_rows, precision=highest)
        if bias_line is not None:
            index_rows = jnp.clip(key_pos[None, :] - query_pos[:, None] + DOC_MAX, 0, 2 * DOC_MAX - 1)
            scores = scores + jnp.take(bias_line, index_rows, axis=1)
        scores = low_back(scores)
        allowed = key_doc[None, :] == query_doc[:, None]
        if causal:
            allowed = allowed & (key_pos[None, :] <= query_pos[:, None])
        scores = jnp.where(allowed[None], scores, -1e+30)
        weights = jax.nn.softmax(scores, axis=-1)
        mixed = jnp.einsum('hqk,khd->qhd', low(weights), value_rows, precision=highest)
        return mixed.reshape(TOK_DEV, H * head_size)
    offsets = jnp.arange(TOKENS // TOK_DEV, dtype=jnp.int32) * TOK_DEV
    return lax.map(jax.checkpoint(one_block), offsets).reshape(TOKENS, queries.shape[1])

def self_block(source, gain, w_query, w_key, w_value, w_out, doc_ids, bias_line, causal):
    normed = low(root_norm(source, gain))
    queries = low_back(low(matmul(normed, w_query)))
    keys = low_back(low(matmul(normed, w_key)))
    values = low_back(low(matmul(normed, w_value)))
    attended = low_back(low(attention(queries, keys, values, doc_ids, bias_line, causal)))
    return source + low_back(matmul(attended, w_out))

def cross_block(source, memory, gain, w_query, w_key, w_value, w_out, doc_ids):
    normed = low(root_norm(source, gain))
    memory_low = low(memory)
    queries = low_back(low(matmul(normed, w_query)))
    keys = low_back(low(matmul(memory_low, w_key)))
    values = low_back(low(matmul(memory_low, w_value)))
    attended = low_back(low(attention(queries, keys, values, doc_ids, None, False)))
    return source + low_back(matmul(attended, w_out))

def feed_block(source, gain, w_gate, w_up, w_down):
    normed = low(root_norm(source, gain))
    gating = low_back(matmul(normed, w_gate))
    upward = low_back(matmul(normed, w_up))
    hidden = low_back(low(jax.nn.gelu(gating, approximate=True) * upward))
    return source + low_back(matmul(hidden, w_down))

def reference(enc_input, dec_input, teacher, valid_mask, doc_lengths, enc_buckets, dec_buckets, enc_norm_attn, enc_query, enc_key, enc_value, enc_out_proj, enc_norm_ff, enc_gate, enc_up, enc_down, enc_rel_bias, dec_norm_self, dec_query, dec_key, dec_value, dec_out_proj, dec_norm_cross, cross_query, cross_key, cross_value, cross_out_proj, dec_norm_ff, dec_gate, dec_up, dec_down, dec_rel_bias):
    params = (enc_norm_attn.astype(jnp.float32), enc_query.astype(jnp.float32), enc_key.astype(jnp.float32), enc_value.astype(jnp.float32), enc_out_proj.astype(jnp.float32), enc_norm_ff.astype(jnp.float32), enc_gate.astype(jnp.float32), enc_up.astype(jnp.float32), enc_down.astype(jnp.float32), enc_rel_bias.astype(jnp.float32), dec_norm_self.astype(jnp.float32), dec_query.astype(jnp.float32), dec_key.astype(jnp.float32), dec_value.astype(jnp.float32), dec_out_proj.astype(jnp.float32), dec_norm_cross.astype(jnp.float32), cross_query.astype(jnp.float32), cross_key.astype(jnp.float32), cross_value.astype(jnp.float32), cross_out_proj.astype(jnp.float32), dec_norm_ff.astype(jnp.float32), dec_gate.astype(jnp.float32), dec_up.astype(jnp.float32), dec_down.astype(jnp.float32), dec_rel_bias.astype(jnp.float32))
    starts = jnp.cumsum(doc_lengths) - doc_lengths
    positions = jnp.arange(TOKENS, dtype=jnp.int32)
    doc_ids = (lax.optimization_barrier(jnp.sum((positions[:, None] >= starts[None, :]).astype(jnp.int32), axis=1)) - 1).astype(jnp.int32)

    def network(enc_x, dec_x, weights):
        e_norm_one, e_query, e_key, e_value, e_out, e_norm_two, e_gate, e_up, e_down, e_bias, d_norm_one, d_query, d_key, d_value, d_out, d_norm_two, c_query, c_key, c_value, c_out, d_norm_three, d_gate, d_up, d_down, d_bias = weights
        enc_line = jnp.take(e_bias, enc_buckets, axis=0).T
        dec_line = jnp.take(d_bias, dec_buckets, axis=0).T
        enc_mid = self_block(enc_x, e_norm_one, e_query, e_key, e_value, e_out, doc_ids, enc_line, False)
        enc_output = feed_block(enc_mid, e_norm_two, e_gate, e_up, e_down)
        dec_mid = self_block(dec_x, d_norm_one, d_query, d_key, d_value, d_out, doc_ids, dec_line, True)
        dec_cross = cross_block(dec_mid, enc_output, d_norm_two, c_query, c_key, c_value, c_out, doc_ids)
        return feed_block(dec_cross, d_norm_three, d_gate, d_up, d_down)
    dec_output, pullback = jax.vjp(network, enc_input, dec_input, params)
    mask_float = valid_mask.astype(jnp.float32)
    difference = dec_output - teacher
    valid_total = jnp.sum(mask_float)
    teacher_loss = jnp.sum(mask_float * lax.optimization_barrier(jnp.sum(difference * difference, axis=-1))) / (D * valid_total)
    cotangent = difference * mask_float[:, None] * (TOKENS / valid_total)
    grad_enc, grad_dec, grads = pullback(cotangent)
    return (teacher_loss, dec_output, grad_enc, grad_dec, grads[0], grads[1], grads[2], grads[3], grads[4], grads[5], grads[6], grads[7], grads[8], grads[9], grads[10], grads[11], grads[12], grads[13], grads[14], grads[15], grads[16], grads[17], grads[18], grads[19], grads[20], grads[21], grads[22], grads[23], grads[24])
```

```python
import functools

import jax
import jax.numpy as jnp
from jax import lax
from jax.experimental import pallas as pl
from jax.experimental.pallas import tpu as pltpu
from jax.sharding import PartitionSpec as P

D = 1472
HEAD = 64
REACH_PAIRS = 4
WIN = 3 * REACH_PAIRS
epsilon = 1e-06
far_below = -1e30
bf16 = jnp.bfloat16
f32 = jnp.float32
MESH = pl.DeviceIdType.MESH
VMEM_LIMIT = 52 * 1024 * 1024


def dot(left, right, left_dim=1, right_dim=0):
    return lax.dot_general(
        left, right, (((left_dim,), (right_dim,)), ((), ())), preferred_element_type=f32
    )


def swap(value):
    return lax.ppermute(value, "fsdp", [(0, 1), (1, 0)])


def flipped(index, bit):
    return index + bit - 2 * bit * lax.rem(index // bit, 2)


def window_kernel(flags, swaps, *refs):
    arrays = len(flags)
    total = arrays + swaps
    ins, outs = refs[:total], refs[total : 2 * total]
    local_sem, send_sem, recv_sem, swap_send, swap_recv = refs[2 * total :]
    R = REACH_PAIRS
    ctx = lax.axis_index("ctx")
    fsdp = lax.axis_index("fsdp")
    groups = lax.axis_size("ctx") // R
    group = ctx // R
    place = lax.rem(ctx, R)
    near, far = flipped(place, 1), flipped(place, 2)
    dev_near, dev_far = group * R + near, group * R + far
    dev_up, dev_down = ctx + R, ctx - R
    has_up, has_down = group < groups - 1, group > 0
    barrier = pltpu.get_barrier_semaphore()

    def greet(device):
        pl.semaphore_signal(barrier, inc=1, device_id=(device, fsdp), device_id_type=MESH)

    greet(dev_near)
    greet(dev_far)
    if swaps:
        pl.semaphore_signal(barrier, inc=1, device_id=(ctx, 1 - fsdp), device_id_type=MESH)

    @pl.when(has_up)
    def _():
        greet(dev_up)

    @pl.when(has_down)
    def _():
        greet(dev_down)

    greeted = 2 + (1 if swaps else 0)
    pl.semaphore_wait(barrier, greeted + has_up.astype(jnp.int32) + has_down.astype(jnp.int32))

    def copies(number, source_slot, slot, device, use=lambda f: True, part=None):
        made = []
        for k, (below, above, split) in enumerate(flags):
            if not use(flags[k]):
                continue
            rows = ins[k].shape[0]
            cut = rows if not split else (rows // 2 if not (below and above) else 3 * rows // 8)
            where = {None: (0, rows), 0: (0, cut), 1: (cut, rows)}[part]
            if where[0] == where[1]:
                continue
            span = pl.ds(where[0], where[1] - where[0])
            source = ins[k] if source_slot is None else outs[k].at[source_slot, span]
            made.append(
                pltpu.make_async_remote_copy(
                    src_ref=source,
                    dst_ref=outs[k].at[slot, span],
                    send_sem=send_sem.at[k, number],
                    recv_sem=recv_sem.at[k, number],
                    device_id=(device, fsdp),
                    device_id_type=MESH,
                )
            )
        return made

    def start(made):
        for copy in made:
            copy.start()

    def arrived(made):
        for copy in made:
            copy.wait_recv()

    def left(made):
        for copy in made:
            copy.wait_send()

    below = lambda flag: flag[0]
    above = lambda flag: flag[1]
    to_up = copies(0, None, place, dev_up, below)
    to_down = copies(1, None, 2 * R + place, dev_down, above)
    to_far = copies(2, None, R + place, dev_far)
    to_near = copies(3, None, R + place, dev_near)
    far_low = copies(4, place, place, dev_far, below, 0)
    far_high = copies(5, 2 * R + place, 2 * R + place, dev_far, above, 0)
    up_far = copies(6, R + far, far, dev_up, below, 1)
    down_far = copies(7, R + far, 2 * R + far, dev_down, above, 1)
    near_low = copies(8, place, place, dev_near, below)
    near_high = copies(9, 2 * R + place, 2 * R + place, dev_near, above)
    near_far = copies(10, R + far, R + far, dev_near)
    near_far_low = copies(11, far, far, dev_near, below)
    near_far_high = copies(12, 2 * R + far, 2 * R + far, dev_near, above)
    own = [
        pltpu.make_async_copy(ins[k], outs[k].at[R + place], local_sem.at[k])
        for k in range(arrays)
    ]

    across = [
        pltpu.make_async_remote_copy(
            src_ref=ins[arrays + k],
            dst_ref=outs[arrays + k],
            send_sem=swap_send.at[k],
            recv_sem=swap_recv.at[k],
            device_id=(ctx, 1 - fsdp),
            device_id_type=MESH,
        )
        for k in range(swaps)
    ]

    @pl.when(has_up)
    def _():
        start(to_up)

    @pl.when(has_down)
    def _():
        start(to_down)

    start(to_far)
    start(to_near)
    start(across)
    start(own)
    arrived(to_far)

    @pl.when(has_up)
    def _():
        start(up_far)

    @pl.when(has_down)
    def _():
        start(down_far)

    start(near_far)

    @pl.when(has_down)
    def _():
        arrived(to_up)
        start(far_low)
        start(near_low)

    @pl.when(has_up)
    def _():
        arrived(to_down)
        start(far_high)
        start(near_high)

    @pl.when(has_down)
    def _():
        arrived(far_low)
        arrived(up_far)
        start(near_far_low)

    @pl.when(has_up)
    def _():
        arrived(far_high)
        arrived(down_far)
        start(near_far_high)

    arrived(to_near)
    arrived(near_far)

    @pl.when(has_down)
    def _():
        arrived(near_low)
        arrived(near_far_low)
        left(far_low)
        left(near_low)
        left(near_far_low)
        left(to_down)
        left(down_far)

    @pl.when(has_up)
    def _():
        arrived(near_high)
        arrived(near_far_high)
        left(far_high)
        left(near_high)
        left(near_far_high)
        left(to_up)
        left(up_far)

    left(to_far)
    left(to_near)
    left(near_far)
    for copy in own + across:
        copy.wait()


BOTH, BELOW, ABOVE = (True, True), (True, False), (False, True)


def window_gather(number, pairs, swapped=()):
    values = [value for value, _ in pairs]
    flags = tuple(
        sides + (value.dtype == bf16 and value.shape[0] % 128 == 0,) for value, sides in pairs
    )
    count, swaps = len(values), len(swapped)
    vmem = pl.BlockSpec(memory_space=pltpu.VMEM)
    specs = [vmem] * count + [pl.BlockSpec(memory_space=pl.ANY)] * swaps
    return pl.pallas_call(
        functools.partial(window_kernel, flags, swaps),
        out_shape=[jax.ShapeDtypeStruct((WIN,) + v.shape, v.dtype) for v in values]
        + [jax.ShapeDtypeStruct(v.shape, v.dtype) for v in swapped],
        in_specs=specs,
        out_specs=specs,
        scratch_shapes=[
            pltpu.SemaphoreType.DMA((count,)),
            pltpu.SemaphoreType.DMA((count, 13)),
            pltpu.SemaphoreType.DMA((count, 13)),
            pltpu.SemaphoreType.DMA((max(swaps, 1),)),
            pltpu.SemaphoreType.DMA((max(swaps, 1),)),
        ],
        compiler_params=pltpu.CompilerParams(
            collective_id=number, has_side_effects=True, vmem_limit_bytes=VMEM_LIMIT
        ),
        cost_estimate=pl.CostEstimate(flops=0, bytes_accessed=50_000_000, transcendentals=0),
        name="window_gather",
    )(*values, *swapped)


def total_kernel(rounds, x_ref, o_ref, mine, theirs, send_sem, recv_sem):
    ctx = lax.axis_index("ctx")
    fsdp = lax.axis_index("fsdp")
    partners = [(ctx, 1 - fsdp)] + [(flipped(ctx, 1 << k), fsdp) for k in range(rounds - 1)]
    barrier = pltpu.get_barrier_semaphore()
    for partner in partners:
        pl.semaphore_signal(barrier, inc=1, device_id=partner, device_id_type=MESH)
    pl.semaphore_wait(barrier, rounds)
    mine[0] = x_ref[...]
    for k, partner in enumerate(partners):
        copy = pltpu.make_async_remote_copy(
            src_ref=mine.at[k],
            dst_ref=theirs.at[k],
            send_sem=send_sem.at[k],
            recv_sem=recv_sem.at[k],
            device_id=partner,
            device_id_type=MESH,
        )
        copy.start()
        copy.wait()
        added = mine[k] + theirs[k]
        if k + 1 < rounds:
            mine[k + 1] = added
        else:
            o_ref[...] = added


def total_over_devices(value, number, ctx_size):
    rounds = ctx_size.bit_length()
    padded = -(-value.shape[0] // 1024) * 1024
    wide = jnp.pad(value, (0, padded - value.shape[0])).reshape(8, padded // 8)
    vmem = pl.BlockSpec(memory_space=pltpu.VMEM)
    made = pl.pallas_call(
        functools.partial(total_kernel, rounds),
        out_shape=jax.ShapeDtypeStruct(wide.shape, f32),
        in_specs=[vmem],
        out_specs=vmem,
        scratch_shapes=[
            pltpu.VMEM((rounds,) + wide.shape, f32),
            pltpu.VMEM((rounds,) + wide.shape, f32),
            pltpu.SemaphoreType.DMA((rounds,)),
            pltpu.SemaphoreType.DMA((rounds,)),
        ],
        compiler_params=pltpu.CompilerParams(collective_id=number, has_side_effects=True),
        cost_estimate=pl.CostEstimate(flops=0, bytes_accessed=30_000_000, transcendentals=0),
        name="total_over_devices",
    )(wide)
    return made.reshape(-1)[: value.shape[0]]


def head_masks(width):
    lanes = lax.broadcasted_iota(jnp.int32, (1, width), 1)
    return [
        (lanes >= h * HEAD) & (lanes < (h + 1) * HEAD) for h in range(width // HEAD)
    ]


def only_head(value, mask):
    return jnp.where(mask, value, jnp.zeros_like(value))


def toeplitz(line_ref, head, block, rows):
    start = pl.multiple_of(block * rows, rows)
    segment = line_ref[pl.ds(head, 1), pl.ds(start, 2 * rows)]
    spread = jnp.broadcast_to(segment, (rows, 2 * rows))
    return pltpu.roll(spread, rows + 1, 1, stride=1, stride_axis=0)[:, :rows]


def halves(value, op):
    half = value.shape[1] // 2
    return op(value[:, :half], value[:, half:])


def forward_kernel(biased, bounds, q_ref, kv_ref, lo_ref, hi_ref, *rest):
    if biased:
        line_ref, rest = rest[0], rest[1:]
    o_ref, l_ref, s_ref, m_ref, sum_ref, acc_ref = rest
    rows, width = q_ref.shape
    heads = width // HEAD
    masks = head_masks(width)
    first, last, key_base = bounds[0], bounds[1], bounds[2]
    lo, hi = lo_ref[...], hi_ref[...]
    m_ref[...] = jnp.full_like(m_ref, far_below)
    sum_ref[...] = jnp.zeros_like(sum_ref)
    acc_ref[...] = jnp.zeros_like(acc_ref)
    q = q_ref[...]

    def scores(block, carry):
        keys = kv_ref[block, :, :width]
        key_pos = key_base + block * rows + lax.broadcasted_iota(jnp.int32, (rows, rows), 1)
        allowed = (key_pos >= lo) & (key_pos <= hi)
        for h in range(heads):
            s = dot(only_head(q, masks[h]), keys, 1, 1)
            if biased:
                s = s + toeplitz(line_ref, h, block, rows)
            s = jnp.where(allowed, s, far_below)
            s_ref[block, h] = s
            m_ref[h] = jnp.maximum(m_ref[h], halves(s, jnp.maximum))
        return carry

    lax.fori_loop(first, last + 1, scores, 0)
    tops = [jnp.max(m_ref[h], axis=1, keepdims=True) for h in range(heads)]

    def mix(block, carry):
        values = kv_ref[block, :, width:]
        total = None
        for h in range(heads):
            p = jnp.exp(s_ref[block, h] - tops[h])
            sum_ref[h] += halves(p, jnp.add)
            part = dot(p.astype(bf16), only_head(values, masks[h]))
            total = part if total is None else total + part
        acc_ref[...] += total
        return carry

    lax.fori_loop(first, last + 1, mix, 0)
    scale = jnp.zeros((rows, width), f32)
    lanes = lax.broadcasted_iota(jnp.int32, (rows, 128), 1)
    logs = jnp.zeros((rows, 128), f32)
    for h in range(heads):
        total = jnp.sum(sum_ref[h], axis=1, keepdims=True)
        scale = jnp.where(masks[h], 1.0 / total, scale)
        logs = jnp.where(lanes == h, tops[h] + jnp.log(total), logs)
    o_ref[...] = acc_ref[...] * scale
    l_ref[...] = logs


def query_kernel(biased, bounds, q_ref, kv_ref, lo_ref, hi_ref, da_ref, l_ref, delta_ref, *rest):
    if biased:
        line_ref, dq_ref, gline_ref, acc_ref = rest
        gline_ref[...] = jnp.zeros_like(gline_ref)
    else:
        dq_ref, acc_ref = rest
    rows, width = q_ref.shape
    heads = width // HEAD
    masks = head_masks(width)
    first, last, key_base = bounds[0], bounds[1], bounds[2]
    lo, hi = lo_ref[...], hi_ref[...]
    acc_ref[...] = jnp.zeros_like(acc_ref)
    q, da = q_ref[...], da_ref[...]
    logs = [l_ref[:, h : h + 1] for h in range(heads)]
    deltas = [delta_ref[:, h : h + 1] for h in range(heads)]

    def step(block, carry):
        keys = kv_ref[block, :, :width]
        values = kv_ref[block, :, width:]
        key_pos = key_base + block * rows + lax.broadcasted_iota(jnp.int32, (rows, rows), 1)
        allowed = (key_pos >= lo) & (key_pos <= hi)
        total = None
        for h in range(heads):
            s = dot(only_head(q, masks[h]), keys, 1, 1)
            if biased:
                s = s + toeplitz(line_ref, h, block, rows)
            p = jnp.exp(jnp.where(allowed, s - logs[h], far_below))
            dp = dot(only_head(da, masks[h]), values, 1, 1)
            ds = (p * (dp - deltas[h])).astype(bf16)
            part = dot(ds, only_head(keys, masks[h]))
            total = part if total is None else total + part
            if biased:
                folded = jnp.concatenate([ds.astype(f32), jnp.zeros((rows, rows), f32)], axis=1)
                half = rows // 2
                while half >= 1:
                    folded = pltpu.roll(folded[:half], half, 1) + folded[half:]
                    half //= 2
                start = pl.multiple_of(block * rows, rows)
                gline_ref[pl.ds(h, 1), pl.ds(start, 2 * rows)] += folded
        acc_ref[...] += total
        return carry

    lax.fori_loop(first, last + 1, step, 0)
    dq_ref[...] = acc_ref[...].astype(bf16)


def key_kernel(biased, bounds, kv_ref, qd_ref, stat_ref, lo_ref, hi_ref, *rest):
    if biased:
        line_ref, rest = rest[0], rest[1:]
    dk_ref, dv_ref, dk_acc, dv_acc = rest
    rows = kv_ref.shape[0]
    width = kv_ref.shape[1] // 2
    heads = width // HEAD
    masks = head_masks(width)
    first, last, query_base = bounds[0], bounds[1], bounds[2]
    lo, hi = lo_ref[...], hi_ref[...]
    dk_acc[...] = jnp.zeros_like(dk_acc)
    dv_acc[...] = jnp.zeros_like(dv_acc)
    keys, values = kv_ref[:, :width], kv_ref[:, width:]

    def step(block, carry):
        q = qd_ref[block, :, :width]
        da = qd_ref[block, :, width:]
        query_pos = query_base + block * rows + lax.broadcasted_iota(jnp.int32, (rows, rows), 1)
        allowed = (query_pos >= lo) & (query_pos <= hi)
        total_k = None
        total_v = None
        for h in range(heads):
            s = dot(only_head(keys, masks[h]), q, 1, 1)
            if biased:
                s = s + toeplitz(line_ref, h, block, rows)
            p = jnp.exp(jnp.where(allowed, s - stat_ref[block, h : h + 1, :], far_below))
            dp = dot(only_head(values, masks[h]), da, 1, 1)
            ds = (p * (dp - stat_ref[block, heads + h : heads + h + 1, :])).astype(bf16)
            part_k = dot(ds, only_head(q, masks[h]))
            part_v = dot(p.astype(bf16), only_head(da, masks[h]))
            total_k = part_k if total_k is None else total_k + part_k
            total_v = part_v if total_v is None else total_v + part_v
        dk_acc[...] += total_k
        dv_acc[...] += total_v
        return carry

    lax.fori_loop(first, last + 1, step, 0)
    dk_ref[...] = dk_acc[...].astype(bf16)
    dv_ref[...] = dv_acc[...].astype(bf16)


def local_call(kernel, out_shape, scratch, name, bounds, *values):
    vmem = pl.BlockSpec(memory_space=pltpu.VMEM)
    smem = pl.BlockSpec(memory_space=pltpu.SMEM)
    return pl.pallas_call(
        kernel,
        out_shape=out_shape,
        in_specs=[smem] + [vmem] * len(values),
        out_specs=jax.tree.map(lambda _: vmem, out_shape),
        scratch_shapes=scratch,
        compiler_params=pltpu.CompilerParams(vmem_limit_bytes=VMEM_LIMIT),
        cost_estimate=pl.CostEstimate(
            flops=1_000_000_000, bytes_accessed=18_000_000, transcendentals=0
        ),
        name=name,
    )(bounds, *values)


def attend(q, kv_window, bounds, lo, hi, line):
    rows, width = q.shape
    heads = width // HEAD
    biased = line is not None
    out, logs = local_call(
        functools.partial(forward_kernel, biased),
        [
            jax.ShapeDtypeStruct((rows, width), f32),
            jax.ShapeDtypeStruct((rows, 128), f32),
        ],
        [
            pltpu.VMEM((WIN, heads, rows, rows), f32),
            pltpu.VMEM((heads, rows, rows // 2), f32),
            pltpu.VMEM((heads, rows, rows // 2), f32),
            pltpu.VMEM((rows, width), f32),
        ],
        "attend_forward",
        bounds,
        q,
        kv_window,
        lo,
        hi,
        *([line] if biased else []),
    )
    return out, logs


def attend_queries(q, kv_window, bounds, lo, hi, da, logs, delta, line):
    rows, width = q.shape
    biased = line is not None
    shapes = [jax.ShapeDtypeStruct((rows, width), bf16)]
    if biased:
        shapes.append(jax.ShapeDtypeStruct(line.shape, f32))
    return local_call(
        functools.partial(query_kernel, biased),
        shapes,
        [pltpu.VMEM((rows, width), f32)],
        "attend_queries",
        bounds,
        q,
        kv_window,
        lo,
        hi,
        da,
        logs,
        delta,
        *([line] if biased else []),
    )


def attend_keys(kv, qd_window, stat_window, bounds, lo, hi, line):
    rows = kv.shape[0]
    width = kv.shape[1] // 2
    biased = line is not None
    return local_call(
        functools.partial(key_kernel, biased),
        [jax.ShapeDtypeStruct((rows, width), bf16)] * 2,
        [pltpu.VMEM((rows, width), f32)] * 2,
        "attend_keys",
        bounds,
        kv,
        qd_window,
        stat_window,
        lo,
        hi,
        *([line] if biased else []),
    )


def inverse_root(inputs):
    return lax.rsqrt(jnp.mean(inputs * inputs, axis=-1, keepdims=True) + epsilon)


def root_norm(inputs, gain):
    return inputs * inverse_root(inputs) * gain


def norm_backward(inputs, gain, grad):
    inverse = inverse_root(inputs)
    scaled = grad * gain
    along = jnp.mean(inputs * scaled, axis=-1, keepdims=True)
    grad_inputs = inverse * scaled - inputs * (inverse * inverse * inverse) * along
    return grad_inputs, jnp.sum(grad * inputs * inverse, axis=0)


def gated_unit(gating, upward):
    return jax.nn.gelu(gating, approximate=True) * upward


def body(
    enc_input,
    dec_input,
    teacher,
    valid_mask,
    doc_lengths,
    enc_buckets,
    dec_buckets,
    enc_norm_attn,
    enc_query,
    enc_key,
    enc_value,
    enc_out_proj,
    enc_norm_ff,
    enc_gate,
    enc_up,
    enc_down,
    enc_rel_bias,
    dec_norm_self,
    dec_query,
    dec_key,
    dec_value,
    dec_out_proj,
    dec_norm_cross,
    cross_query,
    cross_key,
    cross_value,
    cross_out_proj,
    dec_norm_ff,
    dec_gate,
    dec_up,
    dec_down,
    dec_rel_bias,
):
    ctx = lax.axis_index("ctx")
    side = lax.axis_index("fsdp")
    ctx_size = lax.axis_size("ctx")
    own_rows = enc_input.shape[0]
    rows = 2 * own_rows
    width = enc_query.shape[1]
    heads = width // HEAD
    place = lax.rem(ctx, REACH_PAIRS)
    core_bit, far_bit = lax.rem(place, 2), place // 2

    def arranged(bit, mine, other, axis=0):
        first = bit == 0
        return jnp.concatenate(
            [jnp.where(first, mine, other), jnp.where(first, other, mine)], axis=axis
        )

    def ordered(mine, other, axis=0):
        return arranged(side, mine, other, axis)

    def pick(value, index, axis):
        return lax.dynamic_index_in_dim(value, index, axis, keepdims=False)

    def flip(value, bit):
        return lax.ppermute(value, "ctx", [(i, i ^ bit) for i in range(ctx_size)])

    def own(value):
        return lax.dynamic_slice_in_dim(value, side * own_rows, own_rows, 0)

    def others(value):
        return lax.dynamic_slice_in_dim(value, (1 - side) * own_rows, own_rows, 0)

    def summed(partial):
        return partial + swap(partial.astype(bf16)).astype(f32)

    def summed_own(partial):
        return own(partial) + swap(others(partial).astype(bf16)).astype(f32)

    def tie(value, *before):
        return lax.optimization_barrier((value, before))[0]

    count = doc_lengths.shape[0]
    order = jnp.arange(count, dtype=jnp.int32)
    starts = jnp.sum(
        jnp.where(order[None, :] < order[:, None], doc_lengths[None, :], 0), axis=1
    )
    ends = starts + doc_lengths
    positions = ctx * rows + jnp.arange(rows, dtype=jnp.int32)[:, None]
    doc_lo = jnp.max(jnp.where(starts[None, :] <= positions, starts[None, :], 0), axis=1, keepdims=True)
    doc_hi = (
        jnp.min(
            jnp.where(ends[None, :] > positions, ends[None, :], ctx_size * rows),
            axis=1,
            keepdims=True,
        )
        - 1
    )
    base_block = ctx - place - REACH_PAIRS
    first_block = doc_lo[0, 0] // rows - base_block
    last_block = doc_hi[rows - 1, 0] // rows - base_block
    own_block = REACH_PAIRS + place
    base_pos = base_block * rows
    bounds_both = jnp.stack([first_block, last_block, base_pos])
    bounds_below = jnp.stack([first_block, own_block, base_pos])
    bounds_above = jnp.stack([own_block, last_block, base_pos])

    reach = enc_buckets.shape[0] // 2
    line_len = (WIN + 1) * rows
    pad_lo, pad_hi = reach, reach + rows
    line_start = (reach + 1 - rows) + pad_lo - rows * (REACH_PAIRS + place)
    reverse_start = (reach - rows) + pad_lo - rows * (REACH_PAIRS + place)

    def lines(rel_bias, buckets):
        hot = (
            buckets[:, None] == jnp.arange(rel_bias.shape[0], dtype=jnp.int32)[None, :]
        ).astype(f32)
        mine = lax.dynamic_slice_in_dim(rel_bias, side * heads, heads, 1)
        line = lax.dot_general(
            mine, hot, (((0,), (1,)), ((), ())), precision=lax.Precision.HIGHEST
        )
        padded = jnp.pad(line, ((0, 8 - heads), (pad_lo, pad_hi)))
        backward = jnp.pad(line[:, ::-1], ((0, 8 - heads), (pad_lo, pad_hi)))
        return (
            hot,
            lax.dynamic_slice_in_dim(padded, line_start, line_len, 1),
            lax.dynamic_slice_in_dim(backward, reverse_start, line_len, 1),
        )

    enc_hot, enc_line, enc_back = lines(enc_rel_bias, enc_buckets)
    dec_hot, dec_line, dec_back = lines(dec_rel_bias, dec_buckets)

    def bucket_grads(hot, grad_line):
        padded = jnp.zeros((heads, 2 * reach + pad_lo + pad_hi), f32)
        padded = lax.dynamic_update_slice_in_dim(padded, grad_line[:heads], line_start, 1)
        cropped = padded[:, pad_lo : pad_lo + 2 * reach]
        grads = lax.dot_general(
            hot, cropped, (((0,), (1,)), ((), ())), precision=lax.Precision.HIGHEST
        )
        whole = jnp.zeros((hot.shape[1], 2 * heads), f32)
        return lax.dynamic_update_slice_in_dim(whole, grads, side * heads, 1)

    group_list = [
        list(range(g, g + REACH_PAIRS)) for g in range(0, ctx_size, REACH_PAIRS)
    ]

    def group_gather(value):
        return lax.all_gather(value, "ctx", axis=0, tiled=True, axis_index_groups=group_list)

    low = ctx_size // 8

    def route_start(*values):
        columns = values[0].shape[0] // ctx_size
        split = jnp.stack(values).reshape(len(values), low, 2, 2, 2, columns, -1)
        return pick(split, far_bit, 2), flip(pick(split, 1 - far_bit, 2), 2)

    def route_end(mine, other):
        half = jnp.stack([mine, other])
        kept = pick(half, core_bit, 3)
        arrived = flip(pick(half, 1 - core_bit, 3), 1)
        by_core = [jnp.where(core_bit == 0, a, b) for a, b in ((kept, arrived), (arrived, kept))]
        by_far = [
            [jnp.where(far_bit == 0, c[i], c[1 - i]) for c in by_core] for i in range(2)
        ]
        return jnp.concatenate([by_far[0][0], by_far[0][1], by_far[1][0], by_far[1][1]], axis=-1)

    def weight_part(selected, source):
        return dot(selected, source, selected.ndim - 1, 0)

    low_bits = (ctx_size // 8).bit_length() - 1
    low_bit = lax.rem(ctx // REACH_PAIRS, 2)

    def first_leaving(routed, source):
        split = routed.reshape((routed.shape[0], low // 2, 2) + routed.shape[2:])
        return weight_part(pick(split, 1 - low_bit, 2), source).astype(bf16)

    def after_first(routed, source, arrived):
        split = routed.reshape((routed.shape[0], low // 2, 2) + routed.shape[2:])
        return (weight_part(pick(split, low_bit, 2), source) + arrived.astype(f32)).astype(bf16)

    def after_low(part):
        for k in range(1, low_bits):
            step = REACH_PAIRS << k
            bit = lax.rem(ctx // step, 2)
            split = part.reshape((part.shape[0], part.shape[1] // 2, 2) + part.shape[2:])
            arrived = flip(pick(split, 1 - bit, 2), step)
            part = (pick(split, bit, 2).astype(f32) + arrived.astype(f32)).astype(bf16)
        return pick(part[:, 0], side, 1), pick(part[:, 0], 1 - side, 1)

    same_side = side == ctx // (ctx_size // 2)

    def last_start(staying, arrived):
        mine = jnp.where(same_side, staying, arrived)
        return mine, flip(jnp.where(same_side, arrived, staying), ctx_size // 2)

    def last_end(mine, arrived):
        total = mine.astype(f32) + arrived.astype(f32)
        return total.reshape(-1, total.shape[-1])

    def parity_of_whole(*pairs):
        stack = jnp.stack([ordered(mine, other) for mine, other in pairs])
        split = stack.reshape(len(pairs), ctx_size, 2, stack.shape[1] // (2 * ctx_size), -1)
        return pick(split, side, 2)

    def exchanged_parity(*values):
        stack = jnp.stack(values)
        split = stack.reshape(len(values), ctx_size // 2, 2, stack.shape[1] // ctx_size, -1)
        return ordered(pick(split, side, 2), swap(pick(split, 1 - side, 2)), 1)

    def scatter(parts):
        count = sum(part.shape[0] for part, _ in parts)
        columns = parts[0][0].shape[2]
        before, stacked = 0, []
        for part, _ in parts:
            after = count - before - part.shape[0]
            stacked.append(jnp.pad(part, ((before, after),) + ((0, 0),) * 3))
            before += part.shape[0]
        left = jnp.concatenate(stacked, axis=3).transpose(1, 0, 2, 3)
        left = left.reshape(ctx_size * count * columns, -1)
        whole = dot(left, jnp.concatenate([source for _, source in parts], axis=0)).astype(bf16)
        return lax.psum_scatter(whole, "ctx", scatter_dimension=0, tiled=True)

    def project(normed, source, w_query, w_key, w_value):
        q = dot(normed, w_query).astype(bf16)
        kv = jnp.concatenate([dot(source, w_key), dot(source, w_value)], axis=1).astype(bf16)
        return q, kv

    enc_arrived = swap(enc_input.astype(bf16))
    dec_arrived = swap(tie(dec_input, enc_input).astype(bf16))
    cross_key_other = swap(tie(cross_key, enc_arrived))
    enc_pair = ordered(enc_input, enc_arrived.astype(f32))
    dec_pair = ordered(dec_input, dec_arrived.astype(f32))
    enc_normed = root_norm(enc_pair, enc_norm_attn).astype(bf16)
    dec_normed = root_norm(dec_pair, dec_norm_self).astype(bf16)
    enc_q, enc_kv = project(enc_normed, enc_normed, enc_query, enc_key, enc_value)
    dec_q, dec_kv = project(dec_normed, dec_normed, dec_query, dec_key, dec_value)
    teacher_low = jnp.pad(
        jnp.concatenate([teacher.T, valid_mask.astype(f32)[None]], axis=0).astype(bf16),
        ((0, 15), (0, 0)),
    )
    enc_window, dec_window, teacher_other, enc_out_other = window_gather(
        1, [(enc_kv, BOTH), (tie(dec_kv, cross_key_other), BELOW)], [teacher_low, enc_out_proj]
    )

    enc_o, enc_logs = attend(enc_q, enc_window, bounds_both, doc_lo, doc_hi, enc_line)
    enc_attended = enc_o.astype(bf16)
    enc_att_other = swap(enc_attended)
    dec_o, dec_logs = attend(
        tie(dec_q, enc_attended), dec_window, bounds_below, doc_lo, positions, dec_line
    )
    branch = dot(enc_attended, enc_out_proj) + dot(enc_att_other, enc_out_other)
    enc_mid = enc_pair + tie(branch, dec_o)
    dec_out_other = swap(tie(dec_out_proj, enc_att_other))

    def feed_forward(ffn_in, w_gate, w_up):
        gating = dot(w_gate, ffn_in, 0, 1)
        upward = dot(w_up, ffn_in, 0, 1)
        return gating, upward, gated_unit(gating, upward).astype(bf16)

    enc_ffn_in = root_norm(enc_mid, enc_norm_ff).astype(bf16)
    enc_ffn_all = group_gather(enc_ffn_in)
    enc_gating, enc_upward, enc_hidden = feed_forward(enc_ffn_in, enc_gate, enc_up)
    partial = dot(enc_hidden, enc_down, 0, 0)
    branch = summed(tie(partial, dec_out_other))
    enc_hidden_route = route_start(tie(enc_hidden, partial))

    dec_attended = tie(dec_o.astype(bf16), partial)
    dec_att_other = swap(dec_attended)
    dec_mid = (
        dec_pair + dot(dec_attended, dec_out_proj) + dot(dec_att_other, dec_out_other)
    )
    cross_normed = root_norm(dec_mid, dec_norm_cross).astype(bf16)
    cross_q = dot(cross_normed, cross_query).astype(bf16)
    memory = (enc_mid + tie(branch, cross_q)).astype(bf16)
    cross_kv = jnp.concatenate(
        [dot(memory, cross_key), dot(memory, cross_value)], axis=1
    ).astype(bf16)
    cross_window, cross_out_other = window_gather(2, [(cross_kv, BOTH)], [cross_out_proj])
    cross_o, cross_logs = attend(cross_q, cross_window, bounds_both, doc_lo, doc_hi, None)
    cross_attended = cross_o.astype(bf16)
    cross_att_other = swap(cross_attended)
    cross_query_other = swap(tie(cross_query, cross_att_other))
    enc_hidden_routed = route_end(*tie(enc_hidden_route, cross_o))
    dec_cross = (
        dec_mid
        + dot(cross_attended, cross_out_proj)
        + dot(tie(cross_att_other, enc_hidden_routed), cross_out_other)
    )
    dec_ffn_in = root_norm(dec_cross, dec_norm_ff).astype(bf16)
    dec_ffn_all = group_gather(dec_ffn_in)
    dec_gating, dec_upward, dec_hidden = feed_forward(dec_ffn_in, dec_gate, dec_up)
    partial = dot(dec_hidden, dec_down, 0, 0)
    branch = summed(tie(partial, cross_query_other))
    dec_hidden_route = route_start(tie(dec_hidden, partial))
    teacher_arrived = teacher_other.T.astype(f32)
    teacher_pair = ordered(teacher, teacher_arrived[:, :D])
    mask_pair = ordered(valid_mask.astype(f32)[:, None], teacher_arrived[:, D : D + 1])
    dec_output = dec_cross + branch

    difference = dec_output - teacher_pair
    grad_seed = difference * mask_pair
    loss_part = jnp.sum(own(grad_seed * difference))
    valid_part = jnp.sum(valid_mask.astype(f32))

    def feed_backward(grad_branch, gating, upward, w_gate, w_up, w_down):
        grad_hidden = dot(w_down, grad_branch, 1, 1).astype(bf16).astype(f32)
        unit_back = jax.vjp(gated_unit, gating, upward)[1]
        grad_gating, grad_upward = unit_back(grad_hidden)
        grad_gating = grad_gating.astype(bf16)
        grad_upward = grad_upward.astype(bf16)
        partial = dot(grad_gating, w_gate, 0, 1) + dot(grad_upward, w_up, 0, 1)
        return grad_gating, grad_upward, partial

    def attention_start(grad, q, out, logs, w_out):
        grad_branch = grad.astype(bf16)
        da = dot(grad_branch, w_out, 1, 1).astype(bf16)
        delta = jnp.sum((da.astype(f32) * out).reshape(rows, heads, HEAD), axis=2)
        stats = jnp.concatenate(
            [logs[:, :heads].T, delta.T, jnp.zeros((8 - 2 * heads, rows), f32)], axis=0
        )
        delta_wide = jnp.pad(delta, ((0, 0), (0, 128 - heads)))
        return grad_branch, da, delta_wide, jnp.concatenate([q, da], axis=1), stats

    dec_branch = grad_seed.astype(bf16)
    dec_branch_all = group_gather(dec_branch)
    grad_gating, grad_upward, partial = feed_backward(
        dec_branch, dec_gating, dec_upward, dec_gate, dec_up, dec_down
    )
    grad_ffn_in = summed(partial)
    dec_gu_route = route_start(*tie((grad_gating, grad_upward), partial))
    dec_hidden_routed = route_end(*tie(dec_hidden_route, partial))
    grad_ffn_in = tie(grad_ffn_in, dec_gu_route[0], dec_hidden_routed)
    part, g_dec_norm_ff = norm_backward(dec_cross, dec_norm_ff, grad_ffn_in)
    grad_cross = grad_seed + part

    cross_branch, da, delta_wide, qd, stats = attention_start(
        grad_cross, cross_q, cross_o, cross_logs, cross_out_proj
    )
    qd_window, stat_window, cross_value_other = window_gather(
        3, [(qd, BOTH), (stats, BOTH)], [cross_value.T]
    )
    cross_dk, cross_dv = attend_keys(
        cross_kv, qd_window, stat_window, bounds_both, doc_lo, doc_hi, None
    )
    dkv_other = swap(jnp.concatenate([cross_dk, cross_dv], axis=1))
    dk_other, dv_other = dkv_other[:, :width], dkv_other[:, width:]
    dec_gu_routed = route_end(*tie(dec_gu_route, cross_dk))
    dec_ffn_all, dec_branch_all = tie((dec_ffn_all, dec_branch_all), cross_dk)
    dec_gu_leaving = first_leaving(dec_gu_routed, dec_ffn_all)
    dec_down_leaving = first_leaving(dec_hidden_routed, dec_branch_all)
    grad_memory = dot(cross_dk, cross_key, 1, 1) + dot(cross_dv, cross_value, 1, 1)
    dk_other, dv_other = tie((dk_other, dv_other), dec_gu_leaving, dec_down_leaving, grad_memory)
    grad_memory = (
        grad_memory
        + dot(dk_other, cross_key_other, 1, 1)
        + dot(dv_other, cross_value_other, 1, 0)
    )
    dec_gu_arrived = flip(dec_gu_leaving, REACH_PAIRS)
    dec_down_arrived = flip(dec_down_leaving, REACH_PAIRS)

    enc_out_branch = grad_memory.astype(bf16)
    enc_branch_all = group_gather(enc_out_branch)
    grad_gating, grad_upward, partial = feed_backward(
        enc_out_branch, enc_gating, enc_upward, enc_gate, enc_up, enc_down
    )
    grad_ffn_in = summed(partial)

    (cross_dq,) = attend_queries(
        tie(cross_q, partial), cross_window, bounds_both, doc_lo, doc_hi, da, cross_logs, delta_wide, None
    )
    dq_other = swap(cross_dq)
    enc_gu_route = route_start(*tie((grad_gating, grad_upward), cross_dq))
    grad_normed = dot(cross_dq, cross_query, 1, 1)
    grad_ffn_in = tie(grad_ffn_in, enc_gu_route[0], grad_normed)
    part, g_enc_norm_ff = norm_backward(enc_mid, enc_norm_ff, grad_ffn_in)
    grad_enc_mid = grad_memory + part
    enc_branch, enc_da, enc_delta, enc_qd, enc_stats = attention_start(
        grad_enc_mid, enc_q, enc_o, enc_logs, enc_out_proj
    )
    grad_normed = grad_normed + dot(tie(dq_other, grad_ffn_in), cross_query_other, 1, 1)
    part, g_dec_norm_cross = norm_backward(dec_mid, dec_norm_cross, grad_normed)
    grad_mid = grad_cross + part
    self_branch, self_da, self_delta, self_qd, self_stats = attention_start(
        grad_mid, dec_q, dec_o, dec_logs, dec_out_proj
    )
    dec_gu_arrived, dec_down_arrived = tie((dec_gu_arrived, dec_down_arrived), self_qd, enc_qd)
    dec_gu_kept, dec_gu_sent = after_low(after_first(dec_gu_routed, dec_ffn_all, dec_gu_arrived))
    dec_down_kept, dec_down_sent = after_low(
        after_first(dec_hidden_routed, dec_branch_all, dec_down_arrived)
    )
    (
        enc_qd_window,
        enc_stat_window,
        self_qd_window,
        self_stat_window,
        dec_gu_sent,
        dec_down_sent,
    ) = window_gather(
        4,
        [(enc_qd, BOTH), (enc_stats, BOTH), (self_qd, ABOVE), (self_stats, ABOVE)],
        [dec_gu_sent, dec_down_sent],
    )
    dec_gu_last = last_start(dec_gu_kept, dec_gu_sent)
    dec_down_last = last_start(dec_down_kept, dec_down_sent)
    enc_gu_routed = route_end(*tie(enc_gu_route, enc_qd_window))
    enc_gu_leaving = first_leaving(enc_gu_routed, enc_ffn_all)
    enc_down_leaving = first_leaving(enc_hidden_routed, tie(enc_branch_all, enc_qd_window))
    enc_gu_arrived = flip(enc_gu_leaving, REACH_PAIRS)
    enc_down_arrived = flip(enc_down_leaving, REACH_PAIRS)

    enc_dk, enc_dv = attend_keys(
        tie(enc_kv, enc_gu_leaving, enc_down_leaving, dec_gu_last[0], dec_down_last[0]),
        enc_qd_window,
        enc_stat_window,
        bounds_both,
        doc_lo,
        doc_hi,
        enc_back,
    )
    enc_dq, enc_grad_line = attend_queries(
        enc_q, enc_window, bounds_both, doc_lo, doc_hi, enc_da, enc_logs, enc_delta, enc_line
    )
    self_dk, self_dv = attend_keys(
        dec_kv, self_qd_window, self_stat_window, bounds_above, positions, doc_hi, dec_back
    )
    self_dq, dec_grad_line = attend_queries(
        dec_q, dec_window, bounds_below, doc_lo, positions, self_da, dec_logs, self_delta, dec_line
    )
    enc_partial = (
        dot(enc_dq, enc_query, 1, 1) + dot(enc_dk, enc_key, 1, 1) + dot(enc_dv, enc_value, 1, 1)
    )
    self_partial = (
        dot(self_dq, dec_query, 1, 1) + dot(self_dk, dec_key, 1, 1) + dot(self_dv, dec_value, 1, 1)
    )
    blocks = exchanged_parity(enc_dq.T, enc_dk.T, enc_dv.T, self_dq.T, self_dk.T, self_dv.T)
    attended_blocks = parity_of_whole(
        (enc_attended.T, enc_att_other.T), (dec_attended.T, dec_att_other.T)
    )
    both_shard = scatter(
        [
            (blocks[:3], enc_normed),
            (attended_blocks[:1], enc_branch),
            (blocks[3:], dec_normed),
            (attended_blocks[1:], self_branch),
        ]
    )
    part, g_enc_norm_attn = norm_backward(enc_input, enc_norm_attn, summed_own(tie(enc_partial, blocks)))
    grad_enc_input = own(grad_enc_mid) + part
    part, g_dec_norm_self = norm_backward(dec_input, dec_norm_self, summed_own(tie(self_partial, blocks)))
    grad_dec_input = own(grad_mid) + part

    cross_blocks = parity_of_whole(
        (cross_dq.T, dq_other.T),
        (cross_dk.T, dk_other.T),
        (cross_dv.T, dv_other.T),
        (cross_attended.T, cross_att_other.T),
    )
    cross_shard = scatter(
        [
            (cross_blocks[:1], cross_normed),
            (cross_blocks[1:3], memory),
            (cross_blocks[3:], cross_branch),
        ]
    )

    enc_gu_arrived, enc_down_arrived = tie((enc_gu_arrived, enc_down_arrived), enc_partial, self_partial)
    enc_gu_kept, enc_gu_sent = after_low(after_first(enc_gu_routed, enc_ffn_all, enc_gu_arrived))
    enc_down_kept, enc_down_sent = after_low(
        after_first(enc_hidden_routed, enc_branch_all, enc_down_arrived)
    )
    enc_gu_last = last_start(enc_gu_kept, swap(enc_gu_sent))
    enc_down_last = last_start(enc_down_kept, swap(enc_down_sent))
    dec_gu, dec_down_rows = last_end(*dec_gu_last), last_end(*dec_down_last)
    enc_gu, enc_down_rows = last_end(*enc_gu_last), last_end(*enc_down_last)

    enc_bias_part = bucket_grads(enc_hot, enc_grad_line)
    dec_bias_part = bucket_grads(dec_hot, dec_grad_line)
    gains = jnp.concatenate(
        [
            g_enc_norm_attn,
            0.5 * g_enc_norm_ff,
            g_dec_norm_self,
            0.5 * g_dec_norm_cross,
            0.5 * g_dec_norm_ff,
        ]
    )
    small = jnp.concatenate(
        [
            gains,
            enc_bias_part.reshape(-1),
            dec_bias_part.reshape(-1),
            loss_part[None],
            valid_part[None],
        ]
    )
    small = total_over_devices(small, 5, ctx_size)
    squared_total, valid_total = small[-2], small[-1]
    teacher_loss = squared_total / (D * valid_total)
    scale = (own_rows * 2 * ctx_size) / valid_total
    small = small * scale
    gain = [small[i * D : (i + 1) * D] for i in range(5)]
    bias_size = enc_bias_part.size
    bias = [
        small[5 * D + i * bias_size : 5 * D + (i + 1) * bias_size].reshape(enc_bias_part.shape)
        for i in range(2)
    ]

    def pieces(shard, kinds):
        each = shard.shape[0] // len(kinds)
        made = []
        for i, transposed in enumerate(kinds):
            piece = shard[i * each : (i + 1) * each].astype(f32) * scale
            made.append(piece.T if transposed else piece)
        return made

    dec_gate_up = pieces(dec_gu, (True, True))
    dec_down_g = pieces(dec_down_rows, (False,))
    enc_gate_up = pieces(enc_gu, (True, True))
    enc_down_g = pieces(enc_down_rows, (False,))
    kinds = (True, True, True, False)
    both_attn = pieces(both_shard, kinds + kinds)
    enc_attn = both_attn[:4]
    dec_attn = both_attn[4:] + pieces(cross_shard, kinds)
    return (
        teacher_loss,
        own(dec_output),
        grad_enc_input * scale,
        grad_dec_input * scale,
        gain[0],
        *enc_attn,
        gain[1],
        *enc_gate_up,
        *enc_down_g,
        bias[0],
        gain[2],
        *dec_attn[:4],
        gain[3],
        *dec_attn[4:],
        gain[4],
        *dec_gate_up,
        *dec_down_g,
        bias[1],
    )


def solution(mesh):
    rows = P(("ctx", "fsdp"), None)
    split_columns = P(None, "fsdp")
    split_rows = P("fsdp", None)
    attention_in = (split_columns,) * 3 + (split_rows,)
    feed_in = (split_columns,) * 2 + (split_rows,)
    in_specs = (
        (rows,) * 3
        + (P(("ctx", "fsdp")), P(), P(), P())
        + (P(),)
        + attention_in
        + (P(),)
        + feed_in
        + (P(), P())
        + attention_in
        + (P(),)
        + attention_in
        + (P(),)
        + feed_in
        + (P(),)
    )
    columns = P(None, ("ctx", "fsdp"))
    attention_out = (columns,) * 3 + (rows,)
    feed_out = (columns,) * 2 + (rows,)
    out_specs = (
        (P(),)
        + (rows,) * 3
        + (P(),)
        + attention_out
        + (P(),)
        + feed_out
        + (P(), P())
        + attention_out
        + (P(),)
        + attention_out
        + (P(),)
        + feed_out
        + (P(),)
    )
    return jax.shard_map(body, mesh=mesh, in_specs=in_specs, out_specs=out_specs, check_vma=False)
```

```python
import functools

import jax
import jax.numpy as jnp
from jax import lax
from jax.experimental import pallas as pl
from jax.experimental.pallas import tpu as pltpu
from jax.sharding import PartitionSpec as P

D = 1472
HEAD = 64
REACH_PAIRS = 4
WIN = 3 * REACH_PAIRS
epsilon = 1e-06
far_below = -1e30
bf16 = jnp.bfloat16
f32 = jnp.float32
MESH = pl.DeviceIdType.MESH
FEED_LIMIT = 16 * 1024 * 1024
SMALL_COST = pl.CostEstimate(flops=0, bytes_accessed=500_000, transcendentals=0)


def dot(left, right, left_dim=1, right_dim=0):
    return lax.dot_general(
        left, right, (((left_dim,), (right_dim,)), ((), ())), preferred_element_type=f32
    )


def swap(value):
    return lax.ppermute(value, "fsdp", [(0, 1), (1, 0)])


def flipped(index, bit):
    return index + bit - 2 * bit * lax.rem(index // bit, 2)


def window_kernel(flags, swaps, *refs):
    arrays = len(flags)
    total = arrays + swaps
    ins, outs = refs[:total], refs[total : 2 * total]
    local_sem, send_sem, recv_sem, swap_send, swap_recv = refs[2 * total :]
    R = REACH_PAIRS
    ctx = lax.axis_index("ctx")
    fsdp = lax.axis_index("fsdp")
    groups = lax.axis_size("ctx") // R
    group = ctx // R
    place = lax.rem(ctx, R)
    near, far = flipped(place, 1), flipped(place, 2)
    dev_near, dev_far = group * R + near, group * R + far
    dev_up, dev_down = ctx + R, ctx - R
    has_up, has_down = group < groups - 1, group > 0
    barrier = pltpu.get_barrier_semaphore()

    def greet(device):
        pl.semaphore_signal(barrier, inc=1, device_id=(device, fsdp), device_id_type=MESH)

    greet(dev_near)
    greet(dev_far)
    if swaps:
        pl.semaphore_signal(barrier, inc=1, device_id=(ctx, 1 - fsdp), device_id_type=MESH)

    @pl.when(has_up)
    def _():
        greet(dev_up)

    @pl.when(has_down)
    def _():
        greet(dev_down)

    greeted = 2 + (1 if swaps else 0)
    pl.semaphore_wait(barrier, greeted + has_up.astype(jnp.int32) + has_down.astype(jnp.int32))

    def copies(number, source_slot, slot, device, use=lambda f: True, part=None):
        made = []
        for k, (below, above, split) in enumerate(flags):
            if not use(flags[k]):
                continue
            rows = ins[k].shape[0]
            cut = rows if not split else (rows // 2 if not (below and above) else 3 * rows // 8)
            where = {None: (0, rows), 0: (0, cut), 1: (cut, rows)}[part]
            if where[0] == where[1]:
                continue
            span = pl.ds(where[0], where[1] - where[0])
            source = ins[k] if source_slot is None else outs[k].at[source_slot, span]
            made.append(
                pltpu.make_async_remote_copy(
                    src_ref=source,
                    dst_ref=outs[k].at[slot, span],
                    send_sem=send_sem.at[k, number],
                    recv_sem=recv_sem.at[k, number],
                    device_id=(device, fsdp),
                    device_id_type=MESH,
                )
            )
        return made

    def start(made):
        for copy in made:
            copy.start()

    def arrived(made):
        for copy in made:
            copy.wait_recv()

    def left(made):
        for copy in made:
            copy.wait_send()

    below = lambda flag: flag[0]
    above = lambda flag: flag[1]
    to_up = copies(0, None, place, dev_up, below)
    to_down = copies(1, None, 2 * R + place, dev_down, above)
    to_far = copies(2, None, R + place, dev_far)
    to_near = copies(3, None, R + place, dev_near)
    far_low = copies(4, place, place, dev_far, below, 0)
    far_high = copies(5, 2 * R + place, 2 * R + place, dev_far, above, 0)
    up_far = copies(6, R + far, far, dev_up, below, 1)
    down_far = copies(7, R + far, 2 * R + far, dev_down, above, 1)
    near_low = copies(8, place, place, dev_near, below)
    near_high = copies(9, 2 * R + place, 2 * R + place, dev_near, above)
    near_far = copies(10, R + far, R + far, dev_near)
    near_far_low = copies(11, far, far, dev_near, below)
    near_far_high = copies(12, 2 * R + far, 2 * R + far, dev_near, above)
    own = [
        pltpu.make_async_copy(ins[k], outs[k].at[R + place], local_sem.at[k])
        for k in range(arrays)
    ]

    across = [
        pltpu.make_async_remote_copy(
            src_ref=ins[arrays + k],
            dst_ref=outs[arrays + k],
            send_sem=swap_send.at[k],
            recv_sem=swap_recv.at[k],
            device_id=(ctx, 1 - fsdp),
            device_id_type=MESH,
        )
        for k in range(swaps)
    ]

    @pl.when(has_up)
    def _():
        start(to_up)

    @pl.when(has_down)
    def _():
        start(to_down)

    start(to_far)
    start(to_near)
    start(across)
    start(own)
    arrived(to_far)

    @pl.when(has_up)
    def _():
        start(up_far)

    @pl.when(has_down)
    def _():
        start(down_far)

    start(near_far)

    @pl.when(has_down)
    def _():
        arrived(to_up)
        start(far_low)
        start(near_low)

    @pl.when(has_up)
    def _():
        arrived(to_down)
        start(far_high)
        start(near_high)

    @pl.when(has_down)
    def _():
        arrived(far_low)
        arrived(up_far)
        start(near_far_low)

    @pl.when(has_up)
    def _():
        arrived(far_high)
        arrived(down_far)
        start(near_far_high)

    arrived(to_near)
    arrived(near_far)

    @pl.when(has_down)
    def _():
        arrived(near_low)
        arrived(near_far_low)
        left(far_low)
        left(near_low)
        left(near_far_low)
        left(to_down)
        left(down_far)

    @pl.when(has_up)
    def _():
        arrived(near_high)
        arrived(near_far_high)
        left(far_high)
        left(near_high)
        left(near_far_high)
        left(to_up)
        left(up_far)

    left(to_far)
    left(to_near)
    left(near_far)
    for copy in own + across:
        copy.wait()


BOTH, BELOW, ABOVE = (True, True), (True, False), (False, True)


def window_gather(number, pairs, swapped=()):
    values = [value for value, _ in pairs]
    flags = tuple(
        sides + (value.dtype == bf16 and value.shape[0] % 128 == 0,) for value, sides in pairs
    )
    count, swaps = len(values), len(swapped)
    vmem = pl.BlockSpec(memory_space=pltpu.VMEM)
    specs = [vmem] * count + [pl.BlockSpec(memory_space=pl.ANY)] * swaps
    return pl.pallas_call(
        functools.partial(window_kernel, flags, swaps),
        out_shape=[jax.ShapeDtypeStruct((WIN,) + v.shape, v.dtype) for v in values]
        + [jax.ShapeDtypeStruct(v.shape, v.dtype) for v in swapped],
        in_specs=specs,
        out_specs=specs,
        scratch_shapes=[
            pltpu.SemaphoreType.DMA((count,)),
            pltpu.SemaphoreType.DMA((count, 13)),
            pltpu.SemaphoreType.DMA((count, 13)),
            pltpu.SemaphoreType.DMA((max(swaps, 1),)),
            pltpu.SemaphoreType.DMA((max(swaps, 1),)),
        ],
        compiler_params=pltpu.CompilerParams(
            collective_id=number, has_side_effects=True, vmem_limit_bytes=4 << 20
        ),
        cost_estimate=SMALL_COST,
        name="window_gather",
    )(*values, *swapped)


def total_kernel(rounds, x_ref, o_ref, mine, theirs, send_sem, recv_sem):
    ctx = lax.axis_index("ctx")
    fsdp = lax.axis_index("fsdp")
    partners = [(ctx, 1 - fsdp)] + [(flipped(ctx, 1 << k), fsdp) for k in range(rounds - 1)]
    barrier = pltpu.get_barrier_semaphore()
    for partner in partners:
        pl.semaphore_signal(barrier, inc=1, device_id=partner, device_id_type=MESH)
    pl.semaphore_wait(barrier, rounds)
    mine[0] = x_ref[...]
    for k, partner in enumerate(partners):
        copy = pltpu.make_async_remote_copy(
            src_ref=mine.at[k],
            dst_ref=theirs.at[k],
            send_sem=send_sem.at[k],
            recv_sem=recv_sem.at[k],
            device_id=partner,
            device_id_type=MESH,
        )
        copy.start()
        copy.wait()
        added = mine[k] + theirs[k]
        if k + 1 < rounds:
            mine[k + 1] = added
        else:
            o_ref[...] = added


def total_over_devices(value, number, ctx_size):
    rounds = ctx_size.bit_length()
    padded = -(-value.shape[0] // 1024) * 1024
    wide = jnp.pad(value, (0, padded - value.shape[0])).reshape(8, padded // 8)
    vmem = pl.BlockSpec(memory_space=pltpu.VMEM)
    made = pl.pallas_call(
        functools.partial(total_kernel, rounds),
        out_shape=jax.ShapeDtypeStruct(wide.shape, f32),
        in_specs=[vmem],
        out_specs=vmem,
        scratch_shapes=[
            pltpu.VMEM((rounds,) + wide.shape, f32),
            pltpu.VMEM((rounds,) + wide.shape, f32),
            pltpu.SemaphoreType.DMA((rounds,)),
            pltpu.SemaphoreType.DMA((rounds,)),
        ],
        compiler_params=pltpu.CompilerParams(collective_id=number, has_side_effects=True),
        cost_estimate=SMALL_COST,
        name="total_over_devices",
    )(wide)
    return made.reshape(-1)[: value.shape[0]]


def head_rows(width):
    rows = lax.broadcasted_iota(jnp.int32, (width, 1), 0)
    return [(rows >= h * HEAD) & (rows < (h + 1) * HEAD) for h in range(width // HEAD)]


def head_lanes(width):
    lanes = lax.broadcasted_iota(jnp.int32, (1, width), 1)
    return [(lanes >= h * HEAD) & (lanes < (h + 1) * HEAD) for h in range(width // HEAD)]


def only(value, mask):
    return jnp.where(mask, value, jnp.zeros_like(value))


def by_token(value):
    width, rows = value.shape
    full = -(-width // 128) * 128
    return jnp.concatenate([value, jnp.zeros((full - width, rows), value.dtype)], axis=0).T[:, :width]


def toeplitz(line_ref, head, block, rows):
    start = pl.multiple_of(block * rows, rows)
    segment = line_ref[pl.ds(head, 1), pl.ds(start, 2 * rows)]
    spread = jnp.broadcast_to(segment, (rows, 2 * rows))
    return pltpu.roll(spread, rows + 1, 1, stride=1, stride_axis=0)[:, :rows]


def halves(value, op):
    half = value.shape[1] // 2
    return op(value[:, :half], value[:, half:])


def forward_kernel(biased, bounds, q_ref, kv_ref, lo_ref, hi_ref, *rest):
    if biased:
        line_ref, rest = rest[0], rest[1:]
    o_ref, att_ref, l_ref, s_ref, m_ref, sum_ref, acc_ref = rest
    width, rows = q_ref.shape
    heads = width // HEAD
    lanes, bands = head_lanes(width), head_rows(width)
    first, last, key_base = bounds[0], bounds[1], bounds[2]
    lo, hi = lo_ref[...], hi_ref[...]
    m_ref[...] = jnp.full_like(m_ref, far_below)
    sum_ref[...] = jnp.zeros_like(sum_ref)
    acc_ref[...] = jnp.zeros_like(acc_ref)
    q = by_token(q_ref[...])

    def scores(block, carry):
        keys = kv_ref[block, :width]
        key_pos = key_base + block * rows + lax.broadcasted_iota(jnp.int32, (rows, rows), 1)
        allowed = (key_pos >= lo) & (key_pos <= hi)
        for h in range(heads):
            s = dot(only(q, lanes[h]), keys)
            if biased:
                s = s + toeplitz(line_ref, h, block, rows)
            s = jnp.where(allowed, s, far_below)
            s_ref[block, h] = s
            m_ref[h] = jnp.maximum(m_ref[h], halves(s, jnp.maximum))
        return carry

    lax.fori_loop(first, last + 1, scores, 0)
    tops = [jnp.max(m_ref[h], axis=1, keepdims=True) for h in range(heads)]

    def mix(block, carry):
        values = kv_ref[block, width:]
        total = None
        for h in range(heads):
            p = jnp.exp(s_ref[block, h] - tops[h])
            sum_ref[h] += halves(p, jnp.add)
            part = dot(only(values, bands[h]), p.astype(bf16), 1, 1)
            total = part if total is None else total + part
        acc_ref[...] += total
        return carry

    lax.fori_loop(first, last + 1, mix, 0)
    column = lax.broadcasted_iota(jnp.int32, (rows, 128), 1)
    both = jnp.zeros((rows, 128), f32)
    for h in range(heads):
        total = jnp.sum(sum_ref[h], axis=1, keepdims=True)
        both = jnp.where(column == h, tops[h] + jnp.log(total), both)
        both = jnp.where(column == heads + h, 1.0 / total, both)
    across = both.T
    scale = jnp.zeros((width, rows), f32)
    for h in range(heads):
        scale = jnp.where(bands[h], across[heads + h : heads + h + 1], scale)
    out = acc_ref[...] * scale
    o_ref[...] = out
    att_ref[...] = out.astype(bf16)
    l_ref[...] = across[:8]


def query_kernel(biased, bounds, qd_ref, kv_ref, lo_ref, hi_ref, stat_ref, *rest):
    if biased:
        line_ref, dq_ref, gline_ref, acc_ref = rest
        gline_ref[...] = jnp.zeros_like(gline_ref)
    else:
        dq_ref, acc_ref = rest
    width, rows = qd_ref.shape[0] // 2, qd_ref.shape[1]
    heads = width // HEAD
    lanes, bands = head_lanes(width), head_rows(width)
    first, last, key_base = bounds[0], bounds[1], bounds[2]
    lo, hi = lo_ref[...], hi_ref[...]
    acc_ref[...] = jnp.zeros_like(acc_ref)
    q, da = by_token(qd_ref[:width]), by_token(qd_ref[width:])
    logs = [stat_ref[:, h : h + 1] for h in range(heads)]
    deltas = [stat_ref[:, heads + h : heads + h + 1] for h in range(heads)]

    def step(block, carry):
        keys = kv_ref[block, :width]
        values = kv_ref[block, width:]
        key_pos = key_base + block * rows + lax.broadcasted_iota(jnp.int32, (rows, rows), 1)
        allowed = (key_pos >= lo) & (key_pos <= hi)
        total = None
        for h in range(heads):
            s = dot(only(q, lanes[h]), keys)
            if biased:
                s = s + toeplitz(line_ref, h, block, rows)
            p = jnp.exp(jnp.where(allowed, s - logs[h], far_below))
            dp = dot(only(da, lanes[h]), values)
            ds = (p * (dp - deltas[h])).astype(bf16)
            part = dot(only(keys, bands[h]), ds, 1, 1)
            total = part if total is None else total + part
            if biased:
                folded = jnp.concatenate([ds.astype(f32), jnp.zeros((rows, rows), f32)], axis=1)
                half = rows // 2
                while half >= 1:
                    folded = pltpu.roll(folded[:half], half, 1) + folded[half:]
                    half //= 2
                start = pl.multiple_of(block * rows, rows)
                gline_ref[pl.ds(h, 1), pl.ds(start, 2 * rows)] += folded
        acc_ref[...] += total
        return carry

    lax.fori_loop(first, last + 1, step, 0)
    dq_ref[...] = acc_ref[...].astype(bf16)


def key_kernel(biased, bounds, kv_ref, qd_ref, stat_ref, lo_ref, hi_ref, *rest):
    if biased:
        line_ref, rest = rest[0], rest[1:]
    dkv_ref, dk_acc, dv_acc = rest
    width, rows = kv_ref.shape[0] // 2, kv_ref.shape[1]
    heads = width // HEAD
    lanes, bands = head_lanes(width), head_rows(width)
    first, last, query_base = bounds[0], bounds[1], bounds[2]
    lo, hi = lo_ref[...], hi_ref[...]
    dk_acc[...] = jnp.zeros_like(dk_acc)
    dv_acc[...] = jnp.zeros_like(dv_acc)
    keys, values = by_token(kv_ref[:width]), by_token(kv_ref[width:])

    def step(block, carry):
        q = qd_ref[block, :width]
        da = qd_ref[block, width:]
        query_pos = query_base + block * rows + lax.broadcasted_iota(jnp.int32, (rows, rows), 1)
        allowed = (query_pos >= lo) & (query_pos <= hi)
        total_k = None
        total_v = None
        for h in range(heads):
            s = dot(only(keys, lanes[h]), q)
            if biased:
                s = s + toeplitz(line_ref, h, block, rows)
            p = jnp.exp(jnp.where(allowed, s - stat_ref[block, h : h + 1, :], far_below))
            dp = dot(only(values, lanes[h]), da)
            ds = (p * (dp - stat_ref[block, heads + h : heads + h + 1, :])).astype(bf16)
            part_k = dot(only(q, bands[h]), ds, 1, 1)
            part_v = dot(only(da, bands[h]), p.astype(bf16), 1, 1)
            total_k = part_k if total_k is None else total_k + part_k
            total_v = part_v if total_v is None else total_v + part_v
        dk_acc[...] += total_k
        dv_acc[...] += total_v
        return carry

    lax.fori_loop(first, last + 1, step, 0)
    dkv_ref[:width] = dk_acc[...].astype(bf16)
    dkv_ref[width:] = dv_acc[...].astype(bf16)


def local_call(kernel, out_shape, scratch, name, limit, bounds, *values):
    vmem = pl.BlockSpec(memory_space=pltpu.VMEM)
    smem = pl.BlockSpec(memory_space=pltpu.SMEM)
    return pl.pallas_call(
        kernel,
        out_shape=out_shape,
        in_specs=[smem] + [vmem] * len(values),
        out_specs=jax.tree.map(lambda _: vmem, out_shape),
        scratch_shapes=scratch,
        compiler_params=pltpu.CompilerParams(vmem_limit_bytes=limit << 20),
        cost_estimate=SMALL_COST,
        name=name,
    )(bounds, *values)


def attend(q, kv_window, bounds, lo, hi, line):
    width, rows = q.shape
    heads = width // HEAD
    biased = line is not None
    return local_call(
        functools.partial(forward_kernel, biased),
        [
            jax.ShapeDtypeStruct((width, rows), f32),
            jax.ShapeDtypeStruct((width, rows), bf16),
            jax.ShapeDtypeStruct((8, rows), f32),
        ],
        [
            pltpu.VMEM((WIN, heads, rows, rows), f32),
            pltpu.VMEM((heads, rows, rows // 2), f32),
            pltpu.VMEM((heads, rows, rows // 2), f32),
            pltpu.VMEM((width, rows), f32),
        ],
        "attend_forward",
        20,
        bounds,
        q,
        kv_window,
        lo,
        hi,
        *([line] if biased else []),
    )


def attend_queries(qd, kv_window, bounds, lo, hi, stats, line):
    width, rows = qd.shape[0] // 2, qd.shape[1]
    biased = line is not None
    shapes = [jax.ShapeDtypeStruct((width, rows), bf16)]
    if biased:
        shapes.append(jax.ShapeDtypeStruct(line.shape, f32))
    return local_call(
        functools.partial(query_kernel, biased),
        shapes,
        [pltpu.VMEM((width, rows), f32)],
        "attend_queries",
        14,
        bounds,
        qd,
        kv_window,
        lo,
        hi,
        stats,
        *([line] if biased else []),
    )


def attend_keys(kv, qd_window, stat_window, bounds, lo, hi, line):
    width, rows = kv.shape[0] // 2, kv.shape[1]
    biased = line is not None
    return local_call(
        functools.partial(key_kernel, biased),
        jax.ShapeDtypeStruct((2 * width, rows), bf16),
        [pltpu.VMEM((width, rows), f32)] * 2,
        "attend_keys",
        14,
        bounds,
        kv,
        qd_window,
        stat_window,
        lo,
        hi,
        *([line] if biased else []),
    )


def prepare_kernel(grad_ref, w_ref, q_ref, o_ref, log_ref, qd_ref, row_ref, wide_ref):
    width, rows = q_ref.shape
    heads = width // HEAD
    da = dot(w_ref[...], grad_ref[...]).astype(bf16)
    qd_ref[:width] = q_ref[...]
    qd_ref[width:] = da
    product = da.astype(f32) * o_ref[...]
    row = lax.broadcasted_iota(jnp.int32, (128, rows), 0)
    stats = jnp.concatenate([log_ref[...], jnp.zeros((120, rows), f32)], axis=0)
    for h, mask in enumerate(head_rows(width)):
        delta = jnp.sum(only(product, mask), axis=0, keepdims=True)
        stats = jnp.where(row == heads + h, delta, stats)
    row_ref[...] = stats[:8]
    wide_ref[...] = stats.T


def prepare(grad, w_out, q, out, log_rows):
    width, rows = q.shape
    vmem = pl.BlockSpec(memory_space=pltpu.VMEM)
    return pl.pallas_call(
        prepare_kernel,
        out_shape=[
            jax.ShapeDtypeStruct((2 * width, rows), bf16),
            jax.ShapeDtypeStruct((8, rows), f32),
            jax.ShapeDtypeStruct((rows, 128), f32),
        ],
        in_specs=[vmem] * 5,
        out_specs=[vmem] * 3,
        compiler_params=pltpu.CompilerParams(vmem_limit_bytes=10 << 20),
        cost_estimate=SMALL_COST,
        name="attention_prepare",
    )(grad, w_out, q, out, log_rows)


KINDS = 4


def small_kernel(blocks, width, mirrored, counts, kinds, place, *refs):
    own, other = refs[: counts[0]], refs[counts[0] : sum(counts)]
    sources, out_ref = refs[sum(counts) : -1], refs[-1]
    columns = width // blocks
    side = place[0]
    row = lax.broadcasted_iota(jnp.int32, (blocks * KINDS * columns, 1), 0)
    block = row // (KINDS * columns)
    if mirrored:
        left, block_of = block, jnp.zeros_like(block)
        for _ in range(blocks.bit_length() - 1):
            block_of = 2 * block_of + lax.rem(left, 2)
            left = left // 2
        block = block_of
    kind = lax.rem(row // columns, KINDS)
    column = columns * (2 * block + side) + lax.rem(row, columns)
    away = jnp.where(column // width == side, 0, 1)
    wanted = away * (KINDS * width) + kind * width + lax.rem(column, width)
    values = jnp.concatenate([ref[...] for ref in own + other], axis=0)
    spot = lax.broadcasted_iota(jnp.int32, (1, values.shape[0]), 1)
    onehot = jnp.where(wanted == spot, 1.0, 0.0).astype(bf16)
    chosen = dot(onehot, values).astype(bf16)
    total = None
    for (first, last), source in zip(kinds, sources):
        part = dot(only(chosen, (kind >= first) & (kind <= last)), source[...], 1, 1)
        total = part if total is None else total + part
    out_ref[...] = total.astype(bf16)


def small_part(blocks, width, side, own, other, sources, mirrored):
    vmem = pl.BlockSpec(memory_space=pltpu.VMEM)
    smem = pl.BlockSpec(memory_space=pltpu.SMEM)
    depth = sources[0][1].shape[0]
    kinds = tuple(span for span, _ in sources)
    values = (*own, *other, *[source for _, source in sources])
    return pl.pallas_call(
        functools.partial(
            small_kernel, blocks, width, mirrored, (len(own), len(other)), kinds
        ),
        out_shape=jax.ShapeDtypeStruct((KINDS * width, depth), bf16),
        in_specs=[smem] + [vmem] * len(values),
        out_specs=vmem,
        compiler_params=pltpu.CompilerParams(vmem_limit_bytes=28 << 20),
        cost_estimate=SMALL_COST,
        name="attention_weight_part",
    )(jnp.stack([side]), *values)


CHUNK = 256
GELU_RATE = 0.7978845608028654
GELU_CUBE = 0.044715


def feed_kernel(x_ref, gate_ref, up_ref, down_ref, sum_ref, low_ref, hidden_ref, d1_ref, d2_ref):
    x = x_ref[...].T
    for start in range(0, gate_ref.shape[1], CHUNK):
        span = slice(start, start + CHUNK)
        gating = dot(x, gate_ref[:, span]).T
        upward = dot(x, up_ref[:, span]).T
        square = gating * gating
        t = jnp.tanh(GELU_RATE * gating * (1.0 + GELU_CUBE * square))
        half = 0.5 * (1.0 + t)
        unit = gating * half
        slope = half + 0.5 * gating * (1.0 - t * t) * (
            GELU_RATE * (1.0 + 3.0 * GELU_CUBE * square)
        )
        hidden_ref[span, :] = (unit * upward).astype(bf16)
        d1_ref[span, :] = slope * upward
        d2_ref[span, :] = unit
    total = dot(down_ref[...], hidden_ref[...])
    sum_ref[...] = total
    low_ref[...] = total.astype(bf16)


def feed_back_kernel(e_ref, gate_ref, up_ref, down_ref, d1_ref, d2_ref, sum_ref, low_ref, gg_ref, gu_ref):
    e = e_ref[...].T
    for start in range(0, gate_ref.shape[1], CHUNK):
        span = slice(start, start + CHUNK)
        grad_hidden = dot(e, down_ref[:, span]).astype(bf16).astype(f32).T
        gg_ref[span, :] = (grad_hidden * d1_ref[span, :]).astype(bf16)
        gu_ref[span, :] = (grad_hidden * d2_ref[span, :]).astype(bf16)
    total = dot(gate_ref[...], gg_ref[...]) + dot(up_ref[...], gu_ref[...])
    sum_ref[...] = total
    low_ref[...] = total.astype(bf16)


def feed_call(kernel, name, source, weights, chunked, outs):
    depth, rows = source.shape
    columns = weights[0].shape[1]
    vmem = pl.BlockSpec(memory_space=pltpu.VMEM)
    return pl.pallas_call(
        kernel,
        out_shape=[
            jax.ShapeDtypeStruct((depth, rows), f32),
            jax.ShapeDtypeStruct((depth, rows), bf16),
        ]
        + [jax.ShapeDtypeStruct((columns, rows), kind) for kind in outs],
        in_specs=[vmem] * (4 + len(chunked)),
        out_specs=[vmem] * (2 + len(outs)),
        compiler_params=pltpu.CompilerParams(vmem_limit_bytes=FEED_LIMIT),
        cost_estimate=SMALL_COST,
        name=name,
    )(source, *weights, *chunked)


def feed_forward(source, weights):
    return feed_call(feed_kernel, "feed_forward", source, weights, (), (bf16, f32, f32))


def feed_backward(grad, weights, d1, d2):
    return feed_call(feed_back_kernel, "feed_backward", grad, weights, (d1, d2), (bf16, bf16))


def inverse_root(inputs):
    return lax.rsqrt(jnp.mean(inputs * inputs, axis=0, keepdims=True) + epsilon)


def root_norm(inputs, gain):
    return inputs * inverse_root(inputs) * gain[:, None]


def norm_backward(inputs, gain, grad):
    inverse = inverse_root(inputs)
    scaled = grad * gain[:, None]
    along = jnp.mean(inputs * scaled, axis=0, keepdims=True)
    grad_inputs = inverse * scaled - inputs * (inverse * inverse * inverse) * along
    return grad_inputs, jnp.sum(grad * inputs * inverse, axis=1)


def body(
    enc_input,
    dec_input,
    teacher,
    valid_mask,
    doc_lengths,
    enc_buckets,
    dec_buckets,
    enc_norm_attn,
    enc_query,
    enc_key,
    enc_value,
    enc_out_proj,
    enc_norm_ff,
    enc_gate,
    enc_up,
    enc_down,
    enc_rel_bias,
    dec_norm_self,
    dec_query,
    dec_key,
    dec_value,
    dec_out_proj,
    dec_norm_cross,
    cross_query,
    cross_key,
    cross_value,
    cross_out_proj,
    dec_norm_ff,
    dec_gate,
    dec_up,
    dec_down,
    dec_rel_bias,
):
    ctx = lax.axis_index("ctx")
    side = lax.axis_index("fsdp")
    ctx_size = lax.axis_size("ctx")
    own_rows = enc_input.shape[0]
    rows = 2 * own_rows
    width = enc_query.shape[1]
    heads = width // HEAD
    place = lax.rem(ctx, REACH_PAIRS)
    core_bit, far_bit = lax.rem(place, 2), place // 2

    def ordered(mine, other, axis=1):
        first = side == 0
        return jnp.concatenate(
            [jnp.where(first, mine, other), jnp.where(first, other, mine)], axis=axis
        )

    def pick(value, index, axis):
        return lax.dynamic_index_in_dim(value, index, axis, keepdims=False)

    def flip(value, bit):
        return lax.ppermute(value, "ctx", [(i, i ^ bit) for i in range(ctx_size)])

    def own(value):
        return lax.dynamic_slice_in_dim(value, side * own_rows, own_rows, 1)

    def others(value):
        return lax.dynamic_slice_in_dim(value, (1 - side) * own_rows, own_rows, 1)

    def together(*values):
        return lax.optimization_barrier(values)

    count = doc_lengths.shape[0]
    order = jnp.arange(count, dtype=jnp.int32)
    starts = jnp.sum(
        jnp.where(order[None, :] < order[:, None], doc_lengths[None, :], 0), axis=1
    )
    ends = starts + doc_lengths
    positions = ctx * rows + jnp.arange(rows, dtype=jnp.int32)[:, None]
    doc_lo = jnp.max(jnp.where(starts[None, :] <= positions, starts[None, :], 0), axis=1, keepdims=True)
    doc_hi = (
        jnp.min(
            jnp.where(ends[None, :] > positions, ends[None, :], ctx_size * rows),
            axis=1,
            keepdims=True,
        )
        - 1
    )
    base_block = ctx - place - REACH_PAIRS
    first_block = doc_lo[0, 0] // rows - base_block
    last_block = doc_hi[rows - 1, 0] // rows - base_block
    own_block = REACH_PAIRS + place
    base_pos = base_block * rows
    bounds_both = jnp.stack([first_block, last_block, base_pos])
    bounds_below = jnp.stack([first_block, own_block, base_pos])
    bounds_above = jnp.stack([own_block, last_block, base_pos])

    reach = enc_buckets.shape[0] // 2
    line_len = (WIN + 1) * rows
    pad_lo, pad_hi = reach, reach + rows
    line_start = (reach + 1 - rows) + pad_lo - rows * (REACH_PAIRS + place)
    reverse_start = (reach - rows) + pad_lo - rows * (REACH_PAIRS + place)

    def lines(rel_bias, buckets):
        hot = (
            buckets[:, None] == jnp.arange(rel_bias.shape[0], dtype=jnp.int32)[None, :]
        ).astype(f32)
        mine = lax.dynamic_slice_in_dim(rel_bias, side * heads, heads, 1)
        line = lax.dot_general(
            mine, hot, (((0,), (1,)), ((), ())), precision=lax.Precision.HIGHEST
        )
        hot_back = (
            buckets[::-1][:, None] == jnp.arange(rel_bias.shape[0], dtype=jnp.int32)[None, :]
        ).astype(f32)
        line_back = lax.dot_general(
            mine, hot_back, (((0,), (1,)), ((), ())), precision=lax.Precision.HIGHEST
        )
        padded = jnp.pad(line, ((0, 8 - heads), (pad_lo, pad_hi)))
        backward = jnp.pad(line_back, ((0, 8 - heads), (pad_lo, pad_hi)))
        return (
            hot,
            lax.dynamic_slice_in_dim(padded, line_start, line_len, 1),
            lax.dynamic_slice_in_dim(backward, reverse_start, line_len, 1),
        )

    enc_hot, enc_line, enc_back = lines(enc_rel_bias, enc_buckets)
    dec_hot, dec_line, dec_back = lines(dec_rel_bias, dec_buckets)

    def bucket_grads(hot, grad_line):
        padded = jnp.zeros((heads, 2 * reach + pad_lo + pad_hi), f32)
        padded = lax.dynamic_update_slice_in_dim(padded, grad_line[:heads], line_start, 1)
        cropped = padded[:, pad_lo : pad_lo + 2 * reach]
        grads = lax.dot_general(
            hot, cropped, (((0,), (1,)), ((), ())), precision=lax.Precision.HIGHEST
        )
        whole = jnp.zeros((hot.shape[1], 2 * heads), f32)
        return lax.dynamic_update_slice_in_dim(whole, grads, side * heads, 1)

    def gather_start(value):
        return value, flip(value, 2)

    def gather_end(value, far):
        both = jnp.concatenate([value, far], axis=1)
        return jnp.concatenate([both, flip(both, 1)], axis=1)

    low = ctx_size // 8

    def route_start(*values):
        columns = values[0].shape[0] // ctx_size
        split = jnp.stack(values).reshape(len(values), low, 2, 2, 2, columns, -1)
        return pick(split, far_bit, 2), flip(pick(split, 1 - far_bit, 2), 2)

    def route_end(mine, other):
        half = jnp.concatenate([mine, other], axis=5)
        return jnp.concatenate(
            [pick(half, core_bit, 2), flip(pick(half, 1 - core_bit, 2), 1)], axis=4
        )

    def weight_part(selected, source):
        return dot(selected, source, selected.ndim - 1, 1)

    low_bits = (ctx_size // 8).bit_length() - 1
    low_bit = lax.rem(ctx // REACH_PAIRS, 2)

    def first_leaving(routed, source):
        split = routed.reshape((routed.shape[0], low // 2, 2) + routed.shape[2:])
        return weight_part(pick(split, 1 - low_bit, 2), source).astype(bf16)

    def after_first(routed, source, arrived):
        split = routed.reshape((routed.shape[0], low // 2, 2) + routed.shape[2:])
        return (weight_part(pick(split, low_bit, 2), source) + arrived.astype(f32)).astype(bf16)

    def after_low(part):
        for k in range(1, low_bits):
            step = REACH_PAIRS << k
            bit = lax.rem(ctx // step, 2)
            split = part.reshape((part.shape[0], part.shape[1] // 2, 2) + part.shape[2:])
            arrived = flip(pick(split, 1 - bit, 2), step)
            part = (pick(split, bit, 2).astype(f32) + arrived.astype(f32)).astype(bf16)
        return pick(part[:, 0], side, 1), pick(part[:, 0], 1 - side, 1)

    same_side = side == ctx // (ctx_size // 2)

    def last_start(staying, arrived):
        mine = jnp.where(same_side, staying, arrived)
        return mine, flip(jnp.where(same_side, arrived, staying), ctx_size // 2)

    def last_end(mine, arrived):
        total = mine.astype(f32) + arrived.astype(f32)
        return total.reshape(-1, total.shape[-1])

    def halve(part, step):
        bit = lax.rem(ctx // step, 2)
        half = part.shape[0] // 2
        arrived = flip(lax.dynamic_slice_in_dim(part, (1 - bit) * half, half, 0), step)
        return lax.dynamic_slice_in_dim(part, bit * half, half, 0), arrived

    def halved(staying, arrived):
        total = staying.astype(f32) + arrived.astype(f32)
        return total if total.shape[0] == 1 else total.astype(bf16)

    def halving(part, step):
        while step < ctx_size:
            part = halved(*halve(part, step))
            step *= 2
        return part[0]

    enc_in, dec_in = enc_input.T, dec_input.T
    enc_arrived = swap(enc_in.astype(bf16))
    dec_arrived = swap(dec_in.astype(bf16))
    teacher_other = swap(
        jnp.pad(
            jnp.concatenate([teacher.T, valid_mask.astype(f32)[None]], axis=0).astype(bf16),
            ((0, 15), (0, 0)),
        )
    )
    enc_pair = ordered(enc_in, enc_arrived.astype(f32))
    dec_pair = ordered(dec_in, dec_arrived.astype(f32))
    enc_normed = root_norm(enc_pair, enc_norm_attn).astype(bf16)
    dec_normed = root_norm(dec_pair, dec_norm_self).astype(bf16)

    def project(normed, *weights):
        made = [dot(w, normed, 0, 0).astype(bf16) for w in weights]
        return made[0] if len(made) == 1 else jnp.concatenate(made, axis=0)

    enc_kv = project(enc_normed, enc_key, enc_value)
    dec_kv = project(dec_normed, dec_key, dec_value)
    enc_kv, enc_line, enc_back, dec_line, dec_back = together(
        enc_kv, enc_line, enc_back, dec_line, dec_back
    )
    enc_window, dec_window, enc_out_other = window_gather(
        1, [(enc_kv, BOTH), (dec_kv, BELOW)], [enc_out_proj]
    )
    enc_q = project(enc_normed, enc_query)
    dec_q = project(dec_normed, dec_query)

    enc_o, enc_att, enc_logs = attend(enc_q, enc_window, bounds_both, doc_lo, doc_hi, enc_line)
    enc_att_other = swap(enc_att)
    enc_att, dec_q = together(enc_att, dec_q)
    dec_o, dec_att, dec_logs = attend(dec_q, dec_window, bounds_below, doc_lo, positions, dec_line)
    dec_att_other = swap(dec_att)
    enc_att_other, dec_att, dec_out_here = together(enc_att_other, dec_att, dec_out_proj)
    dec_out_other = swap(dec_out_here)
    enc_mid = (
        enc_pair + dot(enc_out_proj, enc_att, 0, 0) + dot(enc_out_other, enc_att_other, 0, 0)
    )
    enc_ffn_in = root_norm(enc_mid, enc_norm_ff).astype(bf16)
    enc_weights = (enc_gate, enc_up, enc_down.T)
    partial, low_part, enc_hidden, enc_d1, enc_d2 = feed_forward(enc_ffn_in, enc_weights)
    low_part, dec_att, enc_hidden = together(low_part, dec_att, enc_hidden)
    branch = swap(low_part).astype(f32)

    enc_hidden_route = route_start(enc_hidden)
    enc_ffn_gather = gather_start(enc_ffn_in)
    dec_mid = (
        dec_pair + dot(dec_out_proj, dec_att, 0, 0) + dot(dec_out_other, dec_att_other, 0, 0)
    )
    cross_normed = root_norm(dec_mid, dec_norm_cross).astype(bf16)
    cross_q = project(cross_normed, cross_query)
    branch, cross_q = together(branch, cross_q)
    memory = (enc_mid + partial + branch).astype(bf16)
    cross_kv = project(memory, cross_key, cross_value)
    cross_window, cross_out_other = window_gather(2, [(cross_kv, BOTH)], [cross_out_proj])
    cross_o, cross_att, cross_logs = attend(
        cross_q, cross_window, bounds_both, doc_lo, doc_hi, None
    )
    cross_att_other = swap(cross_att)
    cross_att, enc_hidden_route, enc_ffn_gather, cross_query_here = together(
        cross_att, enc_hidden_route, enc_ffn_gather, cross_query
    )
    cross_query_other = swap(cross_query_here.T)
    enc_hidden_routed = route_end(*enc_hidden_route)
    cross_att_other, enc_hidden_routed = together(cross_att_other, enc_hidden_routed)
    dec_cross = (
        dec_mid + dot(cross_out_proj, cross_att, 0, 0) + dot(cross_out_other, cross_att_other, 0, 0)
    )
    dec_ffn_in = root_norm(dec_cross, dec_norm_ff).astype(bf16)
    dec_ffn_gather = gather_start(dec_ffn_in)
    dec_weights = (dec_gate, dec_up, dec_down.T)
    partial, low_part, dec_hidden, dec_d1, dec_d2 = feed_forward(dec_ffn_in, dec_weights)
    low_part, dec_hidden, cross_query_other, enc_ffn_gather = together(
        low_part, dec_hidden, cross_query_other, enc_ffn_gather
    )
    branch = swap(low_part).astype(f32)
    dec_hidden_route = route_start(dec_hidden)
    teacher_arrived = teacher_other.astype(f32)
    teacher_pair = ordered(teacher.T, teacher_arrived[:D])
    mask_pair = ordered(valid_mask.astype(f32)[None], teacher_arrived[D : D + 1])
    before = dec_cross + partial - teacher_pair
    enc_ffn_all = gather_end(*enc_ffn_gather)
    branch, before, enc_ffn_all = together(branch, before, enc_ffn_all)

    difference = before + branch
    grad_seed = difference * mask_pair

    dec_branch = grad_seed.astype(bf16)
    cross_key_here, dec_branch = together(cross_key, dec_branch)
    cross_key_other = swap(cross_key_here.T)
    partial, low_part, grad_gating, grad_upward = feed_backward(
        dec_branch, dec_weights, dec_d1, dec_d2
    )
    low_part, grad_gating, grad_upward, dec_hidden_route, dec_ffn_gather = together(
        low_part, grad_gating, grad_upward, dec_hidden_route, dec_ffn_gather
    )
    branch = swap(low_part).astype(f32)
    dec_gu_route = route_start(grad_gating, grad_upward)
    dec_hidden_routed = route_end(*dec_hidden_route)
    dec_ffn_all = gather_end(*dec_ffn_gather)
    dec_output = own(difference) + teacher.T
    branch, dec_hidden_routed, dec_ffn_all, dec_output = together(
        branch, dec_hidden_routed, dec_ffn_all, dec_output
    )
    part, g_dec_norm_ff = norm_backward(dec_cross, dec_norm_ff, partial + branch)
    grad_cross = grad_seed + part

    cross_branch = grad_cross.astype(bf16)
    qd, stats, cross_wide = prepare(cross_branch, cross_out_proj, cross_q, cross_o, cross_logs)
    qd_window, stat_window, cross_value_other = window_gather(
        3, [(qd, BOTH), (stats, BOTH)], [cross_value.T]
    )
    qd_window, dec_gu_route, dec_branch = together(qd_window, dec_gu_route, dec_branch)
    dec_branch_gather = gather_start(dec_branch)
    dec_gu_routed = route_end(*dec_gu_route)
    dec_gu_leaving = first_leaving(dec_gu_routed, dec_ffn_all)
    qd_window, dec_gu_leaving = together(qd_window, dec_gu_leaving)
    dec_gu_arrived = flip(dec_gu_leaving, REACH_PAIRS)
    cross_dkv = attend_keys(
        cross_kv, qd_window, stat_window, bounds_both, doc_lo, doc_hi, None
    )
    dkv_other = swap(cross_dkv)
    cross_dkv, qd = together(cross_dkv, qd)
    (cross_dq,) = attend_queries(
        qd, cross_window, bounds_both, doc_lo, doc_hi, cross_wide, None
    )
    grad_memory = dot(cross_key, cross_dkv[:width]) + dot(cross_value, cross_dkv[width:])
    dkv_other, cross_dq, grad_memory = together(dkv_other, cross_dq, grad_memory)
    dq_other = swap(cross_dq)
    grad_memory = (
        grad_memory
        + dot(cross_key_other, dkv_other[:width], 0, 0)
        + dot(cross_value_other, dkv_other[width:], 0, 0)
    )

    memory_branch = grad_memory.astype(bf16)
    partial, low_part, grad_gating, grad_upward = feed_backward(
        memory_branch, enc_weights, enc_d1, enc_d2
    )
    low_part, grad_gating, grad_upward, dec_branch_gather, dq_other = together(
        low_part, grad_gating, grad_upward, dec_branch_gather, dq_other
    )
    branch = swap(low_part).astype(f32)
    enc_gu_route = route_start(grad_gating, grad_upward)

    dec_branch_all = gather_end(*dec_branch_gather)
    dec_down_leaving = first_leaving(dec_hidden_routed, dec_branch_all)
    grad_normed = dot(cross_query, cross_dq) + dot(cross_query_other, dq_other, 0, 0)
    part, g_dec_norm_cross = norm_backward(dec_mid, dec_norm_cross, grad_normed)
    grad_mid = grad_cross + part
    self_branch = grad_mid.astype(bf16)
    self_qd, self_stats, self_wide = prepare(self_branch, dec_out_proj, dec_q, dec_o, dec_logs)
    self_qd, dec_down_leaving, dec_gu_arrived = together(self_qd, dec_down_leaving, dec_gu_arrived)
    dec_down_arrived = flip(dec_down_leaving, REACH_PAIRS)
    dec_gu_kept, dec_gu_sent = after_low(after_first(dec_gu_routed, dec_ffn_all, dec_gu_arrived))
    branch, dec_gu_sent, dec_gu_kept = together(branch, dec_gu_sent, dec_gu_kept)
    part, g_enc_norm_ff = norm_backward(enc_mid, enc_norm_ff, partial + branch)
    grad_enc_mid = grad_memory + part

    enc_branch = grad_enc_mid.astype(bf16)
    enc_qd, enc_stats, enc_wide = prepare(enc_branch, enc_out_proj, enc_q, enc_o, enc_logs)
    enc_qd_window, enc_stat_window, self_qd_window, self_stat_window, dec_gu_sent = window_gather(
        4,
        [(enc_qd, BOTH), (enc_stats, BOTH), (self_qd, ABOVE), (self_stats, ABOVE)],
        [dec_gu_sent],
    )
    dec_gu_last = last_start(dec_gu_kept, dec_gu_sent)
    enc_qd_window, enc_gu_route, memory_branch, dec_gu_mine = together(
        enc_qd_window, enc_gu_route, memory_branch, dec_gu_last[0]
    )
    enc_branch_gather = gather_start(memory_branch)
    enc_gu_routed = route_end(*enc_gu_route)
    enc_gu_leaving = first_leaving(enc_gu_routed, enc_ffn_all)
    enc_qd_window, enc_gu_leaving = together(enc_qd_window, enc_gu_leaving)
    enc_gu_arrived = flip(enc_gu_leaving, REACH_PAIRS)
    enc_dkv = attend_keys(
        enc_kv, enc_qd_window, enc_stat_window, bounds_both, doc_lo, doc_hi, enc_back
    )
    enc_dkv, enc_qd, dec_down_arrived = together(enc_dkv, enc_qd, dec_down_arrived)
    dec_down_kept, dec_down_sent = after_low(
        after_first(dec_hidden_routed, dec_branch_all, dec_down_arrived)
    )
    enc_qd, dec_down_sent, dec_down_kept = together(enc_qd, dec_down_sent, dec_down_kept)
    dec_down_other = swap(dec_down_sent)
    enc_dq, enc_grad_line = attend_queries(
        enc_qd, enc_window, bounds_both, doc_lo, doc_hi, enc_wide, enc_line
    )
    enc_grads = jnp.concatenate([enc_dq, enc_dkv], axis=0)
    enc_grads, self_qd_window, enc_branch_gather, dec_down_other = together(
        enc_grads, self_qd_window, enc_branch_gather, dec_down_other
    )
    enc_grads_other = swap(enc_grads)
    enc_branch_all = gather_end(*enc_branch_gather)
    enc_down_leaving = first_leaving(enc_hidden_routed, enc_branch_all)
    dec_down_last = last_start(dec_down_kept, dec_down_other)
    self_qd_window, enc_down_leaving, dec_down_mine = together(
        self_qd_window, enc_down_leaving, dec_down_last[0]
    )
    enc_down_arrived = flip(enc_down_leaving, REACH_PAIRS)
    self_dkv = attend_keys(
        dec_kv, self_qd_window, self_stat_window, bounds_above, positions, doc_hi, dec_back
    )
    self_dq, dec_grad_line = attend_queries(
        self_qd, dec_window, bounds_below, doc_lo, positions, self_wide, dec_line
    )
    self_grads = jnp.concatenate([self_dq, self_dkv], axis=0)
    self_grads, enc_grads_other, enc_att = together(self_grads, enc_grads_other, enc_att)
    self_grads_other = swap(self_grads)

    def blocks_of(*arguments):
        part = small_part(ctx_size, width, side, *arguments, True)
        return part.reshape(ctx_size, -1, part.shape[1])

    enc_part = blocks_of(
        [enc_grads, enc_att],
        [enc_grads_other, enc_att_other],
        [((0, 2), enc_normed), ((3, 3), enc_branch)],
    )
    enc_half = halve(enc_part, 1)
    enc_kept, self_grads_other, self_grads = together(enc_half[0], self_grads_other, self_grads)
    self_part = blocks_of(
        [self_grads, dec_att],
        [self_grads_other, dec_att_other],
        [((0, 2), dec_normed), ((3, 3), self_branch)],
    )
    self_half = halve(self_part, 1)
    enc_half = halve(halved(enc_kept, enc_half[1]), 2)
    self_kept, enc_kept, cross_att = together(self_half[0], enc_half[0], cross_att)
    cross_part = blocks_of(
        [cross_dq, cross_dkv, cross_att],
        [dq_other, dkv_other, cross_att_other],
        [((0, 0), cross_normed), ((1, 2), memory), ((3, 3), cross_branch)],
    )
    cross_half = halve(cross_part, 1)
    self_half = halve(halved(self_kept, self_half[1]), 2)
    cross_kept, self_kept, enc_gu_arrived = together(cross_half[0], self_half[0], enc_gu_arrived)

    enc_gu_kept, enc_gu_sent = after_low(after_first(enc_gu_routed, enc_ffn_all, enc_gu_arrived))
    enc_gu_other = swap(enc_gu_sent)
    cross_half = halve(halved(cross_kept, cross_half[1]), 2)
    enc_gu_kept, cross_kept, enc_kept, enc_arrived = together(
        enc_gu_kept, cross_half[0], enc_kept, enc_half[1]
    )
    enc_half = halve(halved(enc_kept, enc_arrived), 4)
    enc_partial = (
        dot(enc_query, enc_dq) + dot(enc_key, enc_dkv[:width]) + dot(enc_value, enc_dkv[width:])
    )
    self_partial = (
        dot(dec_query, self_dq) + dot(dec_key, self_dkv[:width]) + dot(dec_value, self_dkv[width:])
    )
    enc_other_low, self_other_low, enc_gu_other, enc_kept, enc_down_arrived = together(
        others(enc_partial).astype(bf16),
        others(self_partial).astype(bf16),
        enc_gu_other,
        enc_half[0],
        enc_down_arrived,
    )
    enc_gu_last = last_start(enc_gu_kept, enc_gu_other)
    enc_down_kept, enc_down_sent = after_low(
        after_first(enc_hidden_routed, enc_branch_all, enc_down_arrived)
    )
    enc_gu_mine, enc_down_kept, enc_down_sent, enc_other_low, self_other_low = together(
        enc_gu_last[0], enc_down_kept, enc_down_sent, enc_other_low, self_other_low
    )
    enc_down_other = swap(enc_down_sent)
    partial_other = swap(enc_other_low).astype(f32)
    part, g_enc_norm_attn = norm_backward(enc_in, enc_norm_attn, own(enc_partial) + partial_other)
    grad_enc_input = own(grad_enc_mid) + part
    self_kept, self_arrived, g_enc_norm_attn, enc_down_other = together(
        self_kept, self_half[1], g_enc_norm_attn, enc_down_other
    )
    enc_down_last = last_start(enc_down_kept, enc_down_other)
    self_half = halve(halved(self_kept, self_arrived), 4)
    partial_other = swap(self_other_low).astype(f32)
    part, g_dec_norm_self = norm_backward(dec_in, dec_norm_self, own(self_partial) + partial_other)
    grad_dec_input = own(grad_mid) + part
    loss_part = jnp.sum(own(grad_seed * difference))
    valid_part = jnp.sum(valid_mask.astype(f32))
    enc_down_mine, self_kept, g_dec_norm_self, loss_part, cross_kept, cross_arrived = together(
        enc_down_last[0], self_half[0], g_dec_norm_self, loss_part, cross_kept, cross_half[1]
    )
    cross_half = halve(halved(cross_kept, cross_arrived), 4)
    enc_shard = halving(halved(enc_kept, enc_half[1]), 8)
    self_shard = halving(halved(self_kept, self_half[1]), 8)
    cross_shard = halving(halved(*cross_half), 8)
    dec_gu, dec_down_rows = last_end(dec_gu_mine, dec_gu_last[1]), last_end(
        dec_down_mine, dec_down_last[1]
    )
    enc_gu, enc_down_rows = last_end(enc_gu_mine, enc_gu_last[1]), last_end(
        enc_down_mine, enc_down_last[1]
    )

    enc_bias_part = bucket_grads(enc_hot, enc_grad_line)
    dec_bias_part = bucket_grads(dec_hot, dec_grad_line)
    gains = jnp.concatenate(
        [
            g_enc_norm_attn,
            0.5 * g_enc_norm_ff,
            g_dec_norm_self,
            0.5 * g_dec_norm_cross,
            0.5 * g_dec_norm_ff,
        ]
    )
    small = jnp.concatenate(
        [
            gains,
            enc_bias_part.reshape(-1),
            dec_bias_part.reshape(-1),
            loss_part[None],
            valid_part[None],
        ]
    )
    small = total_over_devices(small, 6, ctx_size)
    squared_total, valid_total = small[-2], small[-1]
    teacher_loss = squared_total / (D * valid_total)
    scale = (own_rows * 2 * ctx_size) / valid_total
    small = small * scale
    gain = [small[i * D : (i + 1) * D] for i in range(5)]
    bias_size = enc_bias_part.size
    bias = [
        small[5 * D + i * bias_size : 5 * D + (i + 1) * bias_size].reshape(enc_bias_part.shape)
        for i in range(2)
    ]

    def pieces(shard, kinds):
        each = shard.shape[0] // len(kinds)
        made = []
        for i, transposed in enumerate(kinds):
            piece = shard[i * each : (i + 1) * each].astype(f32) * scale
            made.append(piece.T if transposed else piece)
        return made

    dec_gate_up = pieces(dec_gu, (True, True))
    dec_down_g = pieces(dec_down_rows, (False,))
    enc_gate_up = pieces(enc_gu, (True, True))
    enc_down_g = pieces(enc_down_rows, (False,))
    kinds = (True, True, True, False)
    enc_attn = pieces(enc_shard, kinds)
    dec_attn = pieces(self_shard, kinds) + pieces(cross_shard, kinds)
    return (
        teacher_loss,
        dec_output.T,
        (grad_enc_input * scale).T,
        (grad_dec_input * scale).T,
        gain[0],
        *enc_attn,
        gain[1],
        *enc_gate_up,
        *enc_down_g,
        bias[0],
        gain[2],
        *dec_attn[:4],
        gain[3],
        *dec_attn[4:],
        gain[4],
        *dec_gate_up,
        *dec_down_g,
        bias[1],
    )


def solution(mesh):
    rows = P(("ctx", "fsdp"), None)
    split_columns = P(None, "fsdp")
    split_rows = P("fsdp", None)
    attention_in = (split_columns,) * 3 + (split_rows,)
    feed_in = (split_columns,) * 2 + (split_rows,)
    in_specs = (
        (rows,) * 3
        + (P(("ctx", "fsdp")), P(), P(), P())
        + (P(),)
        + attention_in
        + (P(),)
        + feed_in
        + (P(), P())
        + attention_in
        + (P(),)
        + attention_in
        + (P(),)
        + feed_in
        + (P(),)
    )
    columns = P(None, ("ctx", "fsdp"))
    attention_out = (columns,) * 3 + (rows,)
    feed_out = (columns,) * 2 + (rows,)
    out_specs = (
        (P(),)
        + (rows,) * 3
        + (P(),)
        + attention_out
        + (P(),)
        + feed_out
        + (P(), P())
        + attention_out
        + (P(),)
        + attention_out
        + (P(),)
        + feed_out
        + (P(),)
    )
    return jax.shard_map(body, mesh=mesh, in_specs=in_specs, out_specs=out_specs, check_vma=False)
```

```python
import functools

import jax
import jax.numpy as jnp
from jax import lax
from jax.experimental import pallas as pl
from jax.experimental.pallas import tpu as pltpu
from jax.sharding import PartitionSpec as P

D = 1472
HEAD = 64
REACH_PAIRS = 4
WIN = 3 * REACH_PAIRS
epsilon = 1e-06
far_below = -1e30
bf16 = jnp.bfloat16
f32 = jnp.float32
MESH = pl.DeviceIdType.MESH
FEED_LIMIT = 16 * 1024 * 1024
SMALL_COST = pl.CostEstimate(flops=0, bytes_accessed=500_000, transcendentals=0)


def dot(left, right, left_dim=1, right_dim=0):
    return lax.dot_general(
        left, right, (((left_dim,), (right_dim,)), ((), ())), preferred_element_type=f32
    )


def swap(value):
    return lax.ppermute(value, "fsdp", [(0, 1), (1, 0)])


def flipped(index, bit):
    return index + bit - 2 * bit * lax.rem(index // bit, 2)


def window_kernel(flags, swaps, summed, *refs):
    arrays = len(flags)
    total = arrays + swaps
    given = total + (1 if summed else 0)
    ins, outs = refs[:given], refs[given : 2 * given]
    local_sem, send_sem, recv_sem, swap_send, swap_recv = refs[2 * given : 2 * given + 5]
    rounds = lax.axis_size("ctx").bit_length() if summed else 0
    if summed:
        sum_mine, sum_theirs, sum_send, sum_recv = refs[2 * given + 5 :]
    R = REACH_PAIRS
    ctx = lax.axis_index("ctx")
    fsdp = lax.axis_index("fsdp")
    groups = lax.axis_size("ctx") // R
    group = ctx // R
    place = lax.rem(ctx, R)
    near, far = flipped(place, 1), flipped(place, 2)
    dev_near, dev_far = group * R + near, group * R + far
    dev_up, dev_down = ctx + R, ctx - R
    has_up, has_down = group < groups - 1, group > 0
    barrier = pltpu.get_barrier_semaphore()

    def greet(device):
        pl.semaphore_signal(barrier, inc=1, device_id=(device, fsdp), device_id_type=MESH)

    greet(dev_near)
    greet(dev_far)
    if swaps:
        pl.semaphore_signal(barrier, inc=1, device_id=(ctx, 1 - fsdp), device_id_type=MESH)

    @pl.when(has_up)
    def _():
        greet(dev_up)

    @pl.when(has_down)
    def _():
        greet(dev_down)

    for k in range(2, rounds - 1):
        greet(flipped(ctx, 1 << k))

    greeted = 2 + (1 if swaps else 0) + max(rounds - 3, 0)
    pl.semaphore_wait(barrier, greeted + has_up.astype(jnp.int32) + has_down.astype(jnp.int32))

    def copies(number, source_slot, slot, device, use=lambda f: True, part=None):
        made = []
        for k, (below, above, split) in enumerate(flags):
            if not use(flags[k]):
                continue
            rows = ins[k].shape[0]
            cut = rows if not split else (rows // 2 if not (below and above) else 3 * rows // 8)
            where = {None: (0, rows), 0: (0, cut), 1: (cut, rows)}[part]
            if where[0] == where[1]:
                continue
            span = pl.ds(where[0], where[1] - where[0])
            source = ins[k] if source_slot is None else outs[k].at[source_slot, span]
            made.append(
                pltpu.make_async_remote_copy(
                    src_ref=source,
                    dst_ref=outs[k].at[slot, span],
                    send_sem=send_sem.at[k, number],
                    recv_sem=recv_sem.at[k, number],
                    device_id=(device, fsdp),
                    device_id_type=MESH,
                )
            )
        return made

    def start(made):
        for copy in made:
            copy.start()

    sums = [
        pltpu.make_async_remote_copy(
            src_ref=sum_mine.at[k],
            dst_ref=sum_theirs.at[k],
            send_sem=sum_send.at[k],
            recv_sem=sum_recv.at[k],
            device_id=(flipped(ctx, 1 << k), fsdp) if k < rounds - 1 else (ctx, 1 - fsdp),
            device_id_type=MESH,
        )
        for k in range(rounds)
    ]

    def sum_step(k):
        if k == 0:
            sum_mine[0] = ins[total][...]
        else:
            sums[k - 1].wait_recv()
            added = sum_mine[k - 1] + sum_theirs[k - 1]
            if k == rounds:
                outs[total][...] = added
            else:
                sum_mine[k] = added
        if k < rounds:
            sums[k].start()

    def arrived(made):
        for copy in made:
            copy.wait_recv()

    def left(made):
        for copy in made:
            copy.wait_send()

    below = lambda flag: flag[0]
    above = lambda flag: flag[1]
    to_up = copies(0, None, place, dev_up, below)
    to_down = copies(1, None, 2 * R + place, dev_down, above)
    to_far = copies(2, None, R + place, dev_far)
    to_near = copies(3, None, R + place, dev_near)
    far_low = copies(4, place, place, dev_far, below, 0)
    far_high = copies(5, 2 * R + place, 2 * R + place, dev_far, above, 0)
    up_far = copies(6, R + far, far, dev_up, below, 1)
    down_far = copies(7, R + far, 2 * R + far, dev_down, above, 1)
    near_low = copies(8, place, place, dev_near, below)
    near_high = copies(9, 2 * R + place, 2 * R + place, dev_near, above)
    near_far = copies(10, R + far, R + far, dev_near)
    near_far_low = copies(11, far, far, dev_near, below)
    near_far_high = copies(12, 2 * R + far, 2 * R + far, dev_near, above)
    own = [
        pltpu.make_async_copy(ins[k], outs[k].at[R + place], local_sem.at[k])
        for k in range(arrays)
    ]

    across = [
        pltpu.make_async_remote_copy(
            src_ref=ins[arrays + k],
            dst_ref=outs[arrays + k],
            send_sem=swap_send.at[k],
            recv_sem=swap_recv.at[k],
            device_id=(ctx, 1 - fsdp),
            device_id_type=MESH,
        )
        for k in range(swaps)
    ]

    @pl.when(has_up)
    def _():
        start(to_up)

    @pl.when(has_down)
    def _():
        start(to_down)

    if summed:
        sum_step(0)
    start(to_far)
    start(to_near)
    start(across)
    start(own)
    if summed:
        sum_step(1)
    arrived(to_far)
    if summed:
        sum_step(2)

    @pl.when(has_up)
    def _():
        start(up_far)

    @pl.when(has_down)
    def _():
        start(down_far)

    start(near_far)

    @pl.when(has_down)
    def _():
        arrived(to_up)
        start(far_low)
        start(near_low)

    @pl.when(has_up)
    def _():
        arrived(to_down)
        start(far_high)
        start(near_high)

    if summed:
        sum_step(3)

    @pl.when(has_down)
    def _():
        arrived(far_low)
        arrived(up_far)
        start(near_far_low)

    @pl.when(has_up)
    def _():
        arrived(far_high)
        arrived(down_far)
        start(near_far_high)

    arrived(to_near)
    arrived(near_far)

    @pl.when(has_down)
    def _():
        arrived(near_low)
        arrived(near_far_low)
        left(far_low)
        left(near_low)
        left(near_far_low)
        left(to_down)
        left(down_far)

    @pl.when(has_up)
    def _():
        arrived(near_high)
        arrived(near_far_high)
        left(far_high)
        left(near_high)
        left(near_far_high)
        left(to_up)
        left(up_far)

    left(to_far)
    left(to_near)
    left(near_far)
    for copy in own + across:
        copy.wait()
    if summed:
        for k in range(4, rounds + 1):
            sum_step(k)
        left(sums)


BOTH, BELOW, ABOVE = (True, True), (True, False), (False, True)


def window_gather(number, pairs, swapped=(), summand=None):
    values = [value for value, _ in pairs]
    flags = tuple(
        sides + (value.dtype == bf16 and value.shape[0] % 128 == 0,) for value, sides in pairs
    )
    count, swaps = len(values), len(swapped)
    vmem = pl.BlockSpec(memory_space=pltpu.VMEM)
    specs = [vmem] * count + [pl.BlockSpec(memory_space=pl.ANY)] * swaps
    extra, sum_scratch = [], []
    if summand is not None:
        specs = specs + [vmem]
        extra = [summand]
        rounds = lax.axis_size("ctx").bit_length()
        sum_scratch = [pltpu.VMEM((rounds,) + summand.shape, f32)] * 2 + [
            pltpu.SemaphoreType.DMA((rounds,))
        ] * 2
    return pl.pallas_call(
        functools.partial(window_kernel, flags, swaps, summand is not None),
        out_shape=[jax.ShapeDtypeStruct((WIN,) + v.shape, v.dtype) for v in values]
        + [jax.ShapeDtypeStruct(v.shape, v.dtype) for v in [*swapped, *extra]],
        in_specs=specs,
        out_specs=specs,
        scratch_shapes=[
            pltpu.SemaphoreType.DMA((count,)),
            pltpu.SemaphoreType.DMA((count, 13)),
            pltpu.SemaphoreType.DMA((count, 13)),
            pltpu.SemaphoreType.DMA((max(swaps, 1),)),
            pltpu.SemaphoreType.DMA((max(swaps, 1),)),
        ]
        + sum_scratch,
        compiler_params=pltpu.CompilerParams(
            collective_id=number, has_side_effects=True, vmem_limit_bytes=4 << 20
        ),
        cost_estimate=SMALL_COST,
        name="window_gather",
    )(*values, *swapped, *extra)


def total_kernel(rounds, sides, x_ref, o_ref, mine, theirs, send_sem, recv_sem):
    ctx = lax.axis_index("ctx")
    fsdp = lax.axis_index("fsdp")
    partners = [(flipped(ctx, 1 << k), fsdp) for k in range(rounds - sides)]
    partners += [(ctx, 1 - fsdp)] * sides
    barrier = pltpu.get_barrier_semaphore()
    for partner in partners:
        pl.semaphore_signal(barrier, inc=1, device_id=partner, device_id_type=MESH)
    pl.semaphore_wait(barrier, rounds)
    mine[0] = x_ref[...]
    for k, partner in enumerate(partners):
        copy = pltpu.make_async_remote_copy(
            src_ref=mine.at[k],
            dst_ref=theirs.at[k],
            send_sem=send_sem.at[k],
            recv_sem=recv_sem.at[k],
            device_id=partner,
            device_id_type=MESH,
        )
        copy.start()
        copy.wait()
        added = mine[k] + theirs[k]
        if k + 1 < rounds:
            mine[k + 1] = added
        else:
            o_ref[...] = added


def total_over_devices(value, number, ctx_size, sides=1):
    rounds = ctx_size.bit_length() - 1 + sides
    padded = -(-value.shape[0] // 1024) * 1024
    wide = jnp.pad(value, (0, padded - value.shape[0])).reshape(8, padded // 8)
    vmem = pl.BlockSpec(memory_space=pltpu.VMEM)
    made = pl.pallas_call(
        functools.partial(total_kernel, rounds, sides),
        out_shape=jax.ShapeDtypeStruct(wide.shape, f32),
        in_specs=[vmem],
        out_specs=vmem,
        scratch_shapes=[
            pltpu.VMEM((rounds,) + wide.shape, f32),
            pltpu.VMEM((rounds,) + wide.shape, f32),
            pltpu.SemaphoreType.DMA((rounds,)),
            pltpu.SemaphoreType.DMA((rounds,)),
        ],
        compiler_params=pltpu.CompilerParams(collective_id=number, has_side_effects=True),
        cost_estimate=SMALL_COST,
        name="total_over_devices",
    )(wide)
    return made.reshape(-1)[: value.shape[0]]


def head_rows(width):
    rows = lax.broadcasted_iota(jnp.int32, (width, 1), 0)
    return [(rows >= h * HEAD) & (rows < (h + 1) * HEAD) for h in range(width // HEAD)]


def head_lanes(width):
    lanes = lax.broadcasted_iota(jnp.int32, (1, width), 1)
    return [(lanes >= h * HEAD) & (lanes < (h + 1) * HEAD) for h in range(width // HEAD)]


def only(value, mask):
    return jnp.where(mask, value, jnp.zeros_like(value))


def by_token(value):
    width, rows = value.shape
    full = -(-width // 128) * 128
    return jnp.concatenate([value, jnp.zeros((full - width, rows), value.dtype)], axis=0).T[:, :width]


def toeplitz(line_ref, head, block, rows):
    start = pl.multiple_of(block * rows, rows)
    segment = line_ref[pl.ds(head, 1), pl.ds(start, 2 * rows)]
    spread = jnp.broadcast_to(segment, (rows, 2 * rows))
    return pltpu.roll(spread, rows + 1, 1, stride=1, stride_axis=0)[:, :rows]


def halves(value, op):
    half = value.shape[1] // 2
    return op(value[:, :half], value[:, half:])


def forward_kernel(biased, bounds, q_ref, kv_ref, lo_ref, hi_ref, *rest):
    if biased:
        line_ref, rest = rest[0], rest[1:]
    o_ref, att_ref, l_ref, s_ref, m_ref, sum_ref, acc_ref, rest_ref = rest
    width, rows = q_ref.shape
    heads = width // HEAD
    lanes, bands = head_lanes(width), head_rows(width)
    first, last, key_base = bounds[0], bounds[1], bounds[2]
    lo, hi = lo_ref[...], hi_ref[...]
    m_ref[...] = jnp.full_like(m_ref, far_below)
    sum_ref[...] = jnp.zeros_like(sum_ref)
    acc_ref[...] = jnp.zeros_like(acc_ref)
    q = by_token(q_ref[...])

    def scores(block, carry):
        keys = kv_ref[block, :width]
        key_pos = key_base + block * rows + lax.broadcasted_iota(jnp.int32, (rows, rows), 1)
        allowed = (key_pos >= lo) & (key_pos <= hi)
        for h in range(heads):
            s = dot(only(q, lanes[h]), keys)
            if biased:
                s = s + toeplitz(line_ref, h, block, rows)
            s = jnp.where(allowed, s, far_below)
            s_ref[block, h] = s
            m_ref[h] = jnp.maximum(m_ref[h], halves(s, jnp.maximum))
        return carry

    lax.fori_loop(first, last + 1, scores, 0)
    tops = [jnp.max(m_ref[h], axis=1, keepdims=True) for h in range(heads)]

    def weigh(block, carry):
        for h in range(heads):
            p = jnp.exp(s_ref[block, h] - tops[h])
            s_ref[block, h] = p
            sum_ref[h] += halves(p, jnp.add)
        return carry

    lax.fori_loop(first, last + 1, weigh, 0)
    totals = [jnp.sum(sum_ref[h], axis=1, keepdims=True) for h in range(heads)]
    shares = [1.0 / total for total in totals]
    rest_ref[...] = jnp.zeros_like(rest_ref)

    def mix(block, carry):
        values = kv_ref[block, width:]
        total, left = None, None
        for h in range(heads):
            p = s_ref[block, h] * shares[h]
            low_p = p.astype(bf16)
            band = only(values, bands[h])
            part = dot(band, low_p, 1, 1)
            rest_part = dot(band, (p - low_p.astype(f32)).astype(bf16), 1, 1)
            total = part if total is None else total + part
            left = rest_part if left is None else left + rest_part
        acc_ref[...] += total
        rest_ref[...] += left
        return carry

    lax.fori_loop(first, last + 1, mix, 0)
    column = lax.broadcasted_iota(jnp.int32, (rows, 128), 1)
    logs = jnp.zeros((rows, 128), f32)
    for h in range(heads):
        logs = jnp.where(column == h, tops[h] + jnp.log(totals[h]), logs)
    o_ref[...] = acc_ref[...] + rest_ref[...]
    att_ref[...] = acc_ref[...].astype(bf16)
    l_ref[...] = logs.T[:8]


def query_kernel(biased, bounds, qd_ref, kv_ref, lo_ref, hi_ref, stat_ref, *rest):
    if biased:
        line_ref, dq_ref, gline_ref, acc_ref = rest
        gline_ref[...] = jnp.zeros_like(gline_ref)
    else:
        dq_ref, acc_ref = rest
    width, rows = qd_ref.shape[0] // 2, qd_ref.shape[1]
    heads = width // HEAD
    lanes, bands = head_lanes(width), head_rows(width)
    first, last, key_base = bounds[0], bounds[1], bounds[2]
    lo, hi = lo_ref[...], hi_ref[...]
    acc_ref[...] = jnp.zeros_like(acc_ref)
    q, da = by_token(qd_ref[:width]), by_token(qd_ref[width:])
    logs = [stat_ref[:, h : h + 1] for h in range(heads)]
    deltas = [stat_ref[:, heads + h : heads + h + 1] for h in range(heads)]

    def step(block, carry):
        keys = kv_ref[block, :width]
        values = kv_ref[block, width:]
        key_pos = key_base + block * rows + lax.broadcasted_iota(jnp.int32, (rows, rows), 1)
        allowed = (key_pos >= lo) & (key_pos <= hi)
        total = None
        for h in range(heads):
            s = dot(only(q, lanes[h]), keys)
            if biased:
                s = s + toeplitz(line_ref, h, block, rows)
            p = jnp.exp(jnp.where(allowed, s - logs[h], far_below))
            dp = dot(only(da, lanes[h]), values)
            ds = (p * (dp - deltas[h])).astype(bf16)
            part = dot(only(keys, bands[h]), ds, 1, 1)
            total = part if total is None else total + part
            if biased:
                folded = jnp.concatenate([ds.astype(f32), jnp.zeros((rows, rows), f32)], axis=1)
                half = rows // 2
                while half >= 1:
                    folded = pltpu.roll(folded[:half], half, 1) + folded[half:]
                    half //= 2
                start = pl.multiple_of(block * rows, rows)
                gline_ref[pl.ds(h, 1), pl.ds(start, 2 * rows)] += folded
        acc_ref[...] += total
        return carry

    lax.fori_loop(first, last + 1, step, 0)
    dq_ref[...] = acc_ref[...].astype(bf16)


def key_kernel(biased, bounds, kv_ref, qd_ref, stat_ref, lo_ref, hi_ref, *rest):
    if biased:
        line_ref, rest = rest[0], rest[1:]
    dkv_ref, dk_acc, dv_acc = rest
    width, rows = kv_ref.shape[0] // 2, kv_ref.shape[1]
    heads = width // HEAD
    lanes, bands = head_lanes(width), head_rows(width)
    first, last, query_base = bounds[0], bounds[1], bounds[2]
    lo, hi = lo_ref[...], hi_ref[...]
    dk_acc[...] = jnp.zeros_like(dk_acc)
    dv_acc[...] = jnp.zeros_like(dv_acc)
    keys, values = by_token(kv_ref[:width]), by_token(kv_ref[width:])

    def step(block, carry):
        q = qd_ref[block, :width]
        da = qd_ref[block, width:]
        query_pos = query_base + block * rows + lax.broadcasted_iota(jnp.int32, (rows, rows), 1)
        allowed = (query_pos >= lo) & (query_pos <= hi)
        total_k = None
        total_v = None
        for h in range(heads):
            s = dot(only(keys, lanes[h]), q)
            if biased:
                s = s + toeplitz(line_ref, h, block, rows)
            p = jnp.exp(jnp.where(allowed, s - stat_ref[block, h : h + 1, :], far_below))
            dp = dot(only(values, lanes[h]), da)
            ds = (p * (dp - stat_ref[block, heads + h : heads + h + 1, :])).astype(bf16)
            part_k = dot(only(q, bands[h]), ds, 1, 1)
            part_v = dot(only(da, bands[h]), p.astype(bf16), 1, 1)
            total_k = part_k if total_k is None else total_k + part_k
            total_v = part_v if total_v is None else total_v + part_v
        dk_acc[...] += total_k
        dv_acc[...] += total_v
        return carry

    lax.fori_loop(first, last + 1, step, 0)
    dkv_ref[:width] = dk_acc[...].astype(bf16)
    dkv_ref[width:] = dv_acc[...].astype(bf16)


def local_call(kernel, out_shape, scratch, name, limit, bounds, *values):
    vmem = pl.BlockSpec(memory_space=pltpu.VMEM)
    smem = pl.BlockSpec(memory_space=pltpu.SMEM)
    return pl.pallas_call(
        kernel,
        out_shape=out_shape,
        in_specs=[smem] + [vmem] * len(values),
        out_specs=jax.tree.map(lambda _: vmem, out_shape),
        scratch_shapes=scratch,
        compiler_params=pltpu.CompilerParams(vmem_limit_bytes=limit << 20),
        cost_estimate=SMALL_COST,
        name=name,
    )(bounds, *values)


def attend(q, kv_window, bounds, lo, hi, line):
    width, rows = q.shape
    heads = width // HEAD
    biased = line is not None
    return local_call(
        functools.partial(forward_kernel, biased),
        [
            jax.ShapeDtypeStruct((width, rows), f32),
            jax.ShapeDtypeStruct((width, rows), bf16),
            jax.ShapeDtypeStruct((8, rows), f32),
        ],
        [
            pltpu.VMEM((WIN, heads, rows, rows), f32),
            pltpu.VMEM((heads, rows, rows // 2), f32),
            pltpu.VMEM((heads, rows, rows // 2), f32),
            pltpu.VMEM((width, rows), f32),
            pltpu.VMEM((width, rows), f32),
        ],
        "attend_forward",
        20,
        bounds,
        q,
        kv_window,
        lo,
        hi,
        *([line] if biased else []),
    )


def attend_queries(qd, kv_window, bounds, lo, hi, stats, line):
    width, rows = qd.shape[0] // 2, qd.shape[1]
    biased = line is not None
    shapes = [jax.ShapeDtypeStruct((width, rows), bf16)]
    if biased:
        shapes.append(jax.ShapeDtypeStruct(line.shape, f32))
    return local_call(
        functools.partial(query_kernel, biased),
        shapes,
        [pltpu.VMEM((width, rows), f32)],
        "attend_queries",
        14,
        bounds,
        qd,
        kv_window,
        lo,
        hi,
        stats,
        *([line] if biased else []),
    )


def attend_keys(kv, qd_window, stat_window, bounds, lo, hi, line):
    width, rows = kv.shape[0] // 2, kv.shape[1]
    biased = line is not None
    return local_call(
        functools.partial(key_kernel, biased),
        jax.ShapeDtypeStruct((2 * width, rows), bf16),
        [pltpu.VMEM((width, rows), f32)] * 2,
        "attend_keys",
        14,
        bounds,
        kv,
        qd_window,
        stat_window,
        lo,
        hi,
        *([line] if biased else []),
    )


def prepare_kernel(grad_ref, w_ref, q_ref, o_ref, log_ref, qd_ref, row_ref, wide_ref):
    width, rows = q_ref.shape
    heads = width // HEAD
    da = dot(w_ref[...], grad_ref[...]).astype(bf16)
    qd_ref[:width] = q_ref[...]
    qd_ref[width:] = da
    product = da.astype(f32) * o_ref[...]
    row = lax.broadcasted_iota(jnp.int32, (128, rows), 0)
    stats = jnp.concatenate([log_ref[...], jnp.zeros((120, rows), f32)], axis=0)
    for h, mask in enumerate(head_rows(width)):
        delta = jnp.sum(only(product, mask), axis=0, keepdims=True)
        stats = jnp.where(row == heads + h, delta, stats)
    row_ref[...] = stats[:8]
    wide_ref[...] = stats.T


def prepare(grad, w_out, q, out, log_rows):
    width, rows = q.shape
    vmem = pl.BlockSpec(memory_space=pltpu.VMEM)
    return pl.pallas_call(
        prepare_kernel,
        out_shape=[
            jax.ShapeDtypeStruct((2 * width, rows), bf16),
            jax.ShapeDtypeStruct((8, rows), f32),
            jax.ShapeDtypeStruct((rows, 128), f32),
        ],
        in_specs=[vmem] * 5,
        out_specs=[vmem] * 3,
        compiler_params=pltpu.CompilerParams(vmem_limit_bytes=10 << 20),
        cost_estimate=SMALL_COST,
        name="attention_prepare",
    )(grad, w_out, q, out, log_rows)


KINDS = 4


def small_kernel(blocks, width, layout, place, *refs):
    out_ref = refs[-1]
    columns = width // blocks
    side = place[0]
    row = lax.broadcasted_iota(jnp.int32, (blocks * KINDS * columns, 1), 0)
    left, block = row // (KINDS * columns), jnp.zeros_like(row)
    for _ in range(blocks.bit_length() - 1):
        block = 2 * block + lax.rem(left, 2)
        left = left // 2
    kind = lax.rem(row // columns, KINDS)
    column = columns * (2 * block + side) + lax.rem(row, columns)
    away = jnp.where(column // width == side, 0, 1)
    wanted = away * (KINDS * width) + kind * width + lax.rem(column, width)
    used = 0
    for number, (counted, kinds) in enumerate(layout):
        values = jnp.concatenate([ref[...] for ref in refs[used : used + counted]], axis=0)
        sources = refs[used + counted : used + counted + len(kinds)]
        used += counted + len(kinds)
        spot = lax.broadcasted_iota(jnp.int32, (1, values.shape[0]), 1)
        onehot = jnp.where(wanted == spot, 1.0, 0.0).astype(bf16)
        chosen = dot(onehot, values).astype(bf16)
        total = None
        for (first, last), source in zip(kinds, sources):
            part = dot(only(chosen, (kind >= first) & (kind <= last)), source[...], 1, 1)
            total = part if total is None else total + part
        total = total.astype(bf16)
        depth = KINDS * columns
        for index in range(blocks):
            out_ref[index, number * depth : (number + 1) * depth] = total[
                index * depth : (index + 1) * depth
            ]


def small_parts(blocks, width, side, parts):
    vmem = pl.BlockSpec(memory_space=pltpu.VMEM)
    smem = pl.BlockSpec(memory_space=pltpu.SMEM)
    layout, values = [], []
    for own, other, sources in parts:
        layout.append((len(own) + len(other), tuple(span for span, _ in sources)))
        values += [*own, *other, *[source for _, source in sources]]
    depth = parts[0][2][0][1].shape[0]
    rows = len(parts) * KINDS * (width // blocks)
    return pl.pallas_call(
        functools.partial(small_kernel, blocks, width, tuple(layout)),
        out_shape=jax.ShapeDtypeStruct((blocks, rows, depth), bf16),
        in_specs=[smem] + [vmem] * len(values),
        out_specs=vmem,
        compiler_params=pltpu.CompilerParams(vmem_limit_bytes=28 << 20),
        cost_estimate=SMALL_COST,
        name="attention_weight_part",
    )(jnp.stack([side]), *values)


CHUNK = 256
GELU_RATE = 0.7978845608028654
GELU_CUBE = 0.044715


def feed_kernel(x_ref, gate_ref, up_ref, down_ref, sum_ref, low_ref, hidden_ref, d1_ref, d2_ref):
    x = x_ref[...].T
    for start in range(0, gate_ref.shape[1], CHUNK):
        span = slice(start, start + CHUNK)
        gating = dot(x, gate_ref[:, span]).T
        upward = dot(x, up_ref[:, span]).T
        square = gating * gating
        t = jnp.tanh(GELU_RATE * gating * (1.0 + GELU_CUBE * square))
        half = 0.5 * (1.0 + t)
        unit = gating * half
        slope = half + 0.5 * gating * (1.0 - t * t) * (
            GELU_RATE * (1.0 + 3.0 * GELU_CUBE * square)
        )
        hidden_ref[span, :] = (unit * upward).astype(bf16)
        d1_ref[span, :] = slope * upward
        d2_ref[span, :] = unit
    total = dot(down_ref[...], hidden_ref[...])
    sum_ref[...] = total
    low_ref[...] = total.astype(bf16)


def feed_back_kernel(e_ref, gate_ref, up_ref, down_ref, d1_ref, d2_ref, sum_ref, low_ref, gg_ref, gu_ref):
    e = e_ref[...].T
    for start in range(0, gate_ref.shape[1], CHUNK):
        span = slice(start, start + CHUNK)
        grad_hidden = dot(e, down_ref[:, span]).astype(bf16).astype(f32).T
        gg_ref[span, :] = (grad_hidden * d1_ref[span, :]).astype(bf16)
        gu_ref[span, :] = (grad_hidden * d2_ref[span, :]).astype(bf16)
    total = dot(gate_ref[...], gg_ref[...]) + dot(up_ref[...], gu_ref[...])
    sum_ref[...] = total
    low_ref[...] = total.astype(bf16)


def feed_call(kernel, name, source, weights, chunked, outs):
    depth, rows = source.shape
    columns = weights[0].shape[1]
    vmem = pl.BlockSpec(memory_space=pltpu.VMEM)
    return pl.pallas_call(
        kernel,
        out_shape=[
            jax.ShapeDtypeStruct((depth, rows), f32),
            jax.ShapeDtypeStruct((depth, rows), bf16),
        ]
        + [jax.ShapeDtypeStruct((columns, rows), kind) for kind in outs],
        in_specs=[vmem] * (4 + len(chunked)),
        out_specs=[vmem] * (2 + len(outs)),
        compiler_params=pltpu.CompilerParams(vmem_limit_bytes=FEED_LIMIT),
        cost_estimate=SMALL_COST,
        name=name,
    )(source, *weights, *chunked)


def feed_forward(source, weights):
    return feed_call(feed_kernel, "feed_forward", source, weights, (), (bf16, f32, f32))


def feed_backward(grad, weights, d1, d2):
    return feed_call(feed_back_kernel, "feed_backward", grad, weights, (d1, d2), (bf16, bf16))


def last_kernel(
    part_ref, gu_ref, leave_ref, stay_ref, dec_ref, small_ref,
    both_out, gu_out, down_out, dec_out, small_out,
    near_r, near_s, far_r, far_s, z_r, z_s, top_r,
    gu_x, gu_send, gu_top, down_z, down_sum, down_x, down_send, down_top,
    dec_x, dec_send, dec_top, mine, theirs, send_sem, recv_sem,
):
    ctx = lax.axis_index("ctx")
    side = lax.axis_index("fsdp")
    bits = [lax.rem(ctx // step, 2) for step in (1, 2, 4, 8)]
    across = (ctx, 1 - side)
    partners = [(flipped(ctx, step), side) for step in (1, 2, 4, 8)]
    same = side == bits[3]
    barrier = pltpu.get_barrier_semaphore()
    for device in [across] + partners:
        pl.semaphore_signal(barrier, inc=1, device_id=device, device_id_type=MESH)
    pl.semaphore_wait(barrier, 5)

    def copy(number, source, target, device):
        made = pltpu.make_async_remote_copy(
            src_ref=source,
            dst_ref=target,
            send_sem=send_sem.at[number],
            recv_sem=recv_sem.at[number],
            device_id=device,
            device_id_type=MESH,
        )
        made.start()
        return made

    def added(kept, arrived):
        return kept.astype(f32) + arrived.astype(f32)

    def small_copy(k, device):
        return copy(9 if k == 4 else 12 + k, mine.at[k], theirs.at[k], device)

    def small_sum(k, made):
        made.wait_recv()
        total = mine[k] + theirs[k]
        if k < 4:
            mine[k + 1] = total
        else:
            small_out[...] = total

    near = copy(0, part_ref.at[pl.ds((1 - bits[0]) * 8, 8)], near_r, partners[0])
    mine[0] = small_ref[...]
    small_top = small_copy(0, partners[3])
    dec_across = copy(1, dec_ref.at[1 - side], dec_x, across)
    gu_across = copy(2, gu_ref.at[1 - side], gu_x, across)
    small_sum(0, small_top)
    small_z = small_copy(1, partners[2])
    down_first = copy(3, leave_ref, down_z, partners[2])

    near.wait_recv()
    near_s[...] = added(part_ref[pl.ds(bits[0] * 8, 8)], near_r[...]).astype(bf16)
    small_sum(1, small_z)
    small_far = small_copy(2, partners[1])
    far = copy(4, near_s.at[pl.ds((1 - bits[1]) * 4, 4)], far_r, partners[1])
    small_sum(2, small_far)
    small_near = small_copy(3, partners[0])

    dec_across.wait_recv()
    dec_send[...] = jnp.where(same, dec_x[...], dec_ref[side])
    dec_last = copy(5, dec_send, dec_top, partners[3])
    gu_across.wait_recv()
    gu_send[...] = jnp.where(same, gu_x[...], gu_ref[side])
    gu_last = copy(6, gu_send, gu_top, partners[3])
    small_sum(3, small_near)
    small_across = small_copy(4, across)
    down_first.wait_recv()
    down_sum[...] = added(stay_ref[...], down_z[...]).astype(bf16)
    down_across = copy(7, down_sum.at[1 - side], down_x, across)
    down_across.wait_recv()
    down_send[...] = jnp.where(same, down_x[...], down_sum[side])
    down_last = copy(8, down_send, down_top, partners[3])
    small_sum(4, small_across)

    far.wait_recv()
    far_s[...] = added(near_s[pl.ds(bits[1] * 4, 4)], far_r[...]).astype(bf16)
    z = copy(10, far_s.at[pl.ds((1 - bits[2]) * 2, 2)], z_r, partners[2])
    dec_last.wait_recv()
    dec_out[...] = added(jnp.where(same, dec_ref[side], dec_x[...]), dec_top[...])
    z.wait_recv()
    z_s[...] = added(far_s[pl.ds(bits[2] * 2, 2)], z_r[...]).astype(bf16)
    top = copy(11, z_s.at[1 - bits[3]], top_r, partners[3])
    gu_last.wait_recv()
    gu_out[...] = added(jnp.where(same, gu_ref[side], gu_x[...]), gu_top[...])
    down_last.wait_recv()
    down_out[...] = added(jnp.where(same, down_sum[side], down_x[...]), down_top[...])
    top.wait_recv()
    both_out[...] = added(z_s[bits[3]], top_r[...])
    for made in (
        near, dec_across, gu_across, down_first, far, dec_last, gu_last,
        down_across, down_last, z, top, small_top, small_z, small_far, small_near, small_across,
    ):
        made.wait_send()


def last_exchanges(number, part, gu, leave, stay, dec, small):
    blocks, rows, depth = part.shape
    vmem = pl.BlockSpec(memory_space=pltpu.VMEM)
    wide, narrow = gu.shape[1], dec.shape[1]
    return pl.pallas_call(
        last_kernel,
        out_shape=[
            jax.ShapeDtypeStruct((rows, depth), f32),
            jax.ShapeDtypeStruct((wide, depth), f32),
            jax.ShapeDtypeStruct((narrow, depth), f32),
            jax.ShapeDtypeStruct((narrow, depth), f32),
            jax.ShapeDtypeStruct(small.shape, f32),
        ],
        in_specs=[vmem] * 6,
        out_specs=[vmem] * 5,
        scratch_shapes=[
            pltpu.VMEM((size, rows, depth), bf16)
            for size in (blocks // 2, blocks // 2, blocks // 4, blocks // 4, blocks // 8, blocks // 8)
        ]
        + [pltpu.VMEM((rows, depth), bf16)]
        + [pltpu.VMEM((wide, depth), bf16)] * 3
        + [pltpu.VMEM((2, narrow, depth), bf16)] * 2
        + [pltpu.VMEM((narrow, depth), bf16)] * 6
        + [pltpu.VMEM((5,) + small.shape, f32)] * 2
        + [pltpu.SemaphoreType.DMA((16,)), pltpu.SemaphoreType.DMA((16,))],
        compiler_params=pltpu.CompilerParams(
            collective_id=number, has_side_effects=True, vmem_limit_bytes=28 << 20
        ),
        cost_estimate=SMALL_COST,
        name="last_exchanges",
    )(part, gu, leave, stay, dec, small)


def inverse_root(inputs):
    return lax.rsqrt(jnp.mean(inputs * inputs, axis=0, keepdims=True) + epsilon)


def root_norm(inputs, gain):
    return inputs * inverse_root(inputs) * gain[:, None]


def norm_backward(inputs, gain, grad):
    inverse = inverse_root(inputs)
    scaled = grad * gain[:, None]
    along = jnp.mean(inputs * scaled, axis=0, keepdims=True)
    grad_inputs = inverse * scaled - inputs * (inverse * inverse * inverse) * along
    return grad_inputs, jnp.sum(grad * inputs * inverse, axis=1)


def body(
    enc_input,
    dec_input,
    teacher,
    valid_mask,
    doc_lengths,
    enc_buckets,
    dec_buckets,
    enc_norm_attn,
    enc_query,
    enc_key,
    enc_value,
    enc_out_proj,
    enc_norm_ff,
    enc_gate,
    enc_up,
    enc_down,
    enc_rel_bias,
    dec_norm_self,
    dec_query,
    dec_key,
    dec_value,
    dec_out_proj,
    dec_norm_cross,
    cross_query,
    cross_key,
    cross_value,
    cross_out_proj,
    dec_norm_ff,
    dec_gate,
    dec_up,
    dec_down,
    dec_rel_bias,
):
    ctx = lax.axis_index("ctx")
    side = lax.axis_index("fsdp")
    ctx_size = lax.axis_size("ctx")
    own_rows = enc_input.shape[0]
    rows = 2 * own_rows
    width = enc_query.shape[1]
    heads = width // HEAD
    place = lax.rem(ctx, REACH_PAIRS)
    core_bit, far_bit = lax.rem(place, 2), place // 2

    def ordered(mine, other, axis=1):
        first = side == 0
        return jnp.concatenate(
            [jnp.where(first, mine, other), jnp.where(first, other, mine)], axis=axis
        )

    def pick(value, index, axis):
        return lax.dynamic_index_in_dim(value, index, axis, keepdims=False)

    def flip(value, bit):
        return lax.ppermute(value, "ctx", [(i, i ^ bit) for i in range(ctx_size)])

    def own(value):
        return lax.dynamic_slice_in_dim(value, side * own_rows, own_rows, 1)

    def others(value):
        return lax.dynamic_slice_in_dim(value, (1 - side) * own_rows, own_rows, 1)

    def together(*values):
        return lax.optimization_barrier(values)

    count = doc_lengths.shape[0]
    order = jnp.arange(count, dtype=jnp.int32)
    starts = jnp.sum(
        jnp.where(order[None, :] < order[:, None], doc_lengths[None, :], 0), axis=1
    )
    ends = starts + doc_lengths
    positions = ctx * rows + jnp.arange(rows, dtype=jnp.int32)[:, None]
    doc_lo = jnp.max(jnp.where(starts[None, :] <= positions, starts[None, :], 0), axis=1, keepdims=True)
    doc_hi = (
        jnp.min(
            jnp.where(ends[None, :] > positions, ends[None, :], ctx_size * rows),
            axis=1,
            keepdims=True,
        )
        - 1
    )
    base_block = ctx - place - REACH_PAIRS
    first_block = doc_lo[0, 0] // rows - base_block
    last_block = doc_hi[rows - 1, 0] // rows - base_block
    own_block = REACH_PAIRS + place
    base_pos = base_block * rows
    bounds_both = jnp.stack([first_block, last_block, base_pos])
    bounds_below = jnp.stack([first_block, own_block, base_pos])
    bounds_above = jnp.stack([own_block, last_block, base_pos])

    reach = enc_buckets.shape[0] // 2
    line_len = (WIN + 1) * rows
    pad_lo, pad_hi = reach, reach + rows
    line_start = (reach + 1 - rows) + pad_lo - rows * (REACH_PAIRS + place)
    reverse_start = (reach - rows) + pad_lo - rows * (REACH_PAIRS + place)

    def lines(rel_bias, buckets):
        hot = (
            buckets[:, None] == jnp.arange(rel_bias.shape[0], dtype=jnp.int32)[None, :]
        ).astype(f32)
        mine = lax.dynamic_slice_in_dim(rel_bias, side * heads, heads, 1)
        line = lax.dot_general(
            mine, hot, (((0,), (1,)), ((), ())), precision=lax.Precision.HIGHEST
        )
        hot_back = (
            buckets[::-1][:, None] == jnp.arange(rel_bias.shape[0], dtype=jnp.int32)[None, :]
        ).astype(f32)
        line_back = lax.dot_general(
            mine, hot_back, (((0,), (1,)), ((), ())), precision=lax.Precision.HIGHEST
        )
        padded = jnp.pad(line, ((0, 8 - heads), (pad_lo, pad_hi)))
        backward = jnp.pad(line_back, ((0, 8 - heads), (pad_lo, pad_hi)))
        return (
            hot,
            lax.dynamic_slice_in_dim(padded, line_start, line_len, 1),
            lax.dynamic_slice_in_dim(backward, reverse_start, line_len, 1),
        )

    enc_hot, enc_line, enc_back = lines(enc_rel_bias, enc_buckets)
    dec_hot, dec_line, dec_back = lines(dec_rel_bias, dec_buckets)

    def bucket_grads(hot, grad_line):
        padded = jnp.zeros((heads, 2 * reach + pad_lo + pad_hi), f32)
        padded = lax.dynamic_update_slice_in_dim(padded, grad_line[:heads], line_start, 1)
        cropped = padded[:, pad_lo : pad_lo + 2 * reach]
        grads = lax.dot_general(
            hot, cropped, (((0,), (1,)), ((), ())), precision=lax.Precision.HIGHEST
        )
        whole = jnp.zeros((hot.shape[1], 2 * heads), f32)
        return lax.dynamic_update_slice_in_dim(whole, grads, side * heads, 1)

    def gather_start(value):
        return value, flip(value, 2)

    def gather_end(value, far):
        both = jnp.concatenate([value, far], axis=1)
        return jnp.concatenate([both, flip(both, 1)], axis=1)

    low = ctx_size // 8

    def route_start(*values):
        columns = values[0].shape[0] // ctx_size
        split = jnp.stack(values).reshape(len(values), low, 2, 2, 2, columns, -1)
        return pick(split, far_bit, 2), flip(pick(split, 1 - far_bit, 2), 2)

    def route_end(mine, other):
        half = jnp.concatenate([mine, other], axis=5)
        return jnp.concatenate(
            [pick(half, core_bit, 2), flip(pick(half, 1 - core_bit, 2), 1)], axis=4
        )

    def weight_part(selected, source):
        return dot(selected, source, selected.ndim - 1, 1)

    low_bits = (ctx_size // 8).bit_length() - 1
    low_bit = lax.rem(ctx // REACH_PAIRS, 2)

    def first_leaving(routed, source):
        split = routed.reshape((routed.shape[0], low // 2, 2) + routed.shape[2:])
        return weight_part(pick(split, 1 - low_bit, 2), source).astype(bf16)

    def after_first(routed, source, arrived):
        split = routed.reshape((routed.shape[0], low // 2, 2) + routed.shape[2:])
        return (weight_part(pick(split, low_bit, 2), source) + arrived.astype(f32)).astype(bf16)

    def after_low(part):
        for k in range(1, low_bits):
            step = REACH_PAIRS << k
            bit = lax.rem(ctx // step, 2)
            split = part.reshape((part.shape[0], part.shape[1] // 2, 2) + part.shape[2:])
            arrived = flip(pick(split, 1 - bit, 2), step)
            part = (pick(split, bit, 2).astype(f32) + arrived.astype(f32)).astype(bf16)
        return pick(part[:, 0], side, 1), pick(part[:, 0], 1 - side, 1)

    same_side = side == ctx // (ctx_size // 2)

    def last_start(staying, arrived):
        mine = jnp.where(same_side, staying, arrived)
        return mine, flip(jnp.where(same_side, arrived, staying), ctx_size // 2)

    def last_end(mine, arrived):
        total = mine.astype(f32) + arrived.astype(f32)
        return total.reshape(-1, total.shape[-1])

    def halve(part, step):
        bit = lax.rem(ctx // step, 2)
        half = part.shape[0] // 2
        arrived = flip(lax.dynamic_slice_in_dim(part, (1 - bit) * half, half, 0), step)
        return lax.dynamic_slice_in_dim(part, bit * half, half, 0), arrived

    def halved(staying, arrived):
        total = staying.astype(f32) + arrived.astype(f32)
        return total if total.shape[0] == 1 else total.astype(bf16)

    def halving(part, step):
        while step < ctx_size:
            part = halved(*halve(part, step))
            step *= 2
        return part[0]

    enc_in, dec_in = enc_input.T, dec_input.T
    enc_arrived = swap(enc_in)
    dec_arrived = swap(dec_in)
    enc_pair = ordered(enc_in, enc_arrived)
    dec_pair = ordered(dec_in, dec_arrived)
    enc_normed = root_norm(enc_pair, enc_norm_attn).astype(bf16)
    dec_normed = root_norm(dec_pair, dec_norm_self).astype(bf16)

    def project(normed, *weights):
        made = [dot(w, normed, 0, 0).astype(bf16) for w in weights]
        return made[0] if len(made) == 1 else jnp.concatenate(made, axis=0)

    enc_kv = project(enc_normed, enc_key, enc_value)
    dec_kv = project(dec_normed, dec_key, dec_value)
    teacher_low = jnp.pad(
        jnp.concatenate([teacher.T, valid_mask.astype(f32)[None]], axis=0), ((0, 7), (0, 0))
    )
    enc_kv, enc_line, enc_back, dec_line, dec_back, teacher_low = together(
        enc_kv, enc_line, enc_back, dec_line, dec_back, teacher_low
    )
    enc_window, dec_window, enc_out_other = window_gather(
        1, [(enc_kv, BOTH), (dec_kv, BELOW)], [enc_out_proj]
    )
    enc_q = project(enc_normed, enc_query)
    dec_q = project(dec_normed, dec_query)

    enc_o, enc_att, enc_logs = attend(enc_q, enc_window, bounds_both, doc_lo, doc_hi, enc_line)
    enc_att_other = swap(enc_att)
    enc_att, dec_q = together(enc_att, dec_q)
    dec_o, dec_att, dec_logs = attend(dec_q, dec_window, bounds_below, doc_lo, positions, dec_line)
    dec_att_other = swap(dec_att)
    enc_att_other, dec_att, dec_out_here = together(enc_att_other, dec_att, dec_out_proj)
    dec_out_other = swap(dec_out_here)
    enc_mid = (
        enc_pair + dot(enc_out_proj, enc_att, 0, 0) + dot(enc_out_other, enc_att_other, 0, 0)
    )
    enc_ffn_in = root_norm(enc_mid, enc_norm_ff).astype(bf16)
    enc_weights = (enc_gate, enc_up, enc_down.T)
    partial, low_part, enc_hidden, enc_d1, enc_d2 = feed_forward(enc_ffn_in, enc_weights)
    low_part, dec_att, enc_hidden = together(low_part, dec_att, enc_hidden)
    branch = swap(low_part).astype(f32)

    enc_hidden_route = route_start(enc_hidden)
    enc_ffn_gather = gather_start(enc_ffn_in)
    dec_mid = (
        dec_pair + dot(dec_out_proj, dec_att, 0, 0) + dot(dec_out_other, dec_att_other, 0, 0)
    )
    cross_normed = root_norm(dec_mid, dec_norm_cross).astype(bf16)
    cross_q = project(cross_normed, cross_query)
    branch, cross_q = together(branch, cross_q)
    memory = (enc_mid + partial + branch).astype(bf16)
    cross_kv = project(memory, cross_key, cross_value)
    valid_count = jnp.broadcast_to(jnp.sum(valid_mask.astype(f32)), (8, 128))
    cross_window, cross_out_other, valid_tile = window_gather(
        2, [(cross_kv, BOTH)], [cross_out_proj], valid_count
    )
    valid_total = valid_tile[0, 0]
    scale = (rows * ctx_size) / valid_total
    cross_o, cross_att, cross_logs = attend(
        cross_q, cross_window, bounds_both, doc_lo, doc_hi, None
    )
    cross_att_other = swap(cross_att)
    cross_att, enc_hidden_route, enc_ffn_gather, teacher_low = together(
        cross_att, enc_hidden_route, enc_ffn_gather, teacher_low
    )
    teacher_other = swap(teacher_low)
    enc_hidden_routed = route_end(*enc_hidden_route)
    cross_att_other, enc_hidden_routed = together(cross_att_other, enc_hidden_routed)
    dec_cross = (
        dec_mid + dot(cross_out_proj, cross_att, 0, 0) + dot(cross_out_other, cross_att_other, 0, 0)
    )
    dec_ffn_in = root_norm(dec_cross, dec_norm_ff).astype(bf16)
    dec_ffn_gather = gather_start(dec_ffn_in)
    dec_weights = (dec_gate, dec_up, dec_down.T)
    partial, low_part, dec_hidden, dec_d1, dec_d2 = feed_forward(dec_ffn_in, dec_weights)
    low_part, dec_hidden, teacher_other, enc_ffn_gather = together(
        low_part, dec_hidden, teacher_other, enc_ffn_gather
    )
    mask_pair = ordered(valid_mask.astype(f32)[None], teacher_other[D : D + 1])
    branch = swap(low_part).astype(f32)
    dec_hidden_route = route_start(dec_hidden)
    teacher_pair = ordered(teacher.T, teacher_other[:D])
    before = dec_cross + partial - teacher_pair
    enc_ffn_all = gather_end(*enc_ffn_gather)
    branch, before, enc_ffn_all = together(branch, before, enc_ffn_all)

    difference = before + branch
    grad_seed = difference * (mask_pair * scale)

    dec_branch = grad_seed.astype(bf16)
    cross_key_here, dec_branch = together(cross_key, dec_branch)
    cross_key_other = swap(cross_key_here.T)
    partial, low_part, grad_gating, grad_upward = feed_backward(
        dec_branch, dec_weights, dec_d1, dec_d2
    )
    low_part, grad_gating, grad_upward, dec_hidden_route, dec_ffn_gather = together(
        low_part, grad_gating, grad_upward, dec_hidden_route, dec_ffn_gather
    )
    branch = swap(low_part).astype(f32)
    dec_gu_route = route_start(grad_gating, grad_upward)
    dec_hidden_routed = route_end(*dec_hidden_route)
    dec_ffn_all = gather_end(*dec_ffn_gather)
    dec_output = own(difference) + teacher.T
    branch, dec_hidden_routed, dec_ffn_all, dec_output = together(
        branch, dec_hidden_routed, dec_ffn_all, dec_output
    )
    part, g_dec_norm_ff = norm_backward(dec_cross, dec_norm_ff, partial + branch)
    grad_cross = grad_seed + part

    cross_branch = grad_cross.astype(bf16)
    qd, stats, cross_wide = prepare(cross_branch, cross_out_proj, cross_q, cross_o, cross_logs)
    qd_window, stat_window, cross_value_other = window_gather(
        3, [(qd, BOTH), (stats, BOTH)], [cross_value.T]
    )
    qd_window, dec_gu_route, dec_branch, cross_query_here = together(
        qd_window, dec_gu_route, dec_branch, cross_query
    )
    cross_query_other = swap(cross_query_here.T)
    dec_branch_gather = gather_start(dec_branch)
    dec_gu_routed = route_end(*dec_gu_route)
    dec_gu_leaving = first_leaving(dec_gu_routed, dec_ffn_all)
    qd_window, dec_gu_leaving = together(qd_window, dec_gu_leaving)
    dec_gu_arrived = flip(dec_gu_leaving, REACH_PAIRS)
    cross_dkv = attend_keys(
        cross_kv, qd_window, stat_window, bounds_both, doc_lo, doc_hi, None
    )
    dkv_other = swap(cross_dkv)
    cross_dkv, qd = together(cross_dkv, qd)
    (cross_dq,) = attend_queries(
        qd, cross_window, bounds_both, doc_lo, doc_hi, cross_wide, None
    )
    grad_memory = dot(cross_key, cross_dkv[:width]) + dot(cross_value, cross_dkv[width:])
    dkv_other, cross_dq, grad_memory, cross_query_other = together(
        dkv_other, cross_dq, grad_memory, cross_query_other
    )
    dq_other = swap(cross_dq)
    grad_memory = (
        grad_memory
        + dot(cross_key_other, dkv_other[:width], 0, 0)
        + dot(cross_value_other, dkv_other[width:], 0, 0)
    )

    memory_branch = grad_memory.astype(bf16)
    enc_branch_gather = gather_start(memory_branch)
    partial, low_part, grad_gating, grad_upward = feed_backward(
        memory_branch, enc_weights, enc_d1, enc_d2
    )
    low_part, grad_gating, grad_upward, dec_branch_gather, dq_other = together(
        low_part, grad_gating, grad_upward, dec_branch_gather, dq_other
    )
    branch = swap(low_part).astype(f32)
    enc_gu_route = route_start(grad_gating, grad_upward)

    dec_branch_all = gather_end(*dec_branch_gather)
    dec_down_leaving = first_leaving(dec_hidden_routed, dec_branch_all)
    grad_normed = dot(cross_query, cross_dq) + dot(cross_query_other, dq_other, 0, 0)
    part, g_dec_norm_cross = norm_backward(dec_mid, dec_norm_cross, grad_normed)
    grad_mid = grad_cross + part
    self_branch = grad_mid.astype(bf16)
    self_qd, self_stats, self_wide = prepare(self_branch, dec_out_proj, dec_q, dec_o, dec_logs)
    self_qd, dec_down_leaving, dec_gu_arrived = together(self_qd, dec_down_leaving, dec_gu_arrived)
    dec_down_arrived = flip(dec_down_leaving, REACH_PAIRS)
    dec_gu_kept, dec_gu_sent = after_low(after_first(dec_gu_routed, dec_ffn_all, dec_gu_arrived))
    cross_part = small_parts(
        ctx_size,
        width,
        side,
        [
            (
                [cross_dq, cross_dkv, cross_att],
                [dq_other, dkv_other, cross_att_other],
                [((0, 0), cross_normed), ((1, 2), memory), ((3, 3), cross_branch)],
            )
        ],
    )
    branch, dec_gu_sent, dec_gu_kept, cross_part = together(
        branch, dec_gu_sent, dec_gu_kept, cross_part
    )
    cross_half = halve(cross_part, 1)
    part, g_enc_norm_ff = norm_backward(enc_mid, enc_norm_ff, partial + branch)
    grad_enc_mid = grad_memory + part

    enc_branch = grad_enc_mid.astype(bf16)
    enc_qd, enc_stats, enc_wide = prepare(enc_branch, enc_out_proj, enc_q, enc_o, enc_logs)
    enc_qd_window, enc_stat_window, self_qd_window, self_stat_window, dec_gu_sent = window_gather(
        4,
        [(enc_qd, BOTH), (enc_stats, BOTH), (self_qd, ABOVE), (self_stats, ABOVE)],
        [dec_gu_sent],
    )
    dec_gu_last = last_start(dec_gu_kept, dec_gu_sent)
    enc_qd_window, enc_gu_route, dec_gu_mine, cross_half, dec_down_arrived = together(
        enc_qd_window, enc_gu_route, dec_gu_last[0], cross_half, dec_down_arrived
    )
    enc_gu_routed = route_end(*enc_gu_route)
    enc_gu_leaving = first_leaving(enc_gu_routed, enc_ffn_all)
    enc_qd_window, enc_gu_leaving = together(enc_qd_window, enc_gu_leaving)
    enc_gu_arrived = flip(enc_gu_leaving, REACH_PAIRS)
    enc_dkv = attend_keys(
        enc_kv, enc_qd_window, enc_stat_window, bounds_both, doc_lo, doc_hi, enc_back
    )
    enc_dkv, enc_qd = together(enc_dkv, enc_qd)
    enc_dq, enc_grad_line = attend_queries(
        enc_qd, enc_window, bounds_both, doc_lo, doc_hi, enc_wide, enc_line
    )
    enc_dq, self_qd_window = together(enc_dq, self_qd_window)
    self_dkv = attend_keys(
        dec_kv, self_qd_window, self_stat_window, bounds_above, positions, doc_hi, dec_back
    )
    self_dkv, self_qd = together(self_dkv, self_qd)
    self_dq, dec_grad_line = attend_queries(
        self_qd, dec_window, bounds_below, doc_lo, positions, self_wide, dec_line
    )
    (
        enc_dq, enc_dkv, self_dq, self_dkv, dec_gu_end, enc_gu_arrived, enc_branch_gather,
        cross_half,
    ) = together(
        enc_dq, enc_dkv, self_dq, self_dkv, dec_gu_last[1], enc_gu_arrived, enc_branch_gather,
        cross_half,
    )
    grads = jnp.concatenate([enc_dq, enc_dkv, self_dq, self_dkv], axis=0)
    grads_other = swap(grads)
    cross_half = halve(halved(*cross_half), 2)
    kinds_wide = (KINDS - 1) * width
    enc_partial = (
        dot(enc_query, enc_dq) + dot(enc_key, enc_dkv[:width]) + dot(enc_value, enc_dkv[width:])
    )
    self_partial = (
        dot(dec_query, self_dq) + dot(dec_key, self_dkv[:width]) + dot(dec_value, self_dkv[width:])
    )
    low_others = jnp.concatenate([others(enc_partial), others(self_partial)], axis=0).astype(bf16)
    grads, low_others, enc_gu_arrived, enc_branch_gather = together(
        grads, low_others, enc_gu_arrived, enc_branch_gather
    )
    low_arrived = swap(low_others)

    enc_gu_sum = after_first(enc_gu_routed, enc_ffn_all, enc_gu_arrived)
    dec_down_sum = after_first(dec_hidden_routed, dec_branch_all, dec_down_arrived)
    enc_branch_all = gather_end(*enc_branch_gather)
    enc_down_leaving = first_leaving(enc_hidden_routed, enc_branch_all)
    low_half = enc_hidden_routed.reshape((1, low // 2, 2) + enc_hidden_routed.shape[2:])
    enc_down_staying = weight_part(pick(low_half, low_bit, 2), enc_branch_all)
    dec_gu = last_end(dec_gu_mine, dec_gu_end)
    (
        grads, grads_other, enc_down_leaving, enc_down_staying, enc_gu_sum, dec_down_sum,
        dec_gu, cross_kept, cross_arrived,
    ) = together(
        grads, grads_other, enc_down_leaving, enc_down_staying, enc_gu_sum, dec_down_sum,
        dec_gu, cross_half[0], cross_half[1],
    )
    cross_half = halve(halved(cross_kept, cross_arrived), 4)
    attention_parts = [
        (
            [grads[:kinds_wide], enc_att],
            [grads_other[:kinds_wide], enc_att_other],
            [((0, 2), enc_normed), ((3, 3), enc_branch)],
        ),
        (
            [grads[kinds_wide:], dec_att],
            [grads_other[kinds_wide:], dec_att_other],
            [((0, 2), dec_normed), ((3, 3), self_branch)],
        ),
    ]
    if ctx_size == 16:
        both_part = small_parts(ctx_size, width, side, attention_parts)
        both_part, low_arrived, cross_kept, cross_arrived = together(
            both_part, low_arrived, cross_half[0], cross_half[1]
        )
        cross_half = halve(halved(cross_kept, cross_arrived), 8)
    partial_others = low_arrived.astype(f32)
    part, g_enc_norm_attn = norm_backward(
        enc_in, enc_norm_attn, own(enc_partial) + partial_others[:D]
    )
    grad_enc_input = own(grad_enc_mid) + part
    part, g_dec_norm_self = norm_backward(
        dec_in, dec_norm_self, own(self_partial) + partial_others[D:]
    )
    grad_dec_input = own(grad_mid) + part
    loss_part = jnp.sum(own(difference * difference * mask_pair))

    enc_bias_part = bucket_grads(enc_hot, enc_grad_line)
    dec_bias_part = bucket_grads(dec_hot, dec_grad_line)
    gains = jnp.concatenate(
        [
            g_enc_norm_attn,
            0.5 * g_enc_norm_ff,
            g_dec_norm_self,
            0.5 * g_dec_norm_cross,
            0.5 * g_dec_norm_ff,
        ]
    )
    small = jnp.concatenate(
        [
            gains,
            enc_bias_part.reshape(-1),
            dec_bias_part.reshape(-1),
            loss_part[None],
        ]
    )
    if ctx_size == 16:
        count = small.shape[0]
        padded = -(-count // 1024) * 1024
        small = jnp.pad(small, (0, padded - count)).reshape(8, padded // 8)
        columns = enc_down_leaving.shape[-2]
        both_part, small, cross_kept = together(both_part, small, cross_half[0])
        both_shard, enc_gu, enc_down_rows, dec_down_rows, small = last_exchanges(
            6,
            both_part,
            enc_gu_sum[:, 0].transpose(1, 0, 2, 3).reshape(2, 2 * columns, D),
            enc_down_leaving.reshape(2, columns, D),
            enc_down_staying.reshape(2, columns, D),
            dec_down_sum.reshape(2, columns, D),
            small,
        )
        small, cross_arrived = together(small, cross_half[1])
        small = small.reshape(-1)[:count]
        cross_shard = halved(cross_kept, cross_arrived)[0]
        enc_shard, self_shard = jnp.split(both_shard, 2, axis=0)
    else:
        small = total_over_devices(small, 7, ctx_size)
        enc_shard, self_shard = [
            halving(small_parts(ctx_size, width, side, [part]), 1) for part in attention_parts
        ]
        cross_shard = halving(halved(*cross_half), 8)

        def finished(part):
            kept, sent = after_low(part)
            return last_end(*last_start(kept, swap(sent)))

        enc_gu, dec_down_rows = finished(enc_gu_sum), finished(dec_down_sum)
        enc_down_first = flip(enc_down_leaving, REACH_PAIRS).astype(f32)
        enc_down_rows = finished((enc_down_staying + enc_down_first).astype(bf16))
    teacher_loss = small[-1] / (D * valid_total)
    gain = [small[i * D : (i + 1) * D] for i in range(5)]
    bias_size = enc_bias_part.size
    bias = [
        small[5 * D + i * bias_size : 5 * D + (i + 1) * bias_size].reshape(enc_bias_part.shape)
        for i in range(2)
    ]

    def pieces(shard, kinds):
        each = shard.shape[0] // len(kinds)
        made = []
        for i, transposed in enumerate(kinds):
            piece = shard[i * each : (i + 1) * each].astype(f32)
            made.append(piece.T if transposed else piece)
        return made

    dec_gate_up = pieces(dec_gu, (True, True))
    dec_down_g = pieces(dec_down_rows, (False,))
    enc_gate_up = pieces(enc_gu, (True, True))
    enc_down_g = pieces(enc_down_rows, (False,))
    kinds = (True, True, True, False)
    enc_attn = pieces(enc_shard, kinds)
    dec_attn = pieces(self_shard, kinds) + pieces(cross_shard, kinds)
    return (
        teacher_loss,
        dec_output.T,
        grad_enc_input.T,
        grad_dec_input.T,
        gain[0],
        *enc_attn,
        gain[1],
        *enc_gate_up,
        *enc_down_g,
        bias[0],
        gain[2],
        *dec_attn[:4],
        gain[3],
        *dec_attn[4:],
        gain[4],
        *dec_gate_up,
        *dec_down_g,
        bias[1],
    )


def solution(mesh):
    rows = P(("ctx", "fsdp"), None)
    split_columns = P(None, "fsdp")
    split_rows = P("fsdp", None)
    attention_in = (split_columns,) * 3 + (split_rows,)
    feed_in = (split_columns,) * 2 + (split_rows,)
    in_specs = (
        (rows,) * 3
        + (P(("ctx", "fsdp")), P(), P(), P())
        + (P(),)
        + attention_in
        + (P(),)
        + feed_in
        + (P(), P())
        + attention_in
        + (P(),)
        + attention_in
        + (P(),)
        + feed_in
        + (P(),)
    )
    columns = P(None, ("ctx", "fsdp"))
    attention_out = (columns,) * 3 + (rows,)
    feed_out = (columns,) * 2 + (rows,)
    out_specs = (
        (P(),)
        + (rows,) * 3
        + (P(),)
        + attention_out
        + (P(),)
        + feed_out
        + (P(), P())
        + attention_out
        + (P(),)
        + attention_out
        + (P(),)
        + feed_out
        + (P(),)
    )
    return jax.shard_map(body, mesh=mesh, in_specs=in_specs, out_specs=out_specs, check_vma=False)
```

```python
import functools

import jax
import jax.numpy as jnp
from jax import lax
from jax.experimental import pallas as pl
from jax.experimental.pallas import tpu as pltpu
from jax.sharding import PartitionSpec as P

D = 1472
HEAD = 64
REACH_PAIRS = 4
WIN = 3 * REACH_PAIRS
epsilon = 1e-06
far_below = -1e30
bf16 = jnp.bfloat16
f32 = jnp.float32
MESH = pl.DeviceIdType.MESH
FEED_LIMIT = 16 * 1024 * 1024
SMALL_COST = pl.CostEstimate(flops=0, bytes_accessed=500_000, transcendentals=0)


def dot(left, right, left_dim=1, right_dim=0):
    return lax.dot_general(
        left, right, (((left_dim,), (right_dim,)), ((), ())), preferred_element_type=f32
    )


def swap(value):
    return lax.ppermute(value, "fsdp", [(0, 1), (1, 0)])


def flipped(index, bit):
    return index + bit - 2 * bit * lax.rem(index // bit, 2)


def window_kernel(flags, swaps, summed, *refs):
    arrays = len(flags)
    total = arrays + swaps
    given = total + (1 if summed else 0)
    ins, outs = refs[:given], refs[given : 2 * given]
    local_sem, send_sem, recv_sem, swap_send, swap_recv = refs[2 * given : 2 * given + 5]
    rounds = lax.axis_size("ctx").bit_length() if summed else 0
    if summed:
        sum_mine, sum_theirs, sum_send, sum_recv = refs[2 * given + 5 :]
    R = REACH_PAIRS
    ctx = lax.axis_index("ctx")
    fsdp = lax.axis_index("fsdp")
    groups = lax.axis_size("ctx") // R
    group = ctx // R
    place = lax.rem(ctx, R)
    near, far = flipped(place, 1), flipped(place, 2)
    dev_near, dev_far = group * R + near, group * R + far
    dev_up, dev_down = ctx + R, ctx - R
    has_up, has_down = group < groups - 1, group > 0
    barrier = pltpu.get_barrier_semaphore()

    def greet(device):
        pl.semaphore_signal(barrier, inc=1, device_id=(device, fsdp), device_id_type=MESH)

    greet(dev_near)
    greet(dev_far)
    if swaps:
        pl.semaphore_signal(barrier, inc=1, device_id=(ctx, 1 - fsdp), device_id_type=MESH)

    @pl.when(has_up)
    def _():
        greet(dev_up)

    @pl.when(has_down)
    def _():
        greet(dev_down)

    for k in range(2, rounds - 1):
        greet(flipped(ctx, 1 << k))

    greeted = 2 + (1 if swaps else 0) + max(rounds - 3, 0)
    pl.semaphore_wait(barrier, greeted + has_up.astype(jnp.int32) + has_down.astype(jnp.int32))

    def copies(number, source_slot, slot, device, use=lambda f: True, part=None):
        made = []
        for k, (below, above, split) in enumerate(flags):
            if not use(flags[k]):
                continue
            rows = ins[k].shape[0]
            cut = rows if not split else (rows // 2 if not (below and above) else 3 * rows // 8)
            where = {None: (0, rows), 0: (0, cut), 1: (cut, rows)}[part]
            if where[0] == where[1]:
                continue
            span = pl.ds(where[0], where[1] - where[0])
            source = ins[k] if source_slot is None else outs[k].at[source_slot, span]
            made.append(
                pltpu.make_async_remote_copy(
                    src_ref=source,
                    dst_ref=outs[k].at[slot, span],
                    send_sem=send_sem.at[k, number],
                    recv_sem=recv_sem.at[k, number],
                    device_id=(device, fsdp),
                    device_id_type=MESH,
                )
            )
        return made

    def start(made):
        for copy in made:
            copy.start()

    sums = [
        pltpu.make_async_remote_copy(
            src_ref=sum_mine.at[k],
            dst_ref=sum_theirs.at[k],
            send_sem=sum_send.at[k],
            recv_sem=sum_recv.at[k],
            device_id=(ctx, 1 - fsdp) if k == 0 else (flipped(ctx, 1 << (k - 1)), fsdp),
            device_id_type=MESH,
        )
        for k in range(rounds)
    ]

    def sum_step(k):
        if k == 0:
            sum_mine[0] = ins[total][...]
        else:
            sums[k - 1].wait_recv()
            added = sum_mine[k - 1] + sum_theirs[k - 1]
            if k == rounds:
                outs[total][...] = added
            else:
                sum_mine[k] = added
        if k < rounds:
            sums[k].start()

    def arrived(made):
        for copy in made:
            copy.wait_recv()

    def left(made):
        for copy in made:
            copy.wait_send()

    below = lambda flag: flag[0]
    above = lambda flag: flag[1]
    to_up = copies(0, None, place, dev_up, below)
    to_down = copies(1, None, 2 * R + place, dev_down, above)
    to_far = copies(2, None, R + place, dev_far)
    to_near = copies(3, None, R + place, dev_near)
    far_low = copies(4, place, place, dev_far, below, 0)
    far_high = copies(5, 2 * R + place, 2 * R + place, dev_far, above, 0)
    up_far = copies(6, R + far, far, dev_up, below, 1)
    down_far = copies(7, R + far, 2 * R + far, dev_down, above, 1)
    near_low = copies(8, place, place, dev_near, below)
    near_high = copies(9, 2 * R + place, 2 * R + place, dev_near, above)
    near_far = copies(10, R + far, R + far, dev_near)
    near_far_low = copies(11, far, far, dev_near, below)
    near_far_high = copies(12, 2 * R + far, 2 * R + far, dev_near, above)
    own = [
        pltpu.make_async_copy(ins[k], outs[k].at[R + place], local_sem.at[k])
        for k in range(arrays)
    ]

    across = [
        pltpu.make_async_remote_copy(
            src_ref=ins[arrays + k],
            dst_ref=outs[arrays + k],
            send_sem=swap_send.at[k],
            recv_sem=swap_recv.at[k],
            device_id=(ctx, 1 - fsdp),
            device_id_type=MESH,
        )
        for k in range(swaps)
    ]

    @pl.when(has_up)
    def _():
        start(to_up)

    @pl.when(has_down)
    def _():
        start(to_down)

    if summed:
        sum_step(0)
    start(to_far)
    start(to_near)
    start(across)
    start(own)
    if summed:
        sum_step(1)
    arrived(to_far)
    if summed:
        sum_step(2)

    @pl.when(has_up)
    def _():
        start(up_far)

    @pl.when(has_down)
    def _():
        start(down_far)

    start(near_far)

    @pl.when(has_down)
    def _():
        arrived(to_up)
        start(far_low)
        start(near_low)

    @pl.when(has_up)
    def _():
        arrived(to_down)
        start(far_high)
        start(near_high)

    if summed:
        sum_step(3)

    @pl.when(has_down)
    def _():
        arrived(far_low)
        arrived(up_far)
        start(near_far_low)

    @pl.when(has_up)
    def _():
        arrived(far_high)
        arrived(down_far)
        start(near_far_high)

    arrived(to_near)
    arrived(near_far)

    @pl.when(has_down)
    def _():
        arrived(near_low)
        arrived(near_far_low)
        left(far_low)
        left(near_low)
        left(near_far_low)
        left(to_down)
        left(down_far)

    @pl.when(has_up)
    def _():
        arrived(near_high)
        arrived(near_far_high)
        left(far_high)
        left(near_high)
        left(near_far_high)
        left(to_up)
        left(up_far)

    left(to_far)
    left(to_near)
    left(near_far)
    for copy in own + across:
        copy.wait()
    if summed:
        for k in range(4, rounds + 1):
            sum_step(k)
        left(sums)


BOTH, BELOW, ABOVE = (True, True), (True, False), (False, True)


def window_gather(number, pairs, swapped=(), summand=None):
    values = [value for value, _ in pairs]
    flags = tuple(
        sides + (value.dtype == bf16 and value.shape[0] % 128 == 0,) for value, sides in pairs
    )
    count, swaps = len(values), len(swapped)
    vmem = pl.BlockSpec(memory_space=pltpu.VMEM)
    specs = [vmem] * count + [pl.BlockSpec(memory_space=pl.ANY)] * swaps
    extra, sum_scratch = [], []
    if summand is not None:
        specs = specs + [vmem]
        extra = [summand]
        rounds = lax.axis_size("ctx").bit_length()
        sum_scratch = [pltpu.VMEM((rounds,) + summand.shape, f32)] * 2 + [
            pltpu.SemaphoreType.DMA((rounds,))
        ] * 2
    return pl.pallas_call(
        functools.partial(window_kernel, flags, swaps, summand is not None),
        out_shape=[jax.ShapeDtypeStruct((WIN,) + v.shape, v.dtype) for v in values]
        + [jax.ShapeDtypeStruct(v.shape, v.dtype) for v in [*swapped, *extra]],
        in_specs=specs,
        out_specs=specs,
        scratch_shapes=[
            pltpu.SemaphoreType.DMA((count,)),
            pltpu.SemaphoreType.DMA((count, 13)),
            pltpu.SemaphoreType.DMA((count, 13)),
            pltpu.SemaphoreType.DMA((max(swaps, 1),)),
            pltpu.SemaphoreType.DMA((max(swaps, 1),)),
        ]
        + sum_scratch,
        compiler_params=pltpu.CompilerParams(
            collective_id=number, has_side_effects=True, vmem_limit_bytes=4 << 20
        ),
        cost_estimate=SMALL_COST,
        name="window_gather",
    )(*values, *swapped, *extra)


def total_kernel(rounds, sides, x_ref, o_ref, mine, theirs, send_sem, recv_sem):
    ctx = lax.axis_index("ctx")
    fsdp = lax.axis_index("fsdp")
    partners = [(flipped(ctx, 1 << k), fsdp) for k in range(rounds - sides)]
    partners += [(ctx, 1 - fsdp)] * sides
    barrier = pltpu.get_barrier_semaphore()
    for partner in partners:
        pl.semaphore_signal(barrier, inc=1, device_id=partner, device_id_type=MESH)
    pl.semaphore_wait(barrier, rounds)
    mine[0] = x_ref[...]
    for k, partner in enumerate(partners):
        copy = pltpu.make_async_remote_copy(
            src_ref=mine.at[k],
            dst_ref=theirs.at[k],
            send_sem=send_sem.at[k],
            recv_sem=recv_sem.at[k],
            device_id=partner,
            device_id_type=MESH,
        )
        copy.start()
        copy.wait()
        added = mine[k] + theirs[k]
        if k + 1 < rounds:
            mine[k + 1] = added
        else:
            o_ref[...] = added


def total_over_devices(value, number, ctx_size, sides=1):
    rounds = ctx_size.bit_length() - 1 + sides
    padded = -(-value.shape[0] // 1024) * 1024
    wide = jnp.pad(value, (0, padded - value.shape[0])).reshape(8, padded // 8)
    vmem = pl.BlockSpec(memory_space=pltpu.VMEM)
    made = pl.pallas_call(
        functools.partial(total_kernel, rounds, sides),
        out_shape=jax.ShapeDtypeStruct(wide.shape, f32),
        in_specs=[vmem],
        out_specs=vmem,
        scratch_shapes=[
            pltpu.VMEM((rounds,) + wide.shape, f32),
            pltpu.VMEM((rounds,) + wide.shape, f32),
            pltpu.SemaphoreType.DMA((rounds,)),
            pltpu.SemaphoreType.DMA((rounds,)),
        ],
        compiler_params=pltpu.CompilerParams(collective_id=number, has_side_effects=True),
        cost_estimate=SMALL_COST,
        name="total_over_devices",
    )(wide)
    return made.reshape(-1)[: value.shape[0]]


def head_rows(width):
    rows = lax.broadcasted_iota(jnp.int32, (width, 1), 0)
    return [(rows >= h * HEAD) & (rows < (h + 1) * HEAD) for h in range(width // HEAD)]


def head_lanes(width):
    lanes = lax.broadcasted_iota(jnp.int32, (1, width), 1)
    return [(lanes >= h * HEAD) & (lanes < (h + 1) * HEAD) for h in range(width // HEAD)]


def only(value, mask):
    return jnp.where(mask, value, jnp.zeros_like(value))


def by_token(value):
    width, rows = value.shape
    full = -(-width // 128) * 128
    return jnp.concatenate([value, jnp.zeros((full - width, rows), value.dtype)], axis=0).T[:, :width]


def toeplitz(line_ref, head, block, rows):
    start = pl.multiple_of(block * rows, rows)
    segment = line_ref[pl.ds(head, 1), pl.ds(start, 2 * rows)]
    spread = jnp.broadcast_to(segment, (rows, 2 * rows))
    return pltpu.roll(spread, rows + 1, 1, stride=1, stride_axis=0)[:, :rows]


def halves(value, op):
    half = value.shape[1] // 2
    return op(value[:, :half], value[:, half:])


def forward_kernel(biased, bounds, q_ref, kv_ref, lo_ref, hi_ref, *rest):
    if biased:
        line_ref, rest = rest[0], rest[1:]
    o_ref, att_ref, l_ref, s_ref, m_ref, sum_ref, acc_ref, rest_ref = rest
    width, rows = q_ref.shape
    heads = width // HEAD
    lanes, bands = head_lanes(width), head_rows(width)
    first, last, key_base = bounds[0], bounds[1], bounds[2]
    lo, hi = lo_ref[...], hi_ref[...]
    m_ref[...] = jnp.full_like(m_ref, far_below)
    sum_ref[...] = jnp.zeros_like(sum_ref)
    acc_ref[...] = jnp.zeros_like(acc_ref)
    q = by_token(q_ref[...])

    def scores(block, carry):
        keys = kv_ref[block, :width]
        key_pos = key_base + block * rows + lax.broadcasted_iota(jnp.int32, (rows, rows), 1)
        allowed = (key_pos >= lo) & (key_pos <= hi)
        for h in range(heads):
            s = dot(only(q, lanes[h]), keys)
            if biased:
                s = s + toeplitz(line_ref, h, block, rows)
            s = jnp.where(allowed, s, far_below)
            s_ref[block, h] = s
            m_ref[h] = jnp.maximum(m_ref[h], halves(s, jnp.maximum))
        return carry

    lax.fori_loop(first, last + 1, scores, 0)
    tops = [jnp.max(m_ref[h], axis=1, keepdims=True) for h in range(heads)]

    def weigh(block, carry):
        for h in range(heads):
            p = jnp.exp(s_ref[block, h] - tops[h])
            s_ref[block, h] = p
            sum_ref[h] += halves(p, jnp.add)
        return carry

    lax.fori_loop(first, last + 1, weigh, 0)
    totals = [jnp.sum(sum_ref[h], axis=1, keepdims=True) for h in range(heads)]
    shares = [1.0 / total for total in totals]
    rest_ref[...] = jnp.zeros_like(rest_ref)

    def mix(block, carry):
        values = kv_ref[block, width:]
        total, left = None, None
        for h in range(heads):
            p = s_ref[block, h] * shares[h]
            low_p = p.astype(bf16)
            band = only(values, bands[h])
            part = dot(band, low_p, 1, 1)
            rest_part = dot(band, (p - low_p.astype(f32)).astype(bf16), 1, 1)
            total = part if total is None else total + part
            left = rest_part if left is None else left + rest_part
        acc_ref[...] += total
        rest_ref[...] += left
        return carry

    lax.fori_loop(first, last + 1, mix, 0)
    column = lax.broadcasted_iota(jnp.int32, (rows, 128), 1)
    logs = jnp.zeros((rows, 128), f32)
    for h in range(heads):
        logs = jnp.where(column == h, tops[h] + jnp.log(totals[h]), logs)
    o_ref[...] = acc_ref[...] + rest_ref[...]
    att_ref[...] = acc_ref[...].astype(bf16)
    l_ref[...] = logs.T[:8]


def query_kernel(biased, bounds, qd_ref, kv_ref, lo_ref, hi_ref, stat_ref, *rest):
    if biased:
        line_ref, dq_ref, gline_ref, acc_ref = rest
        gline_ref[...] = jnp.zeros_like(gline_ref)
    else:
        dq_ref, acc_ref = rest
    width, rows = qd_ref.shape[0] // 2, qd_ref.shape[1]
    heads = width // HEAD
    lanes, bands = head_lanes(width), head_rows(width)
    first, last, key_base = bounds[0], bounds[1], bounds[2]
    lo, hi = lo_ref[...], hi_ref[...]
    acc_ref[...] = jnp.zeros_like(acc_ref)
    q, da = by_token(qd_ref[:width]), by_token(qd_ref[width:])
    logs = [stat_ref[:, h : h + 1] for h in range(heads)]
    deltas = [stat_ref[:, heads + h : heads + h + 1] for h in range(heads)]

    def step(block, carry):
        keys = kv_ref[block, :width]
        values = kv_ref[block, width:]
        key_pos = key_base + block * rows + lax.broadcasted_iota(jnp.int32, (rows, rows), 1)
        allowed = (key_pos >= lo) & (key_pos <= hi)
        total = None
        for h in range(heads):
            s = dot(only(q, lanes[h]), keys)
            if biased:
                s = s + toeplitz(line_ref, h, block, rows)
            p = jnp.exp(jnp.where(allowed, s - logs[h], far_below))
            dp = dot(only(da, lanes[h]), values)
            ds = (p * (dp - deltas[h])).astype(bf16)
            part = dot(only(keys, bands[h]), ds, 1, 1)
            total = part if total is None else total + part
            if biased:
                folded = jnp.concatenate([ds.astype(f32), jnp.zeros((rows, rows), f32)], axis=1)
                half = rows // 2
                while half >= 1:
                    folded = pltpu.roll(folded[:half], half, 1) + folded[half:]
                    half //= 2
                start = pl.multiple_of(block * rows, rows)
                gline_ref[pl.ds(h, 1), pl.ds(start, 2 * rows)] += folded
        acc_ref[...] += total
        return carry

    lax.fori_loop(first, last + 1, step, 0)
    dq_ref[...] = acc_ref[...].astype(bf16)


def key_kernel(biased, bounds, kv_ref, qd_ref, stat_ref, lo_ref, hi_ref, *rest):
    if biased:
        line_ref, rest = rest[0], rest[1:]
    dkv_ref, dk_acc, dv_acc = rest
    width, rows = kv_ref.shape[0] // 2, kv_ref.shape[1]
    heads = width // HEAD
    lanes, bands = head_lanes(width), head_rows(width)
    first, last, query_base = bounds[0], bounds[1], bounds[2]
    lo, hi = lo_ref[...], hi_ref[...]
    dk_acc[...] = jnp.zeros_like(dk_acc)
    dv_acc[...] = jnp.zeros_like(dv_acc)
    keys, values = by_token(kv_ref[:width]), by_token(kv_ref[width:])

    def step(block, carry):
        q = qd_ref[block, :width]
        da = qd_ref[block, width:]
        query_pos = query_base + block * rows + lax.broadcasted_iota(jnp.int32, (rows, rows), 1)
        allowed = (query_pos >= lo) & (query_pos <= hi)
        total_k = None
        total_v = None
        for h in range(heads):
            s = dot(only(keys, lanes[h]), q)
            if biased:
                s = s + toeplitz(line_ref, h, block, rows)
            p = jnp.exp(jnp.where(allowed, s - stat_ref[block, h : h + 1, :], far_below))
            dp = dot(only(values, lanes[h]), da)
            ds = (p * (dp - stat_ref[block, heads + h : heads + h + 1, :])).astype(bf16)
            part_k = dot(only(q, bands[h]), ds, 1, 1)
            part_v = dot(only(da, bands[h]), p.astype(bf16), 1, 1)
            total_k = part_k if total_k is None else total_k + part_k
            total_v = part_v if total_v is None else total_v + part_v
        dk_acc[...] += total_k
        dv_acc[...] += total_v
        return carry

    lax.fori_loop(first, last + 1, step, 0)
    dkv_ref[:width] = dk_acc[...].astype(bf16)
    dkv_ref[width:] = dv_acc[...].astype(bf16)


def local_call(kernel, out_shape, scratch, name, limit, bounds, *values):
    vmem = pl.BlockSpec(memory_space=pltpu.VMEM)
    smem = pl.BlockSpec(memory_space=pltpu.SMEM)
    return pl.pallas_call(
        kernel,
        out_shape=out_shape,
        in_specs=[smem] + [vmem] * len(values),
        out_specs=jax.tree.map(lambda _: vmem, out_shape),
        scratch_shapes=scratch,
        compiler_params=pltpu.CompilerParams(vmem_limit_bytes=limit << 20),
        cost_estimate=SMALL_COST,
        name=name,
    )(bounds, *values)


def attend(q, kv_window, bounds, lo, hi, line):
    width, rows = q.shape
    heads = width // HEAD
    biased = line is not None
    return local_call(
        functools.partial(forward_kernel, biased),
        [
            jax.ShapeDtypeStruct((width, rows), f32),
            jax.ShapeDtypeStruct((width, rows), bf16),
            jax.ShapeDtypeStruct((8, rows), f32),
        ],
        [
            pltpu.VMEM((WIN, heads, rows, rows), f32),
            pltpu.VMEM((heads, rows, rows // 2), f32),
            pltpu.VMEM((heads, rows, rows // 2), f32),
            pltpu.VMEM((width, rows), f32),
            pltpu.VMEM((width, rows), f32),
        ],
        "attend_forward",
        16,
        bounds,
        q,
        kv_window,
        lo,
        hi,
        *([line] if biased else []),
    )


def attend_queries(qd, kv_window, bounds, lo, hi, stats, line):
    width, rows = qd.shape[0] // 2, qd.shape[1]
    biased = line is not None
    shapes = [jax.ShapeDtypeStruct((width, rows), bf16)]
    if biased:
        shapes.append(jax.ShapeDtypeStruct(line.shape, f32))
    return local_call(
        functools.partial(query_kernel, biased),
        shapes,
        [pltpu.VMEM((width, rows), f32)],
        "attend_queries",
        10,
        bounds,
        qd,
        kv_window,
        lo,
        hi,
        stats,
        *([line] if biased else []),
    )


def attend_keys(kv, qd_window, stat_window, bounds, lo, hi, line):
    width, rows = kv.shape[0] // 2, kv.shape[1]
    biased = line is not None
    return local_call(
        functools.partial(key_kernel, biased),
        jax.ShapeDtypeStruct((2 * width, rows), bf16),
        [pltpu.VMEM((width, rows), f32)] * 2,
        "attend_keys",
        10,
        bounds,
        kv,
        qd_window,
        stat_window,
        lo,
        hi,
        *([line] if biased else []),
    )


def rows_kernel(left_ref, right_ref, out_ref):
    out_ref[...] = dot(left_ref[...], right_ref[...], 1, 1).astype(bf16)


def rows_product(left, right):
    vmem = pl.BlockSpec(memory_space=pltpu.VMEM)
    return pl.pallas_call(
        rows_kernel,
        out_shape=jax.ShapeDtypeStruct((left.shape[0], right.shape[0]), bf16),
        in_specs=[vmem] * 2,
        out_specs=vmem,
        compiler_params=pltpu.CompilerParams(vmem_limit_bytes=14 << 20),
        cost_estimate=SMALL_COST,
        name="weight_rows",
    )(left, right)


def prepare_kernel(grad_ref, w_ref, q_ref, o_ref, log_ref, qd_ref, row_ref, wide_ref):
    width, rows = q_ref.shape
    heads = width // HEAD
    da = dot(w_ref[...], grad_ref[...]).astype(bf16)
    qd_ref[:width] = q_ref[...]
    qd_ref[width:] = da
    product = da.astype(f32) * o_ref[...]
    row = lax.broadcasted_iota(jnp.int32, (128, rows), 0)
    stats = jnp.concatenate([log_ref[...], jnp.zeros((120, rows), f32)], axis=0)
    for h, mask in enumerate(head_rows(width)):
        delta = jnp.sum(only(product, mask), axis=0, keepdims=True)
        stats = jnp.where(row == heads + h, delta, stats)
    row_ref[...] = stats[:8]
    wide_ref[...] = stats.T


def prepare(grad, w_out, q, out, log_rows):
    width, rows = q.shape
    vmem = pl.BlockSpec(memory_space=pltpu.VMEM)
    return pl.pallas_call(
        prepare_kernel,
        out_shape=[
            jax.ShapeDtypeStruct((2 * width, rows), bf16),
            jax.ShapeDtypeStruct((8, rows), f32),
            jax.ShapeDtypeStruct((rows, 128), f32),
        ],
        in_specs=[vmem] * 5,
        out_specs=[vmem] * 3,
        compiler_params=pltpu.CompilerParams(vmem_limit_bytes=10 << 20),
        cost_estimate=SMALL_COST,
        name="attention_prepare",
    )(grad, w_out, q, out, log_rows)


KINDS = 4


def small_kernel(blocks, width, layout, place, *refs):
    out_ref = refs[-1]
    columns = width // blocks
    side = place[0]
    row = lax.broadcasted_iota(jnp.int32, (blocks * KINDS * columns, 1), 0)
    left, block = row // (KINDS * columns), jnp.zeros_like(row)
    for _ in range(blocks.bit_length() - 1):
        block = 2 * block + lax.rem(left, 2)
        left = left // 2
    kind = lax.rem(row // columns, KINDS)
    column = columns * (2 * block + side) + lax.rem(row, columns)
    away = jnp.where(column // width == side, 0, 1)
    wanted = away * (KINDS * width) + kind * width + lax.rem(column, width)
    used = 0
    for number, (counted, kinds) in enumerate(layout):
        values = jnp.concatenate([ref[...] for ref in refs[used : used + counted]], axis=0)
        sources = refs[used + counted : used + counted + len(kinds)]
        used += counted + len(kinds)
        spot = lax.broadcasted_iota(jnp.int32, (1, values.shape[0]), 1)
        onehot = jnp.where(wanted == spot, 1.0, 0.0).astype(bf16)
        chosen = dot(onehot, values).astype(bf16)
        total = None
        for (first, last), source in zip(kinds, sources):
            part = dot(only(chosen, (kind >= first) & (kind <= last)), source[...], 1, 1)
            total = part if total is None else total + part
        total = total.astype(bf16)
        depth = KINDS * columns
        for index in range(blocks):
            out_ref[index, number * depth : (number + 1) * depth] = total[
                index * depth : (index + 1) * depth
            ]


def small_parts(blocks, width, side, parts):
    vmem = pl.BlockSpec(memory_space=pltpu.VMEM)
    smem = pl.BlockSpec(memory_space=pltpu.SMEM)
    layout, values = [], []
    for own, other, sources in parts:
        layout.append((len(own) + len(other), tuple(span for span, _ in sources)))
        values += [*own, *other, *[source for _, source in sources]]
    depth = parts[0][2][0][1].shape[0]
    rows = len(parts) * KINDS * (width // blocks)
    return pl.pallas_call(
        functools.partial(small_kernel, blocks, width, tuple(layout)),
        out_shape=jax.ShapeDtypeStruct((blocks, rows, depth), bf16),
        in_specs=[smem] + [vmem] * len(values),
        out_specs=vmem,
        compiler_params=pltpu.CompilerParams(vmem_limit_bytes=22 << 20),
        cost_estimate=SMALL_COST,
        name="attention_weight_part",
    )(jnp.stack([side]), *values)


CHUNK = 256
GELU_RATE = 0.7978845608028654
GELU_CUBE = 0.044715


def feed_kernel(x_ref, gate_ref, up_ref, down_ref, sum_ref, low_ref, hidden_ref, d1_ref, d2_ref):
    x = x_ref[...].T
    for start in range(0, gate_ref.shape[1], CHUNK):
        span = slice(start, start + CHUNK)
        gating = dot(x, gate_ref[:, span]).T
        upward = dot(x, up_ref[:, span]).T
        square = gating * gating
        t = jnp.tanh(GELU_RATE * gating * (1.0 + GELU_CUBE * square))
        half = 0.5 * (1.0 + t)
        unit = gating * half
        slope = half + 0.5 * gating * (1.0 - t * t) * (
            GELU_RATE * (1.0 + 3.0 * GELU_CUBE * square)
        )
        hidden_ref[span, :] = (unit * upward).astype(bf16)
        d1_ref[span, :] = slope * upward
        d2_ref[span, :] = unit
    total = dot(down_ref[...], hidden_ref[...])
    sum_ref[...] = total
    low_ref[...] = total.astype(bf16)


def feed_back_kernel(e_ref, gate_ref, up_ref, down_ref, d1_ref, d2_ref, sum_ref, low_ref, gg_ref, gu_ref):
    e = e_ref[...].T
    for start in range(0, gate_ref.shape[1], CHUNK):
        span = slice(start, start + CHUNK)
        grad_hidden = dot(e, down_ref[:, span]).astype(bf16).astype(f32).T
        gg_ref[span, :] = (grad_hidden * d1_ref[span, :]).astype(bf16)
        gu_ref[span, :] = (grad_hidden * d2_ref[span, :]).astype(bf16)
    total = dot(gate_ref[...], gg_ref[...]) + dot(up_ref[...], gu_ref[...])
    sum_ref[...] = total
    low_ref[...] = total.astype(bf16)


def feed_call(kernel, name, source, weights, chunked, outs):
    depth, rows = source.shape
    columns = weights[0].shape[1]
    vmem = pl.BlockSpec(memory_space=pltpu.VMEM)
    return pl.pallas_call(
        kernel,
        out_shape=[
            jax.ShapeDtypeStruct((depth, rows), f32),
            jax.ShapeDtypeStruct((depth, rows), bf16),
        ]
        + [jax.ShapeDtypeStruct((columns, rows), kind) for kind in outs],
        in_specs=[vmem] * (4 + len(chunked)),
        out_specs=[vmem] * (2 + len(outs)),
        compiler_params=pltpu.CompilerParams(vmem_limit_bytes=FEED_LIMIT),
        cost_estimate=SMALL_COST,
        name=name,
    )(source, *weights, *chunked)


def feed_forward(source, weights):
    return feed_call(feed_kernel, "feed_forward", source, weights, (), (bf16, f32, f32))


def feed_backward(grad, weights, d1, d2):
    return feed_call(feed_back_kernel, "feed_backward", grad, weights, (d1, d2), (bf16, bf16))


def last_kernel(
    part_ref, gu_ref, leave_ref, stay_ref, dec_ref, small_ref,
    both_out, gu_out, down_out, dec_out, small_out,
    near_r, near_s, far_r, far_s, z_r, z_s, top_r,
    gu_x, gu_send, gu_top, down_z, down_sum, down_x, down_send, down_top,
    dec_x, dec_send, dec_top, mine, theirs, send_sem, recv_sem,
):
    ctx = lax.axis_index("ctx")
    side = lax.axis_index("fsdp")
    bits = [lax.rem(ctx // step, 2) for step in (1, 2, 4, 8)]
    across = (ctx, 1 - side)
    partners = [(flipped(ctx, step), side) for step in (1, 2, 4, 8)]
    same = side == bits[3]
    barrier = pltpu.get_barrier_semaphore()
    for device in [across] + partners:
        pl.semaphore_signal(barrier, inc=1, device_id=device, device_id_type=MESH)
    pl.semaphore_wait(barrier, 5)

    def copy(number, source, target, device):
        made = pltpu.make_async_remote_copy(
            src_ref=source,
            dst_ref=target,
            send_sem=send_sem.at[number],
            recv_sem=recv_sem.at[number],
            device_id=device,
            device_id_type=MESH,
        )
        made.start()
        return made

    def added(kept, arrived):
        return kept.astype(f32) + arrived.astype(f32)

    def small_copy(k, device):
        return copy(9 if k == 4 else 12 + k, mine.at[k], theirs.at[k], device)

    def small_sum(k, made):
        made.wait_recv()
        total = mine[k] + theirs[k]
        if k < 4:
            mine[k + 1] = total
        else:
            small_out[...] = total

    near = copy(0, part_ref.at[pl.ds((1 - bits[0]) * 8, 8)], near_r, partners[0])
    mine[0] = small_ref[...]
    small_top = small_copy(0, partners[3])
    dec_across = copy(1, dec_ref.at[1 - side], dec_x, across)
    gu_across = copy(2, gu_ref.at[1 - side], gu_x, across)
    small_sum(0, small_top)
    small_z = small_copy(1, partners[2])
    down_first = copy(3, leave_ref, down_z, partners[2])

    near.wait_recv()
    near_s[...] = added(part_ref[pl.ds(bits[0] * 8, 8)], near_r[...]).astype(bf16)
    small_sum(1, small_z)
    small_far = small_copy(2, partners[1])
    far = copy(4, near_s.at[pl.ds((1 - bits[1]) * 4, 4)], far_r, partners[1])
    small_sum(2, small_far)
    small_near = small_copy(3, partners[0])

    dec_across.wait_recv()
    dec_send[...] = jnp.where(same, dec_x[...], dec_ref[side])
    dec_last = copy(5, dec_send, dec_top, partners[3])
    gu_across.wait_recv()
    gu_send[...] = jnp.where(same, gu_x[...], gu_ref[side])
    gu_last = copy(6, gu_send, gu_top, partners[3])
    small_sum(3, small_near)
    small_across = small_copy(4, across)
    down_first.wait_recv()
    down_sum[...] = added(stay_ref[...], down_z[...]).astype(bf16)
    down_across = copy(7, down_sum.at[1 - side], down_x, across)
    down_across.wait_recv()
    down_send[...] = jnp.where(same, down_x[...], down_sum[side])
    down_last = copy(8, down_send, down_top, partners[3])
    small_sum(4, small_across)

    far.wait_recv()
    far_s[...] = added(near_s[pl.ds(bits[1] * 4, 4)], far_r[...]).astype(bf16)
    z = copy(10, far_s.at[pl.ds((1 - bits[2]) * 2, 2)], z_r, partners[2])
    dec_last.wait_recv()
    dec_out[...] = added(jnp.where(same, dec_ref[side], dec_x[...]), dec_top[...])
    z.wait_recv()
    z_s[...] = added(far_s[pl.ds(bits[2] * 2, 2)], z_r[...]).astype(bf16)
    top = copy(11, z_s.at[1 - bits[3]], top_r, partners[3])
    gu_last.wait_recv()
    gu_out[...] = added(jnp.where(same, gu_ref[side], gu_x[...]), gu_top[...])
    down_last.wait_recv()
    down_out[...] = added(jnp.where(same, down_sum[side], down_x[...]), down_top[...])
    top.wait_recv()
    both_out[...] = added(z_s[bits[3]], top_r[...])
    for made in (
        near, dec_across, gu_across, down_first, far, dec_last, gu_last,
        down_across, down_last, z, top, small_top, small_z, small_far, small_near, small_across,
    ):
        made.wait_send()


def last_exchanges(number, part, gu, leave, stay, dec, small):
    blocks, rows, depth = part.shape
    vmem = pl.BlockSpec(memory_space=pltpu.VMEM)
    wide, narrow = gu.shape[1], dec.shape[1]
    return pl.pallas_call(
        last_kernel,
        out_shape=[
            jax.ShapeDtypeStruct((rows, depth), f32),
            jax.ShapeDtypeStruct((wide, depth), f32),
            jax.ShapeDtypeStruct((narrow, depth), f32),
            jax.ShapeDtypeStruct((narrow, depth), f32),
            jax.ShapeDtypeStruct(small.shape, f32),
        ],
        in_specs=[vmem] * 6,
        out_specs=[vmem] * 5,
        scratch_shapes=[
            pltpu.VMEM((size, rows, depth), bf16)
            for size in (blocks // 2, blocks // 2, blocks // 4, blocks // 4, blocks // 8, blocks // 8)
        ]
        + [pltpu.VMEM((rows, depth), bf16)]
        + [pltpu.VMEM((wide, depth), bf16)] * 3
        + [pltpu.VMEM((2, narrow, depth), bf16)] * 2
        + [pltpu.VMEM((narrow, depth), bf16)] * 6
        + [pltpu.VMEM((5,) + small.shape, f32)] * 2
        + [pltpu.SemaphoreType.DMA((16,)), pltpu.SemaphoreType.DMA((16,))],
        compiler_params=pltpu.CompilerParams(
            collective_id=number, has_side_effects=True, vmem_limit_bytes=20 << 20
        ),
        cost_estimate=SMALL_COST,
        name="last_exchanges",
    )(part, gu, leave, stay, dec, small)


def inverse_root(inputs):
    return lax.rsqrt(jnp.mean(inputs * inputs, axis=0, keepdims=True) + epsilon)


def root_norm(inputs, gain):
    return inputs * inverse_root(inputs) * gain[:, None]


def norm_backward(inputs, gain, grad):
    inverse = inverse_root(inputs)
    scaled = grad * gain[:, None]
    along = jnp.mean(inputs * scaled, axis=0, keepdims=True)
    grad_inputs = inverse * scaled - inputs * (inverse * inverse * inverse) * along
    return grad_inputs, jnp.sum(grad * inputs * inverse, axis=1)


def body(
    enc_input,
    dec_input,
    teacher,
    valid_mask,
    doc_lengths,
    enc_buckets,
    dec_buckets,
    enc_norm_attn,
    enc_query,
    enc_key,
    enc_value,
    enc_out_proj,
    enc_norm_ff,
    enc_gate,
    enc_up,
    enc_down,
    enc_rel_bias,
    dec_norm_self,
    dec_query,
    dec_key,
    dec_value,
    dec_out_proj,
    dec_norm_cross,
    cross_query,
    cross_key,
    cross_value,
    cross_out_proj,
    dec_norm_ff,
    dec_gate,
    dec_up,
    dec_down,
    dec_rel_bias,
):
    ctx = lax.axis_index("ctx")
    side = lax.axis_index("fsdp")
    ctx_size = lax.axis_size("ctx")
    own_rows = enc_input.shape[0]
    rows = 2 * own_rows
    width = enc_query.shape[1]
    heads = width // HEAD
    place = lax.rem(ctx, REACH_PAIRS)
    core_bit, far_bit = lax.rem(place, 2), place // 2

    def ordered(mine, other, axis=1):
        first = side == 0
        return jnp.concatenate(
            [jnp.where(first, mine, other), jnp.where(first, other, mine)], axis=axis
        )

    def pick(value, index, axis):
        return lax.dynamic_index_in_dim(value, index, axis, keepdims=False)

    def flip(value, bit):
        return lax.ppermute(value, "ctx", [(i, i ^ bit) for i in range(ctx_size)])

    def own(value):
        return lax.dynamic_slice_in_dim(value, side * own_rows, own_rows, 1)

    def others(value):
        return lax.dynamic_slice_in_dim(value, (1 - side) * own_rows, own_rows, 1)

    def together(*values):
        return lax.optimization_barrier(values)

    count = doc_lengths.shape[0]
    order = jnp.arange(count, dtype=jnp.int32)
    starts = jnp.sum(
        jnp.where(order[None, :] < order[:, None], doc_lengths[None, :], 0), axis=1
    )
    ends = starts + doc_lengths
    positions = ctx * rows + jnp.arange(rows, dtype=jnp.int32)[:, None]
    doc_lo = jnp.max(jnp.where(starts[None, :] <= positions, starts[None, :], 0), axis=1, keepdims=True)
    doc_hi = (
        jnp.min(
            jnp.where(ends[None, :] > positions, ends[None, :], ctx_size * rows),
            axis=1,
            keepdims=True,
        )
        - 1
    )
    base_block = ctx - place - REACH_PAIRS
    first_block = doc_lo[0, 0] // rows - base_block
    last_block = doc_hi[rows - 1, 0] // rows - base_block
    own_block = REACH_PAIRS + place
    base_pos = base_block * rows
    bounds_both = jnp.stack([first_block, last_block, base_pos])
    bounds_below = jnp.stack([first_block, own_block, base_pos])
    bounds_above = jnp.stack([own_block, last_block, base_pos])

    reach = enc_buckets.shape[0] // 2
    line_len = (WIN + 1) * rows
    pad_lo, pad_hi = reach, reach + rows
    line_start = (reach + 1 - rows) + pad_lo - rows * (REACH_PAIRS + place)
    reverse_start = (reach - rows) + pad_lo - rows * (REACH_PAIRS + place)

    def lines(rel_bias, buckets):
        hot = (
            buckets[:, None] == jnp.arange(rel_bias.shape[0], dtype=jnp.int32)[None, :]
        ).astype(f32)
        mine = lax.dynamic_slice_in_dim(rel_bias, side * heads, heads, 1)
        line = lax.dot_general(
            mine, hot, (((0,), (1,)), ((), ())), precision=lax.Precision.HIGHEST
        )
        hot_back = (
            buckets[::-1][:, None] == jnp.arange(rel_bias.shape[0], dtype=jnp.int32)[None, :]
        ).astype(f32)
        line_back = lax.dot_general(
            mine, hot_back, (((0,), (1,)), ((), ())), precision=lax.Precision.HIGHEST
        )
        padded = jnp.pad(line, ((0, 8 - heads), (pad_lo, pad_hi)))
        backward = jnp.pad(line_back, ((0, 8 - heads), (pad_lo, pad_hi)))
        return (
            hot,
            lax.dynamic_slice_in_dim(padded, line_start, line_len, 1),
            lax.dynamic_slice_in_dim(backward, reverse_start, line_len, 1),
        )

    enc_hot, enc_line, enc_back = lines(enc_rel_bias, enc_buckets)
    dec_hot, dec_line, dec_back = lines(dec_rel_bias, dec_buckets)

    def bucket_grads(hot, grad_line):
        padded = jnp.zeros((heads, 2 * reach + pad_lo + pad_hi), f32)
        padded = lax.dynamic_update_slice_in_dim(padded, grad_line[:heads], line_start, 1)
        cropped = padded[:, pad_lo : pad_lo + 2 * reach]
        grads = lax.dot_general(
            hot, cropped, (((0,), (1,)), ((), ())), precision=lax.Precision.HIGHEST
        )
        whole = jnp.zeros((hot.shape[1], 2 * heads), f32)
        return lax.dynamic_update_slice_in_dim(whole, grads, side * heads, 1)

    def gather_start(value):
        return value, flip(value, 2)

    def gather_end(value, far):
        both = jnp.concatenate([value, far], axis=1)
        return jnp.concatenate([both, flip(both, 1)], axis=1)

    low = ctx_size // 8

    def route_start(*values):
        columns = values[0].shape[0] // ctx_size
        split = jnp.stack(values).reshape(len(values), low, 2, 2, 2, columns, -1)
        return pick(split, far_bit, 2), flip(pick(split, 1 - far_bit, 2), 2)

    def route_end(mine, other):
        half = jnp.concatenate([mine, other], axis=5)
        return jnp.concatenate(
            [pick(half, core_bit, 2), flip(pick(half, 1 - core_bit, 2), 1)], axis=4
        )

    def weight_part(selected, source):
        return dot(selected, source, selected.ndim - 1, 1)

    low_bits = (ctx_size // 8).bit_length() - 1
    low_bit = lax.rem(ctx // REACH_PAIRS, 2)

    def first_leaving(routed, source):
        split = routed.reshape((routed.shape[0], low // 2, 2) + routed.shape[2:])
        return weight_part(pick(split, 1 - low_bit, 2), source).astype(bf16)

    def after_first(routed, source, arrived):
        split = routed.reshape((routed.shape[0], low // 2, 2) + routed.shape[2:])
        return (weight_part(pick(split, low_bit, 2), source) + arrived.astype(f32)).astype(bf16)

    def after_low(part):
        for k in range(1, low_bits):
            step = REACH_PAIRS << k
            bit = lax.rem(ctx // step, 2)
            split = part.reshape((part.shape[0], part.shape[1] // 2, 2) + part.shape[2:])
            arrived = flip(pick(split, 1 - bit, 2), step)
            part = (pick(split, bit, 2).astype(f32) + arrived.astype(f32)).astype(bf16)
        return pick(part[:, 0], side, 1), pick(part[:, 0], 1 - side, 1)

    same_side = side == ctx // (ctx_size // 2)

    def last_start(staying, arrived):
        mine = jnp.where(same_side, staying, arrived)
        return mine, flip(jnp.where(same_side, arrived, staying), ctx_size // 2)

    def last_end(mine, arrived):
        total = mine.astype(f32) + arrived.astype(f32)
        return total.reshape(-1, total.shape[-1])

    def halve(part, step):
        bit = lax.rem(ctx // step, 2)
        half = part.shape[0] // 2
        arrived = flip(lax.dynamic_slice_in_dim(part, (1 - bit) * half, half, 0), step)
        return lax.dynamic_slice_in_dim(part, bit * half, half, 0), arrived

    def halved(staying, arrived):
        total = staying.astype(f32) + arrived.astype(f32)
        return total if total.shape[0] == 1 else total.astype(bf16)

    def halving(part, step):
        while step < ctx_size:
            part = halved(*halve(part, step))
            step *= 2
        return part[0]

    enc_in, dec_in = enc_input.T, dec_input.T
    enc_arrived = swap(enc_in)
    dec_arrived = swap(dec_in)
    enc_pair = ordered(enc_in, enc_arrived)
    dec_pair = ordered(dec_in, dec_arrived)
    enc_normed = root_norm(enc_pair, enc_norm_attn).astype(bf16)
    dec_normed = root_norm(dec_pair, dec_norm_self).astype(bf16)

    def project(normed, *weights):
        made = [dot(w, normed, 0, 0).astype(bf16) for w in weights]
        return made[0] if len(made) == 1 else jnp.concatenate(made, axis=0)

    enc_kv = project(enc_normed, enc_key, enc_value)
    dec_kv = project(dec_normed, dec_key, dec_value)
    teacher_low = jnp.pad(
        jnp.concatenate([teacher.T, valid_mask.astype(f32)[None]], axis=0), ((0, 7), (0, 0))
    )
    enc_kv, enc_line, enc_back, dec_line, dec_back, teacher_low = together(
        enc_kv, enc_line, enc_back, dec_line, dec_back, teacher_low
    )
    enc_window, dec_window, enc_out_other = window_gather(
        1, [(enc_kv, BOTH), (dec_kv, BELOW)], [enc_out_proj]
    )
    enc_q = project(enc_normed, enc_query)
    dec_q = project(dec_normed, dec_query)

    enc_o, enc_att, enc_logs = attend(enc_q, enc_window, bounds_both, doc_lo, doc_hi, enc_line)
    enc_att_other = swap(enc_att)
    enc_att, dec_q = together(enc_att, dec_q)
    dec_o, dec_att, dec_logs = attend(dec_q, dec_window, bounds_below, doc_lo, positions, dec_line)
    dec_att_other = swap(dec_att)
    enc_att_other, dec_att, dec_out_here = together(enc_att_other, dec_att, dec_out_proj)
    dec_out_other = swap(dec_out_here)
    enc_mid = (
        enc_pair + dot(enc_out_proj, enc_att, 0, 0) + dot(enc_out_other, enc_att_other, 0, 0)
    )
    enc_ffn_in = root_norm(enc_mid, enc_norm_ff).astype(bf16)
    enc_weights = (enc_gate, enc_up, enc_down.T)
    partial, low_part, enc_hidden, enc_d1, enc_d2 = feed_forward(enc_ffn_in, enc_weights)
    low_part, dec_att, enc_hidden = together(low_part, dec_att, enc_hidden)
    branch = swap(low_part).astype(f32)

    enc_hidden_route = route_start(enc_hidden)
    dec_mid = (
        dec_pair + dot(dec_out_proj, dec_att, 0, 0) + dot(dec_out_other, dec_att_other, 0, 0)
    )
    cross_normed = root_norm(dec_mid, dec_norm_cross).astype(bf16)
    cross_q = project(cross_normed, cross_query)
    branch, cross_q = together(branch, cross_q)
    memory = (enc_mid + partial + branch).astype(bf16)
    cross_kv = project(memory, cross_key, cross_value)
    valid_count = jnp.broadcast_to(jnp.sum(valid_mask.astype(f32)), (8, 128))
    query_halves = jnp.split(cross_query.T, 2, axis=0)
    cross_window, cross_out_other, query_other_low, valid_tile = window_gather(
        2, [(cross_kv, BOTH)], [cross_out_proj, query_halves[0]], valid_count
    )
    cross_window, enc_ffn_in = together(cross_window, enc_ffn_in)
    enc_ffn_gather = gather_start(enc_ffn_in)
    valid_total = valid_tile[0, 0]
    scale = (rows * ctx_size) / valid_total
    cross_o, cross_att, cross_logs = attend(
        cross_q, cross_window, bounds_both, doc_lo, doc_hi, None
    )
    cross_att_other = swap(cross_att)
    cross_att, enc_hidden_route, teacher_low = together(cross_att, enc_hidden_route, teacher_low)
    teacher_other = swap(teacher_low)
    enc_hidden_routed = route_end(*enc_hidden_route)
    cross_att_other, enc_hidden_routed = together(cross_att_other, enc_hidden_routed)
    dec_cross = (
        dec_mid + dot(cross_out_proj, cross_att, 0, 0) + dot(cross_out_other, cross_att_other, 0, 0)
    )
    dec_ffn_in = root_norm(dec_cross, dec_norm_ff).astype(bf16)
    dec_ffn_gather = gather_start(dec_ffn_in)
    dec_weights = (dec_gate, dec_up, dec_down.T)
    partial, low_part, dec_hidden, dec_d1, dec_d2 = feed_forward(dec_ffn_in, dec_weights)
    low_part, dec_hidden, teacher_other, enc_ffn_gather = together(
        low_part, dec_hidden, teacher_other, enc_ffn_gather
    )
    mask_pair = ordered(valid_mask.astype(f32)[None], teacher_other[D : D + 1])
    branch = swap(low_part).astype(f32)
    dec_hidden_route = route_start(dec_hidden)
    teacher_pair = ordered(teacher.T, teacher_other[:D])
    before = dec_cross + partial - teacher_pair
    enc_ffn_all = gather_end(*enc_ffn_gather)
    branch, before, enc_ffn_all = together(branch, before, enc_ffn_all)

    difference = before + branch
    grad_seed = difference * (mask_pair * scale)

    dec_branch = grad_seed.astype(bf16)
    cross_key_here, dec_branch = together(cross_key, dec_branch)
    cross_key_other = swap(cross_key_here.T)
    dec_branch_gather = gather_start(dec_branch)
    partial, low_part, grad_gating, grad_upward = feed_backward(
        dec_branch, dec_weights, dec_d1, dec_d2
    )
    low_part, grad_gating, grad_upward, dec_hidden_route, dec_ffn_gather = together(
        low_part, grad_gating, grad_upward, dec_hidden_route, dec_ffn_gather
    )
    branch = swap(low_part).astype(f32)
    dec_gu_route = route_start(grad_gating, grad_upward)
    dec_hidden_routed = route_end(*dec_hidden_route)
    dec_ffn_all = gather_end(*dec_ffn_gather)
    dec_output = own(difference) + teacher.T
    branch, dec_hidden_routed, dec_ffn_all, dec_output, dec_branch_gather = together(
        branch, dec_hidden_routed, dec_ffn_all, dec_output, dec_branch_gather
    )
    part, g_dec_norm_ff = norm_backward(dec_cross, dec_norm_ff, partial + branch)
    grad_cross = grad_seed + part

    cross_branch = grad_cross.astype(bf16)
    qd, stats, cross_wide = prepare(cross_branch, cross_out_proj, cross_q, cross_o, cross_logs)
    qd_window, stat_window, cross_value_other, query_other_high = window_gather(
        3, [(qd, BOTH), (stats, BOTH)], [cross_value.T, query_halves[1]]
    )
    cross_query_other = jnp.concatenate([query_other_low, query_other_high], axis=0)
    qd_window, dec_gu_route, dec_branch_gather = together(
        qd_window, dec_gu_route, dec_branch_gather
    )
    dec_gu_routed = route_end(*dec_gu_route)
    dec_gu_leaving = first_leaving(dec_gu_routed, dec_ffn_all)
    dec_branch_all = gather_end(*dec_branch_gather)
    dec_down_leaving = first_leaving(dec_hidden_routed, dec_branch_all)
    qd_window, dec_gu_leaving, dec_down_leaving = together(
        qd_window, dec_gu_leaving, dec_down_leaving
    )
    dec_gu_arrived = flip(dec_gu_leaving, REACH_PAIRS)
    dec_down_arrived = flip(dec_down_leaving, REACH_PAIRS)
    cross_dkv = attend_keys(
        cross_kv, qd_window, stat_window, bounds_both, doc_lo, doc_hi, None
    )
    dkv_other = swap(cross_dkv)
    cross_dkv, qd = together(cross_dkv, qd)
    (cross_dq,) = attend_queries(
        qd, cross_window, bounds_both, doc_lo, doc_hi, cross_wide, None
    )
    grad_memory = dot(cross_key, cross_dkv[:width]) + dot(cross_value, cross_dkv[width:])
    dkv_other, cross_dq, grad_memory = together(dkv_other, cross_dq, grad_memory)
    dq_other = swap(cross_dq)
    grad_memory = (
        grad_memory
        + dot(cross_key_other, dkv_other[:width], 0, 0)
        + dot(cross_value_other, dkv_other[width:], 0, 0)
    )

    memory_branch = grad_memory.astype(bf16)
    enc_branch_gather = gather_start(memory_branch)
    partial, low_part, grad_gating, grad_upward = feed_backward(
        memory_branch, enc_weights, enc_d1, enc_d2
    )
    low_part, grad_gating, grad_upward, dq_other = together(
        low_part, grad_gating, grad_upward, dq_other
    )
    branch = swap(low_part).astype(f32)
    enc_gu_route = route_start(grad_gating, grad_upward)

    grad_normed = dot(cross_query, cross_dq) + dot(cross_query_other, dq_other, 0, 0)
    part, g_dec_norm_cross = norm_backward(dec_mid, dec_norm_cross, grad_normed)
    grad_mid = grad_cross + part
    self_branch = grad_mid.astype(bf16)
    self_qd, self_stats, self_wide = prepare(self_branch, dec_out_proj, dec_q, dec_o, dec_logs)
    self_qd, dec_down_arrived, dec_gu_arrived = together(self_qd, dec_down_arrived, dec_gu_arrived)
    dec_gu_kept, dec_gu_sent = after_low(after_first(dec_gu_routed, dec_ffn_all, dec_gu_arrived))
    cross_part = small_parts(
        ctx_size,
        width,
        side,
        [
            (
                [cross_dq, cross_dkv, cross_att],
                [dq_other, dkv_other, cross_att_other],
                [((0, 0), cross_normed), ((1, 2), memory), ((3, 3), cross_branch)],
            )
        ],
    )
    branch, dec_gu_sent, dec_gu_kept, cross_part = together(
        branch, dec_gu_sent, dec_gu_kept, cross_part
    )
    cross_half = halve(cross_part, 1)
    part, g_enc_norm_ff = norm_backward(enc_mid, enc_norm_ff, partial + branch)
    grad_enc_mid = grad_memory + part

    enc_branch = grad_enc_mid.astype(bf16)
    enc_qd, enc_stats, enc_wide = prepare(enc_branch, enc_out_proj, enc_q, enc_o, enc_logs)
    enc_gu_routed = route_end(*enc_gu_route)
    split = enc_gu_routed.reshape((enc_gu_routed.shape[0], low // 2, 2) + enc_gu_routed.shape[2:])
    enc_gu_left = pick(split, 1 - low_bit, 2)
    enc_branch_all = gather_end(*enc_branch_gather)
    enc_down_leaving = first_leaving(enc_hidden_routed, enc_branch_all)
    low_half = enc_hidden_routed.reshape((1, low // 2, 2) + enc_hidden_routed.shape[2:])
    enc_down_staying = weight_part(pick(low_half, low_bit, 2), enc_branch_all)
    enc_qd, enc_gu_left, enc_gu_routed, enc_down_leaving, enc_down_staying = together(
        enc_qd, enc_gu_left, enc_gu_routed, enc_down_leaving, enc_down_staying
    )
    enc_qd_window, enc_stat_window, self_qd_window, self_stat_window, dec_gu_sent = window_gather(
        4,
        [(enc_qd, BOTH), (enc_stats, BOTH), (self_qd, ABOVE), (self_stats, ABOVE)],
        [dec_gu_sent],
    )
    dec_gu_last = last_start(dec_gu_kept, dec_gu_sent)
    enc_qd_window, dec_gu_mine, cross_half, enc_gu_left = together(
        enc_qd_window, dec_gu_last[0], cross_half, enc_gu_left
    )
    flat = enc_gu_left.reshape(-1, enc_gu_left.shape[-1])
    enc_gu_leaving = rows_product(flat, enc_ffn_all).reshape(enc_gu_left.shape[:-1] + (D,))
    enc_qd_window, enc_gu_leaving = together(enc_qd_window, enc_gu_leaving)
    enc_gu_arrived = flip(enc_gu_leaving, REACH_PAIRS)
    enc_dkv = attend_keys(
        enc_kv, enc_qd_window, enc_stat_window, bounds_both, doc_lo, doc_hi, enc_back
    )
    enc_dkv, enc_qd = together(enc_dkv, enc_qd)
    enc_dq, enc_grad_line = attend_queries(
        enc_qd, enc_window, bounds_both, doc_lo, doc_hi, enc_wide, enc_line
    )
    enc_dq, self_qd_window = together(enc_dq, self_qd_window)
    self_dkv = attend_keys(
        dec_kv, self_qd_window, self_stat_window, bounds_above, positions, doc_hi, dec_back
    )
    self_dkv, self_qd = together(self_dkv, self_qd)
    self_dq, dec_grad_line = attend_queries(
        self_qd, dec_window, bounds_below, doc_lo, positions, self_wide, dec_line
    )
    enc_dq, enc_dkv, self_dq, self_dkv, dec_gu_end, enc_gu_arrived, cross_half = together(
        enc_dq, enc_dkv, self_dq, self_dkv, dec_gu_last[1], enc_gu_arrived, cross_half
    )
    grads = jnp.concatenate([enc_dq, enc_dkv, self_dq, self_dkv], axis=0)
    grads_other = swap(grads)
    cross_half = halve(halved(*cross_half), 2)
    kinds_wide = (KINDS - 1) * width
    enc_partial = (
        dot(enc_query, enc_dq) + dot(enc_key, enc_dkv[:width]) + dot(enc_value, enc_dkv[width:])
    )
    self_partial = (
        dot(dec_query, self_dq) + dot(dec_key, self_dkv[:width]) + dot(dec_value, self_dkv[width:])
    )
    low_others = jnp.concatenate([others(enc_partial), others(self_partial)], axis=0).astype(bf16)
    grads, low_others, enc_gu_arrived = together(grads, low_others, enc_gu_arrived)
    low_arrived = swap(low_others)

    enc_gu_sum = after_first(enc_gu_routed, enc_ffn_all, enc_gu_arrived)
    dec_down_sum = after_first(dec_hidden_routed, dec_branch_all, dec_down_arrived)
    dec_gu = last_end(dec_gu_mine, dec_gu_end)
    (
        grads, grads_other, enc_down_leaving, enc_down_staying, enc_gu_sum, dec_down_sum,
        dec_gu, cross_kept, cross_arrived,
    ) = together(
        grads, grads_other, enc_down_leaving, enc_down_staying, enc_gu_sum, dec_down_sum,
        dec_gu, cross_half[0], cross_half[1],
    )
    cross_half = halve(halved(cross_kept, cross_arrived), 4)
    attention_parts = [
        (
            [grads[:kinds_wide], enc_att],
            [grads_other[:kinds_wide], enc_att_other],
            [((0, 2), enc_normed), ((3, 3), enc_branch)],
        ),
        (
            [grads[kinds_wide:], dec_att],
            [grads_other[kinds_wide:], dec_att_other],
            [((0, 2), dec_normed), ((3, 3), self_branch)],
        ),
    ]
    if ctx_size == 16:
        both_part = small_parts(ctx_size, width, side, attention_parts)
        both_part, low_arrived, cross_kept, cross_arrived = together(
            both_part, low_arrived, cross_half[0], cross_half[1]
        )
        cross_half = halve(halved(cross_kept, cross_arrived), 8)
    partial_others = low_arrived.astype(f32)
    part, g_enc_norm_attn = norm_backward(
        enc_in, enc_norm_attn, own(enc_partial) + partial_others[:D]
    )
    grad_enc_input = own(grad_enc_mid) + part
    part, g_dec_norm_self = norm_backward(
        dec_in, dec_norm_self, own(self_partial) + partial_others[D:]
    )
    grad_dec_input = own(grad_mid) + part
    loss_part = jnp.sum(own(difference * difference * mask_pair))

    enc_bias_part = bucket_grads(enc_hot, enc_grad_line)
    dec_bias_part = bucket_grads(dec_hot, dec_grad_line)
    gains = jnp.concatenate(
        [
            g_enc_norm_attn,
            0.5 * g_enc_norm_ff,
            g_dec_norm_self,
            0.5 * g_dec_norm_cross,
            0.5 * g_dec_norm_ff,
        ]
    )
    small = jnp.concatenate(
        [
            gains,
            enc_bias_part.reshape(-1),
            dec_bias_part.reshape(-1),
            loss_part[None],
        ]
    )
    if ctx_size == 16:
        count = small.shape[0]
        padded = -(-count // 1024) * 1024
        small = jnp.pad(small, (0, padded - count)).reshape(8, padded // 8)
        columns = enc_down_leaving.shape[-2]
        both_part, small, cross_kept = together(both_part, small, cross_half[0])
        both_shard, enc_gu, enc_down_rows, dec_down_rows, small = last_exchanges(
            6,
            both_part,
            enc_gu_sum[:, 0].transpose(1, 0, 2, 3).reshape(2, 2 * columns, D),
            enc_down_leaving.reshape(2, columns, D),
            enc_down_staying.reshape(2, columns, D),
            dec_down_sum.reshape(2, columns, D),
            small,
        )
        small, cross_arrived = together(small, cross_half[1])
        small = small.reshape(-1)[:count]
        cross_shard = halved(cross_kept, cross_arrived)[0]
        enc_shard, self_shard = jnp.split(both_shard, 2, axis=0)
    else:
        small = total_over_devices(small, 7, ctx_size)
        enc_shard, self_shard = [
            halving(small_parts(ctx_size, width, side, [part]), 1) for part in attention_parts
        ]
        cross_shard = halving(halved(*cross_half), 8)

        def finished(part):
            kept, sent = after_low(part)
            return last_end(*last_start(kept, swap(sent)))

        enc_gu, dec_down_rows = finished(enc_gu_sum), finished(dec_down_sum)
        enc_down_first = flip(enc_down_leaving, REACH_PAIRS).astype(f32)
        enc_down_rows = finished((enc_down_staying + enc_down_first).astype(bf16))
    teacher_loss = small[-1] / (D * valid_total)
    gain = [small[i * D : (i + 1) * D] for i in range(5)]
    bias_size = enc_bias_part.size
    bias = [
        small[5 * D + i * bias_size : 5 * D + (i + 1) * bias_size].reshape(enc_bias_part.shape)
        for i in range(2)
    ]

    def pieces(shard, kinds):
        each = shard.shape[0] // len(kinds)
        made = []
        for i, transposed in enumerate(kinds):
            piece = shard[i * each : (i + 1) * each].astype(f32)
            made.append(piece.T if transposed else piece)
        return made

    dec_gate_up = pieces(dec_gu, (True, True))
    dec_down_g = pieces(dec_down_rows, (False,))
    enc_gate_up = pieces(enc_gu, (True, True))
    enc_down_g = pieces(enc_down_rows, (False,))
    kinds = (True, True, True, False)
    enc_attn = pieces(enc_shard, kinds)
    dec_attn = pieces(self_shard, kinds) + pieces(cross_shard, kinds)
    return (
        teacher_loss,
        dec_output.T,
        grad_enc_input.T,
        grad_dec_input.T,
        gain[0],
        *enc_attn,
        gain[1],
        *enc_gate_up,
        *enc_down_g,
        bias[0],
        gain[2],
        *dec_attn[:4],
        gain[3],
        *dec_attn[4:],
        gain[4],
        *dec_gate_up,
        *dec_down_g,
        bias[1],
    )


def solution(mesh):
    rows = P(("ctx", "fsdp"), None)
    split_columns = P(None, "fsdp")
    split_rows = P("fsdp", None)
    attention_in = (split_columns,) * 3 + (split_rows,)
    feed_in = (split_columns,) * 2 + (split_rows,)
    in_specs = (
        (rows,) * 3
        + (P(("ctx", "fsdp")), P(), P(), P())
        + (P(),)
        + attention_in
        + (P(),)
        + feed_in
        + (P(), P())
        + attention_in
        + (P(),)
        + attention_in
        + (P(),)
        + feed_in
        + (P(),)
    )
    columns = P(None, ("ctx", "fsdp"))
    attention_out = (columns,) * 3 + (rows,)
    feed_out = (columns,) * 2 + (rows,)
    out_specs = (
        (P(),)
        + (rows,) * 3
        + (P(),)
        + attention_out
        + (P(),)
        + feed_out
        + (P(), P())
        + attention_out
        + (P(),)
        + attention_out
        + (P(),)
        + feed_out
        + (P(),)
    )
    return jax.shard_map(body, mesh=mesh, in_specs=in_specs, out_specs=out_specs, check_vma=False)
```

```python
import functools

import jax
import jax.numpy as jnp
from jax import lax
from jax.experimental import pallas as pl
from jax.experimental.pallas import tpu as pltpu
from jax.sharding import PartitionSpec as P

D = 1472
HEAD = 64
REACH_PAIRS = 4
WIN = 3 * REACH_PAIRS
epsilon = 1e-06
far_below = -1e30
bf16 = jnp.bfloat16
f32 = jnp.float32
MESH = pl.DeviceIdType.MESH
FEED_LIMIT = 16 * 1024 * 1024
SMALL_COST = pl.CostEstimate(flops=0, bytes_accessed=500_000, transcendentals=0)


def dot(left, right, left_dim=1, right_dim=0):
    return lax.dot_general(
        left, right, (((left_dim,), (right_dim,)), ((), ())), preferred_element_type=f32
    )


def swap(value):
    return lax.ppermute(value, "fsdp", [(0, 1), (1, 0)])


def flipped(index, bit):
    return index + bit - 2 * bit * lax.rem(index // bit, 2)


def window_kernel(flags, swaps, summed, *refs):
    arrays = len(flags)
    total = arrays + swaps
    given = total + (1 if summed else 0)
    ins, outs = refs[:given], refs[given : 2 * given]
    local_sem, send_sem, recv_sem, swap_send, swap_recv = refs[2 * given : 2 * given + 5]
    rounds = lax.axis_size("ctx").bit_length() if summed else 0
    if summed:
        sum_mine, sum_theirs, sum_send, sum_recv = refs[2 * given + 5 :]
    R = REACH_PAIRS
    ctx = lax.axis_index("ctx")
    fsdp = lax.axis_index("fsdp")
    groups = lax.axis_size("ctx") // R
    group = ctx // R
    place = lax.rem(ctx, R)
    near, far = flipped(place, 1), flipped(place, 2)
    dev_near, dev_far = group * R + near, group * R + far
    dev_up, dev_down = ctx + R, ctx - R
    has_up, has_down = group < groups - 1, group > 0
    barrier = pltpu.get_barrier_semaphore()

    def greet(device):
        pl.semaphore_signal(barrier, inc=1, device_id=(device, fsdp), device_id_type=MESH)

    greet(dev_near)
    greet(dev_far)
    if swaps:
        pl.semaphore_signal(barrier, inc=1, device_id=(ctx, 1 - fsdp), device_id_type=MESH)

    @pl.when(has_up)
    def _():
        greet(dev_up)

    @pl.when(has_down)
    def _():
        greet(dev_down)

    for k in range(2, rounds - 1):
        greet(flipped(ctx, 1 << k))

    greeted = 2 + (1 if swaps else 0) + max(rounds - 3, 0)
    pl.semaphore_wait(barrier, greeted + has_up.astype(jnp.int32) + has_down.astype(jnp.int32))

    def copies(number, source_slot, slot, device, use=lambda f: True, part=None):
        made = []
        for k, (below, above, split) in enumerate(flags):
            if not use(flags[k]):
                continue
            rows = ins[k].shape[0]
            cut = rows if not split else (rows // 2 if not (below and above) else 3 * rows // 8)
            where = {None: (0, rows), 0: (0, cut), 1: (cut, rows)}[part]
            if where[0] == where[1]:
                continue
            span = pl.ds(where[0], where[1] - where[0])
            source = ins[k] if source_slot is None else outs[k].at[source_slot, span]
            made.append(
                pltpu.make_async_remote_copy(
                    src_ref=source,
                    dst_ref=outs[k].at[slot, span],
                    send_sem=send_sem.at[k, number],
                    recv_sem=recv_sem.at[k, number],
                    device_id=(device, fsdp),
                    device_id_type=MESH,
                )
            )
        return made

    def start(made):
        for copy in made:
            copy.start()

    sums = [
        pltpu.make_async_remote_copy(
            src_ref=sum_mine.at[k],
            dst_ref=sum_theirs.at[k],
            send_sem=sum_send.at[k],
            recv_sem=sum_recv.at[k],
            device_id=(ctx, 1 - fsdp) if k == 0 else (flipped(ctx, 1 << (k - 1)), fsdp),
            device_id_type=MESH,
        )
        for k in range(rounds)
    ]

    def sum_step(k):
        if k == 0:
            sum_mine[0] = ins[total][...]
        else:
            sums[k - 1].wait_recv()
            added = sum_mine[k - 1] + sum_theirs[k - 1]
            if k == rounds:
                outs[total][...] = added
            else:
                sum_mine[k] = added
        if k < rounds:
            sums[k].start()

    def arrived(made):
        for copy in made:
            copy.wait_recv()

    def left(made):
        for copy in made:
            copy.wait_send()

    below = lambda flag: flag[0]
    above = lambda flag: flag[1]
    to_up = copies(0, None, place, dev_up, below)
    to_down = copies(1, None, 2 * R + place, dev_down, above)
    to_far = copies(2, None, R + place, dev_far)
    to_near = copies(3, None, R + place, dev_near)
    far_low = copies(4, place, place, dev_far, below, 0)
    far_high = copies(5, 2 * R + place, 2 * R + place, dev_far, above, 0)
    up_far = copies(6, R + far, far, dev_up, below, 1)
    down_far = copies(7, R + far, 2 * R + far, dev_down, above, 1)
    near_low = copies(8, place, place, dev_near, below)
    near_high = copies(9, 2 * R + place, 2 * R + place, dev_near, above)
    near_far = copies(10, R + far, R + far, dev_near)
    near_far_low = copies(11, far, far, dev_near, below)
    near_far_high = copies(12, 2 * R + far, 2 * R + far, dev_near, above)
    own = [
        pltpu.make_async_copy(ins[k], outs[k].at[R + place], local_sem.at[k])
        for k in range(arrays)
    ]

    across = [
        pltpu.make_async_remote_copy(
            src_ref=ins[arrays + k],
            dst_ref=outs[arrays + k],
            send_sem=swap_send.at[k],
            recv_sem=swap_recv.at[k],
            device_id=(ctx, 1 - fsdp),
            device_id_type=MESH,
        )
        for k in range(swaps)
    ]

    @pl.when(has_up)
    def _():
        start(to_up)

    @pl.when(has_down)
    def _():
        start(to_down)

    if summed:
        sum_step(0)
    start(to_far)
    start(to_near)
    start(across)
    start(own)
    if summed:
        sum_step(1)
    arrived(to_far)
    if summed:
        sum_step(2)

    @pl.when(has_up)
    def _():
        start(up_far)

    @pl.when(has_down)
    def _():
        start(down_far)

    start(near_far)

    @pl.when(has_down)
    def _():
        arrived(to_up)
        start(far_low)
        start(near_low)

    @pl.when(has_up)
    def _():
        arrived(to_down)
        start(far_high)
        start(near_high)

    if summed:
        sum_step(3)

    @pl.when(has_down)
    def _():
        arrived(far_low)
        arrived(up_far)
        start(near_far_low)

    @pl.when(has_up)
    def _():
        arrived(far_high)
        arrived(down_far)
        start(near_far_high)

    arrived(to_near)
    arrived(near_far)

    @pl.when(has_down)
    def _():
        arrived(near_low)
        arrived(near_far_low)
        left(far_low)
        left(near_low)
        left(near_far_low)
        left(to_down)
        left(down_far)

    @pl.when(has_up)
    def _():
        arrived(near_high)
        arrived(near_far_high)
        left(far_high)
        left(near_high)
        left(near_far_high)
        left(to_up)
        left(up_far)

    left(to_far)
    left(to_near)
    left(near_far)
    for copy in own + across:
        copy.wait()
    if summed:
        for k in range(4, rounds + 1):
            sum_step(k)
        left(sums)


BOTH, BELOW, ABOVE = (True, True), (True, False), (False, True)


def window_gather(number, pairs, swapped=(), summand=None):
    values = [value for value, _ in pairs]
    flags = tuple(
        sides + (value.dtype == bf16 and value.shape[0] % 128 == 0,) for value, sides in pairs
    )
    count, swaps = len(values), len(swapped)
    vmem = pl.BlockSpec(memory_space=pltpu.VMEM)
    specs = [vmem] * count + [pl.BlockSpec(memory_space=pl.ANY)] * swaps
    extra, sum_scratch = [], []
    if summand is not None:
        specs = specs + [vmem]
        extra = [summand]
        rounds = lax.axis_size("ctx").bit_length()
        sum_scratch = [pltpu.VMEM((rounds,) + summand.shape, f32)] * 2 + [
            pltpu.SemaphoreType.DMA((rounds,))
        ] * 2
    return pl.pallas_call(
        functools.partial(window_kernel, flags, swaps, summand is not None),
        out_shape=[jax.ShapeDtypeStruct((WIN,) + v.shape, v.dtype) for v in values]
        + [jax.ShapeDtypeStruct(v.shape, v.dtype) for v in [*swapped, *extra]],
        in_specs=specs,
        out_specs=specs,
        scratch_shapes=[
            pltpu.SemaphoreType.DMA((count,)),
            pltpu.SemaphoreType.DMA((count, 13)),
            pltpu.SemaphoreType.DMA((count, 13)),
            pltpu.SemaphoreType.DMA((max(swaps, 1),)),
            pltpu.SemaphoreType.DMA((max(swaps, 1),)),
        ]
        + sum_scratch,
        compiler_params=pltpu.CompilerParams(
            collective_id=number, has_side_effects=True, vmem_limit_bytes=4 << 20
        ),
        cost_estimate=SMALL_COST,
        name="window_gather",
    )(*values, *swapped, *extra)


def total_kernel(rounds, sides, x_ref, o_ref, mine, theirs, send_sem, recv_sem):
    ctx = lax.axis_index("ctx")
    fsdp = lax.axis_index("fsdp")
    partners = [(flipped(ctx, 1 << k), fsdp) for k in range(rounds - sides)]
    partners += [(ctx, 1 - fsdp)] * sides
    barrier = pltpu.get_barrier_semaphore()
    for partner in partners:
        pl.semaphore_signal(barrier, inc=1, device_id=partner, device_id_type=MESH)
    pl.semaphore_wait(barrier, rounds)
    mine[0] = x_ref[...]
    for k, partner in enumerate(partners):
        copy = pltpu.make_async_remote_copy(
            src_ref=mine.at[k],
            dst_ref=theirs.at[k],
            send_sem=send_sem.at[k],
            recv_sem=recv_sem.at[k],
            device_id=partner,
            device_id_type=MESH,
        )
        copy.start()
        copy.wait()
        added = mine[k] + theirs[k]
        if k + 1 < rounds:
            mine[k + 1] = added
        else:
            o_ref[...] = added


def total_over_devices(value, number, ctx_size, sides=1):
    rounds = ctx_size.bit_length() - 1 + sides
    padded = -(-value.shape[0] // 1024) * 1024
    wide = jnp.pad(value, (0, padded - value.shape[0])).reshape(8, padded // 8)
    vmem = pl.BlockSpec(memory_space=pltpu.VMEM)
    made = pl.pallas_call(
        functools.partial(total_kernel, rounds, sides),
        out_shape=jax.ShapeDtypeStruct(wide.shape, f32),
        in_specs=[vmem],
        out_specs=vmem,
        scratch_shapes=[
            pltpu.VMEM((rounds,) + wide.shape, f32),
            pltpu.VMEM((rounds,) + wide.shape, f32),
            pltpu.SemaphoreType.DMA((rounds,)),
            pltpu.SemaphoreType.DMA((rounds,)),
        ],
        compiler_params=pltpu.CompilerParams(collective_id=number, has_side_effects=True),
        cost_estimate=SMALL_COST,
        name="total_over_devices",
    )(wide)
    return made.reshape(-1)[: value.shape[0]]


def head_rows(width):
    rows = lax.broadcasted_iota(jnp.int32, (width, 1), 0)
    return [(rows >= h * HEAD) & (rows < (h + 1) * HEAD) for h in range(width // HEAD)]


def head_lanes(width):
    lanes = lax.broadcasted_iota(jnp.int32, (1, width), 1)
    return [(lanes >= h * HEAD) & (lanes < (h + 1) * HEAD) for h in range(width // HEAD)]


def only(value, mask):
    return jnp.where(mask, value, jnp.zeros_like(value))


def by_token(value):
    width, rows = value.shape
    full = -(-width // 128) * 128
    return jnp.concatenate([value, jnp.zeros((full - width, rows), value.dtype)], axis=0).T[:, :width]


def toeplitz(line_ref, head, block, rows):
    start = pl.multiple_of(block * rows, rows)
    segment = line_ref[pl.ds(head, 1), pl.ds(start, 2 * rows)]
    spread = jnp.broadcast_to(segment, (rows, 2 * rows))
    return pltpu.roll(spread, rows + 1, 1, stride=1, stride_axis=0)[:, :rows]


def halves(value, op):
    half = value.shape[1] // 2
    return op(value[:, :half], value[:, half:])


def forward_kernel(biased, bounds, q_ref, kv_ref, lo_ref, hi_ref, *rest):
    if biased:
        line_ref, rest = rest[0], rest[1:]
    o_ref, att_ref, l_ref, s_ref, m_ref, sum_ref, acc_ref, rest_ref = rest
    width, rows = q_ref.shape
    heads = width // HEAD
    lanes, bands = head_lanes(width), head_rows(width)
    first, last, key_base = bounds[0], bounds[1], bounds[2]
    lo, hi = lo_ref[...], hi_ref[...]
    m_ref[...] = jnp.full_like(m_ref, far_below)
    sum_ref[...] = jnp.zeros_like(sum_ref)
    acc_ref[...] = jnp.zeros_like(acc_ref)
    q = by_token(q_ref[...])

    def scores(block, carry):
        keys = kv_ref[block, :width]
        key_pos = key_base + block * rows + lax.broadcasted_iota(jnp.int32, (rows, rows), 1)
        allowed = (key_pos >= lo) & (key_pos <= hi)
        for h in range(heads):
            s = dot(only(q, lanes[h]), keys)
            if biased:
                s = s + toeplitz(line_ref, h, block, rows)
            s = jnp.where(allowed, s, far_below)
            s_ref[block, h] = s
            m_ref[h] = jnp.maximum(m_ref[h], halves(s, jnp.maximum))
        return carry

    lax.fori_loop(first, last + 1, scores, 0)
    tops = [jnp.max(m_ref[h], axis=1, keepdims=True) for h in range(heads)]

    def weigh(block, carry):
        for h in range(heads):
            p = jnp.exp(s_ref[block, h] - tops[h])
            s_ref[block, h] = p
            sum_ref[h] += halves(p, jnp.add)
        return carry

    lax.fori_loop(first, last + 1, weigh, 0)
    totals = [jnp.sum(sum_ref[h], axis=1, keepdims=True) for h in range(heads)]
    shares = [1.0 / total for total in totals]
    rest_ref[...] = jnp.zeros_like(rest_ref)

    def mix(block, carry):
        values = kv_ref[block, width:]
        total, left = None, None
        for h in range(heads):
            p = s_ref[block, h] * shares[h]
            low_p = p.astype(bf16)
            band = only(values, bands[h])
            part = dot(band, low_p, 1, 1)
            rest_part = dot(band, (p - low_p.astype(f32)).astype(bf16), 1, 1)
            total = part if total is None else total + part
            left = rest_part if left is None else left + rest_part
        acc_ref[...] += total
        rest_ref[...] += left
        return carry

    lax.fori_loop(first, last + 1, mix, 0)
    column = lax.broadcasted_iota(jnp.int32, (rows, 128), 1)
    logs = jnp.zeros((rows, 128), f32)
    for h in range(heads):
        logs = jnp.where(column == h, tops[h] + jnp.log(totals[h]), logs)
    o_ref[...] = acc_ref[...] + rest_ref[...]
    att_ref[...] = acc_ref[...].astype(bf16)
    l_ref[...] = logs.T[:8]


def query_kernel(biased, bounds, qd_ref, kv_ref, lo_ref, hi_ref, stat_ref, *rest):
    if biased:
        line_ref, dq_ref, gline_ref, acc_ref = rest
        gline_ref[...] = jnp.zeros_like(gline_ref)
    else:
        dq_ref, acc_ref = rest
    width, rows = qd_ref.shape[0] // 2, qd_ref.shape[1]
    heads = width // HEAD
    lanes, bands = head_lanes(width), head_rows(width)
    first, last, key_base = bounds[0], bounds[1], bounds[2]
    lo, hi = lo_ref[...], hi_ref[...]
    acc_ref[...] = jnp.zeros_like(acc_ref)
    q, da = by_token(qd_ref[:width]), by_token(qd_ref[width:])
    logs = [stat_ref[:, h : h + 1] for h in range(heads)]
    deltas = [stat_ref[:, heads + h : heads + h + 1] for h in range(heads)]

    def step(block, carry):
        keys = kv_ref[block, :width]
        values = kv_ref[block, width:]
        key_pos = key_base + block * rows + lax.broadcasted_iota(jnp.int32, (rows, rows), 1)
        allowed = (key_pos >= lo) & (key_pos <= hi)
        total = None
        for h in range(heads):
            s = dot(only(q, lanes[h]), keys)
            if biased:
                s = s + toeplitz(line_ref, h, block, rows)
            p = jnp.exp(jnp.where(allowed, s - logs[h], far_below))
            dp = dot(only(da, lanes[h]), values)
            ds = (p * (dp - deltas[h])).astype(bf16)
            part = dot(only(keys, bands[h]), ds, 1, 1)
            total = part if total is None else total + part
            if biased:
                folded = jnp.concatenate([ds.astype(f32), jnp.zeros((rows, rows), f32)], axis=1)
                half = rows // 2
                while half >= 1:
                    folded = pltpu.roll(folded[:half], half, 1) + folded[half:]
                    half //= 2
                start = pl.multiple_of(block * rows, rows)
                gline_ref[pl.ds(h, 1), pl.ds(start, 2 * rows)] += folded
        acc_ref[...] += total
        return carry

    lax.fori_loop(first, last + 1, step, 0)
    dq_ref[...] = acc_ref[...].astype(bf16)


def key_kernel(biased, bounds, kv_ref, qd_ref, stat_ref, lo_ref, hi_ref, *rest):
    if biased:
        line_ref, rest = rest[0], rest[1:]
    dkv_ref, dk_acc, dv_acc = rest
    width, rows = kv_ref.shape[0] // 2, kv_ref.shape[1]
    heads = width // HEAD
    lanes, bands = head_lanes(width), head_rows(width)
    first, last, query_base = bounds[0], bounds[1], bounds[2]
    lo, hi = lo_ref[...], hi_ref[...]
    dk_acc[...] = jnp.zeros_like(dk_acc)
    dv_acc[...] = jnp.zeros_like(dv_acc)
    keys, values = by_token(kv_ref[:width]), by_token(kv_ref[width:])

    def step(block, carry):
        q = qd_ref[block, :width]
        da = qd_ref[block, width:]
        query_pos = query_base + block * rows + lax.broadcasted_iota(jnp.int32, (rows, rows), 1)
        allowed = (query_pos >= lo) & (query_pos <= hi)
        total_k = None
        total_v = None
        for h in range(heads):
            s = dot(only(keys, lanes[h]), q)
            if biased:
                s = s + toeplitz(line_ref, h, block, rows)
            p = jnp.exp(jnp.where(allowed, s - stat_ref[block, h : h + 1, :], far_below))
            dp = dot(only(values, lanes[h]), da)
            ds = (p * (dp - stat_ref[block, heads + h : heads + h + 1, :])).astype(bf16)
            part_k = dot(only(q, bands[h]), ds, 1, 1)
            part_v = dot(only(da, bands[h]), p.astype(bf16), 1, 1)
            total_k = part_k if total_k is None else total_k + part_k
            total_v = part_v if total_v is None else total_v + part_v
        dk_acc[...] += total_k
        dv_acc[...] += total_v
        return carry

    lax.fori_loop(first, last + 1, step, 0)
    dkv_ref[:width] = dk_acc[...].astype(bf16)
    dkv_ref[width:] = dv_acc[...].astype(bf16)


def local_call(kernel, out_shape, scratch, name, limit, bounds, *values):
    vmem = pl.BlockSpec(memory_space=pltpu.VMEM)
    smem = pl.BlockSpec(memory_space=pltpu.SMEM)
    return pl.pallas_call(
        kernel,
        out_shape=out_shape,
        in_specs=[smem] + [vmem] * len(values),
        out_specs=jax.tree.map(lambda _: vmem, out_shape),
        scratch_shapes=scratch,
        compiler_params=pltpu.CompilerParams(vmem_limit_bytes=limit << 20),
        cost_estimate=SMALL_COST,
        name=name,
    )(bounds, *values)


def attend(q, kv_window, bounds, lo, hi, line):
    width, rows = q.shape
    heads = width // HEAD
    biased = line is not None
    return local_call(
        functools.partial(forward_kernel, biased),
        [
            jax.ShapeDtypeStruct((width, rows), f32),
            jax.ShapeDtypeStruct((width, rows), bf16),
            jax.ShapeDtypeStruct((8, rows), f32),
        ],
        [
            pltpu.VMEM((WIN, heads, rows, rows), f32),
            pltpu.VMEM((heads, rows, rows // 2), f32),
            pltpu.VMEM((heads, rows, rows // 2), f32),
            pltpu.VMEM((width, rows), f32),
            pltpu.VMEM((width, rows), f32),
        ],
        "attend_forward",
        16,
        bounds,
        q,
        kv_window,
        lo,
        hi,
        *([line] if biased else []),
    )


def attend_queries(qd, kv_window, bounds, lo, hi, stats, line):
    width, rows = qd.shape[0] // 2, qd.shape[1]
    biased = line is not None
    shapes = [jax.ShapeDtypeStruct((width, rows), bf16)]
    if biased:
        shapes.append(jax.ShapeDtypeStruct(line.shape, f32))
    return local_call(
        functools.partial(query_kernel, biased),
        shapes,
        [pltpu.VMEM((width, rows), f32)],
        "attend_queries",
        10,
        bounds,
        qd,
        kv_window,
        lo,
        hi,
        stats,
        *([line] if biased else []),
    )


def attend_keys(kv, qd_window, stat_window, bounds, lo, hi, line):
    width, rows = kv.shape[0] // 2, kv.shape[1]
    biased = line is not None
    return local_call(
        functools.partial(key_kernel, biased),
        jax.ShapeDtypeStruct((2 * width, rows), bf16),
        [pltpu.VMEM((width, rows), f32)] * 2,
        "attend_keys",
        10,
        bounds,
        kv,
        qd_window,
        stat_window,
        lo,
        hi,
        *([line] if biased else []),
    )


def prepare_kernel(grad_ref, w_ref, q_ref, o_ref, log_ref, qd_ref, row_ref, wide_ref):
    width, rows = q_ref.shape
    heads = width // HEAD
    da = dot(w_ref[...], grad_ref[...]).astype(bf16)
    qd_ref[:width] = q_ref[...]
    qd_ref[width:] = da
    product = da.astype(f32) * o_ref[...]
    row = lax.broadcasted_iota(jnp.int32, (128, rows), 0)
    stats = jnp.concatenate([log_ref[...], jnp.zeros((120, rows), f32)], axis=0)
    for h, mask in enumerate(head_rows(width)):
        delta = jnp.sum(only(product, mask), axis=0, keepdims=True)
        stats = jnp.where(row == heads + h, delta, stats)
    row_ref[...] = stats[:8]
    wide_ref[...] = stats.T


def prepare(grad, w_out, q, out, log_rows):
    width, rows = q.shape
    vmem = pl.BlockSpec(memory_space=pltpu.VMEM)
    return pl.pallas_call(
        prepare_kernel,
        out_shape=[
            jax.ShapeDtypeStruct((2 * width, rows), bf16),
            jax.ShapeDtypeStruct((8, rows), f32),
            jax.ShapeDtypeStruct((rows, 128), f32),
        ],
        in_specs=[vmem] * 5,
        out_specs=[vmem] * 3,
        compiler_params=pltpu.CompilerParams(vmem_limit_bytes=10 << 20),
        cost_estimate=SMALL_COST,
        name="attention_prepare",
    )(grad, w_out, q, out, log_rows)


KINDS = 4


def small_kernel(blocks, width, layout, place, *refs):
    out_ref = refs[-1]
    columns = width // blocks
    side = place[0]
    row = lax.broadcasted_iota(jnp.int32, (blocks * KINDS * columns, 1), 0)
    left, block = row // (KINDS * columns), jnp.zeros_like(row)
    for _ in range(blocks.bit_length() - 1):
        block = 2 * block + lax.rem(left, 2)
        left = left // 2
    kind = lax.rem(row // columns, KINDS)
    column = columns * (2 * block + side) + lax.rem(row, columns)
    away = jnp.where(column // width == side, 0, 1)
    wanted = away * (KINDS * width) + kind * width + lax.rem(column, width)
    used = 0
    for number, (counted, kinds) in enumerate(layout):
        values = jnp.concatenate([ref[...] for ref in refs[used : used + counted]], axis=0)
        sources = refs[used + counted : used + counted + len(kinds)]
        used += counted + len(kinds)
        spot = lax.broadcasted_iota(jnp.int32, (1, values.shape[0]), 1)
        onehot = jnp.where(wanted == spot, 1.0, 0.0).astype(bf16)
        chosen = dot(onehot, values).astype(bf16)
        total = None
        for (first, last), source in zip(kinds, sources):
            part = dot(only(chosen, (kind >= first) & (kind <= last)), source[...], 1, 1)
            total = part if total is None else total + part
        total = total.astype(bf16)
        depth = KINDS * columns
        for index in range(blocks):
            out_ref[index, number * depth : (number + 1) * depth] = total[
                index * depth : (index + 1) * depth
            ]


def small_parts(blocks, width, side, parts):
    vmem = pl.BlockSpec(memory_space=pltpu.VMEM)
    smem = pl.BlockSpec(memory_space=pltpu.SMEM)
    layout, values = [], []
    for own, other, sources in parts:
        layout.append((len(own) + len(other), tuple(span for span, _ in sources)))
        values += [*own, *other, *[source for _, source in sources]]
    depth = parts[0][2][0][1].shape[0]
    rows = len(parts) * KINDS * (width // blocks)
    return pl.pallas_call(
        functools.partial(small_kernel, blocks, width, tuple(layout)),
        out_shape=jax.ShapeDtypeStruct((blocks, rows, depth), bf16),
        in_specs=[smem] + [vmem] * len(values),
        out_specs=vmem,
        compiler_params=pltpu.CompilerParams(vmem_limit_bytes=22 << 20),
        cost_estimate=SMALL_COST,
        name="attention_weight_part",
    )(jnp.stack([side]), *values)


CHUNK = 256
GELU_RATE = 0.7978845608028654
GELU_CUBE = 0.044715


def feed_kernel(x_ref, gate_ref, up_ref, down_ref, sum_ref, low_ref, hidden_ref, d1_ref, d2_ref):
    x = x_ref[...].T
    for start in range(0, gate_ref.shape[1], CHUNK):
        span = slice(start, start + CHUNK)
        gating = dot(x, gate_ref[:, span]).T
        upward = dot(x, up_ref[:, span]).T
        square = gating * gating
        t = jnp.tanh(GELU_RATE * gating * (1.0 + GELU_CUBE * square))
        half = 0.5 * (1.0 + t)
        unit = gating * half
        slope = half + 0.5 * gating * (1.0 - t * t) * (
            GELU_RATE * (1.0 + 3.0 * GELU_CUBE * square)
        )
        hidden_ref[span, :] = (unit * upward).astype(bf16)
        d1_ref[span, :] = slope * upward
        d2_ref[span, :] = unit
    total = dot(down_ref[...], hidden_ref[...])
    sum_ref[...] = total
    low_ref[...] = total.astype(bf16)


def feed_back_kernel(e_ref, gate_ref, up_ref, down_ref, d1_ref, d2_ref, sum_ref, low_ref, gg_ref, gu_ref):
    e = e_ref[...].T
    for start in range(0, gate_ref.shape[1], CHUNK):
        span = slice(start, start + CHUNK)
        grad_hidden = dot(e, down_ref[:, span]).astype(bf16).astype(f32).T
        gg_ref[span, :] = (grad_hidden * d1_ref[span, :]).astype(bf16)
        gu_ref[span, :] = (grad_hidden * d2_ref[span, :]).astype(bf16)
    total = dot(gate_ref[...], gg_ref[...]) + dot(up_ref[...], gu_ref[...])
    sum_ref[...] = total
    low_ref[...] = total.astype(bf16)


def feed_call(kernel, name, source, weights, chunked, outs):
    depth, rows = source.shape
    columns = weights[0].shape[1]
    vmem = pl.BlockSpec(memory_space=pltpu.VMEM)
    return pl.pallas_call(
        kernel,
        out_shape=[
            jax.ShapeDtypeStruct((depth, rows), f32),
            jax.ShapeDtypeStruct((depth, rows), bf16),
        ]
        + [jax.ShapeDtypeStruct((columns, rows), kind) for kind in outs],
        in_specs=[vmem] * (4 + len(chunked)),
        out_specs=[vmem] * (2 + len(outs)),
        compiler_params=pltpu.CompilerParams(vmem_limit_bytes=FEED_LIMIT),
        cost_estimate=SMALL_COST,
        name=name,
    )(source, *weights, *chunked)


def feed_forward(source, weights):
    return feed_call(feed_kernel, "feed_forward", source, weights, (), (bf16, f32, f32))


def feed_backward(grad, weights, d1, d2):
    return feed_call(feed_back_kernel, "feed_backward", grad, weights, (d1, d2), (bf16, bf16))


def last_kernel(
    part_ref, gu_ref, leave_ref, stay_ref, dec_ref, small_ref,
    both_out, gu_out, down_out, dec_out, small_out,
    near_r, near_s, far_r, far_s, z_r, z_s, top_r,
    gu_x, gu_send, gu_top, down_z, down_sum, down_x, down_send, down_top,
    dec_x, dec_send, dec_top, mine, theirs, send_sem, recv_sem,
):
    ctx = lax.axis_index("ctx")
    side = lax.axis_index("fsdp")
    bits = [lax.rem(ctx // step, 2) for step in (1, 2, 4, 8)]
    across = (ctx, 1 - side)
    partners = [(flipped(ctx, step), side) for step in (1, 2, 4, 8)]
    same = side == bits[3]
    barrier = pltpu.get_barrier_semaphore()
    for device in [across] + partners:
        pl.semaphore_signal(barrier, inc=1, device_id=device, device_id_type=MESH)
    pl.semaphore_wait(barrier, 5)

    def copy(number, source, target, device):
        made = pltpu.make_async_remote_copy(
            src_ref=source,
            dst_ref=target,
            send_sem=send_sem.at[number],
            recv_sem=recv_sem.at[number],
            device_id=device,
            device_id_type=MESH,
        )
        made.start()
        return made

    def added(kept, arrived):
        return kept.astype(f32) + arrived.astype(f32)

    def small_copy(k, device):
        return copy(9 if k == 4 else 12 + k, mine.at[k], theirs.at[k], device)

    def small_sum(k, made):
        made.wait_recv()
        total = mine[k] + theirs[k]
        if k < 4:
            mine[k + 1] = total
        else:
            small_out[...] = total

    near = copy(0, part_ref.at[pl.ds((1 - bits[0]) * 8, 8)], near_r, partners[0])
    mine[0] = small_ref[...]
    small_top = small_copy(0, partners[3])
    dec_across = copy(1, dec_ref.at[1 - side], dec_x, across)
    gu_across = copy(2, gu_ref.at[1 - side], gu_x, across)
    small_sum(0, small_top)
    small_z = small_copy(1, partners[2])
    down_first = copy(3, leave_ref, down_z, partners[2])

    near.wait_recv()
    near_s[...] = added(part_ref[pl.ds(bits[0] * 8, 8)], near_r[...]).astype(bf16)
    small_sum(1, small_z)
    small_far = small_copy(2, partners[1])
    far = copy(4, near_s.at[pl.ds((1 - bits[1]) * 4, 4)], far_r, partners[1])
    small_sum(2, small_far)
    small_near = small_copy(3, partners[0])

    dec_across.wait_recv()
    dec_send[...] = jnp.where(same, dec_x[...], dec_ref[side])
    dec_last = copy(5, dec_send, dec_top, partners[3])
    gu_across.wait_recv()
    gu_send[...] = jnp.where(same, gu_x[...], gu_ref[side])
    gu_last = copy(6, gu_send, gu_top, partners[3])
    small_sum(3, small_near)
    small_across = small_copy(4, across)
    down_first.wait_recv()
    down_sum[...] = added(stay_ref[...], down_z[...]).astype(bf16)
    down_across = copy(7, down_sum.at[1 - side], down_x, across)
    down_across.wait_recv()
    down_send[...] = jnp.where(same, down_x[...], down_sum[side])
    down_last = copy(8, down_send, down_top, partners[3])
    small_sum(4, small_across)

    far.wait_recv()
    far_s[...] = added(near_s[pl.ds(bits[1] * 4, 4)], far_r[...]).astype(bf16)
    z = copy(10, far_s.at[pl.ds((1 - bits[2]) * 2, 2)], z_r, partners[2])
    dec_last.wait_recv()
    dec_out[...] = added(jnp.where(same, dec_ref[side], dec_x[...]), dec_top[...])
    z.wait_recv()
    z_s[...] = added(far_s[pl.ds(bits[2] * 2, 2)], z_r[...]).astype(bf16)
    top = copy(11, z_s.at[1 - bits[3]], top_r, partners[3])
    gu_last.wait_recv()
    gu_out[...] = added(jnp.where(same, gu_ref[side], gu_x[...]), gu_top[...])
    down_last.wait_recv()
    down_out[...] = added(jnp.where(same, down_sum[side], down_x[...]), down_top[...])
    top.wait_recv()
    both_out[...] = added(z_s[bits[3]], top_r[...])
    for made in (
        near, dec_across, gu_across, down_first, far, dec_last, gu_last,
        down_across, down_last, z, top, small_top, small_z, small_far, small_near, small_across,
    ):
        made.wait_send()


def last_exchanges(number, part, gu, leave, stay, dec, small):
    blocks, rows, depth = part.shape
    vmem = pl.BlockSpec(memory_space=pltpu.VMEM)
    wide, narrow = gu.shape[1], dec.shape[1]
    return pl.pallas_call(
        last_kernel,
        out_shape=[
            jax.ShapeDtypeStruct((rows, depth), f32),
            jax.ShapeDtypeStruct((wide, depth), f32),
            jax.ShapeDtypeStruct((narrow, depth), f32),
            jax.ShapeDtypeStruct((narrow, depth), f32),
            jax.ShapeDtypeStruct(small.shape, f32),
        ],
        in_specs=[vmem] * 6,
        out_specs=[vmem] * 5,
        scratch_shapes=[
            pltpu.VMEM((size, rows, depth), bf16)
            for size in (blocks // 2, blocks // 2, blocks // 4, blocks // 4, blocks // 8, blocks // 8)
        ]
        + [pltpu.VMEM((rows, depth), bf16)]
        + [pltpu.VMEM((wide, depth), bf16)] * 3
        + [pltpu.VMEM((2, narrow, depth), bf16)] * 2
        + [pltpu.VMEM((narrow, depth), bf16)] * 6
        + [pltpu.VMEM((5,) + small.shape, f32)] * 2
        + [pltpu.SemaphoreType.DMA((16,)), pltpu.SemaphoreType.DMA((16,))],
        compiler_params=pltpu.CompilerParams(
            collective_id=number, has_side_effects=True, vmem_limit_bytes=20 << 20
        ),
        cost_estimate=SMALL_COST,
        name="last_exchanges",
    )(part, gu, leave, stay, dec, small)


def inverse_root(inputs):
    return lax.rsqrt(jnp.mean(inputs * inputs, axis=0, keepdims=True) + epsilon)


def root_norm(inputs, gain):
    return inputs * inverse_root(inputs) * gain[:, None]


def norm_backward(inputs, gain, grad):
    inverse = inverse_root(inputs)
    scaled = grad * gain[:, None]
    along = jnp.mean(inputs * scaled, axis=0, keepdims=True)
    grad_inputs = inverse * scaled - inputs * (inverse * inverse * inverse) * along
    return grad_inputs, jnp.sum(grad * inputs * inverse, axis=1)


def body(
    enc_input,
    dec_input,
    teacher,
    valid_mask,
    doc_lengths,
    enc_buckets,
    dec_buckets,
    enc_norm_attn,
    enc_query,
    enc_key,
    enc_value,
    enc_out_proj,
    enc_norm_ff,
    enc_gate,
    enc_up,
    enc_down,
    enc_rel_bias,
    dec_norm_self,
    dec_query,
    dec_key,
    dec_value,
    dec_out_proj,
    dec_norm_cross,
    cross_query,
    cross_key,
    cross_value,
    cross_out_proj,
    dec_norm_ff,
    dec_gate,
    dec_up,
    dec_down,
    dec_rel_bias,
):
    ctx = lax.axis_index("ctx")
    side = lax.axis_index("fsdp")
    ctx_size = lax.axis_size("ctx")
    own_rows = enc_input.shape[0]
    rows = 2 * own_rows
    width = enc_query.shape[1]
    heads = width // HEAD
    place = lax.rem(ctx, REACH_PAIRS)
    core_bit, far_bit = lax.rem(place, 2), place // 2

    def ordered(mine, other, axis=1):
        first = side == 0
        return jnp.concatenate(
            [jnp.where(first, mine, other), jnp.where(first, other, mine)], axis=axis
        )

    def pick(value, index, axis):
        return lax.dynamic_index_in_dim(value, index, axis, keepdims=False)

    def flip(value, bit):
        return lax.ppermute(value, "ctx", [(i, i ^ bit) for i in range(ctx_size)])

    def own(value):
        return lax.dynamic_slice_in_dim(value, side * own_rows, own_rows, 1)

    def others(value):
        return lax.dynamic_slice_in_dim(value, (1 - side) * own_rows, own_rows, 1)

    def together(*values):
        return lax.optimization_barrier(values)

    count = doc_lengths.shape[0]
    order = jnp.arange(count, dtype=jnp.int32)
    starts = jnp.sum(
        jnp.where(order[None, :] < order[:, None], doc_lengths[None, :], 0), axis=1
    )
    ends = starts + doc_lengths
    positions = ctx * rows + jnp.arange(rows, dtype=jnp.int32)[:, None]
    doc_lo = jnp.max(jnp.where(starts[None, :] <= positions, starts[None, :], 0), axis=1, keepdims=True)
    doc_hi = (
        jnp.min(
            jnp.where(ends[None, :] > positions, ends[None, :], ctx_size * rows),
            axis=1,
            keepdims=True,
        )
        - 1
    )
    base_block = ctx - place - REACH_PAIRS
    first_block = doc_lo[0, 0] // rows - base_block
    last_block = doc_hi[rows - 1, 0] // rows - base_block
    own_block = REACH_PAIRS + place
    base_pos = base_block * rows
    bounds_both = jnp.stack([first_block, last_block, base_pos])
    bounds_below = jnp.stack([first_block, own_block, base_pos])
    bounds_above = jnp.stack([own_block, last_block, base_pos])

    reach = enc_buckets.shape[0] // 2
    line_len = (WIN + 1) * rows
    pad_lo, pad_hi = reach, reach + rows
    line_start = (reach + 1 - rows) + pad_lo - rows * (REACH_PAIRS + place)
    reverse_start = (reach - rows) + pad_lo - rows * (REACH_PAIRS + place)

    def lines(rel_bias, buckets):
        hot = (
            buckets[:, None] == jnp.arange(rel_bias.shape[0], dtype=jnp.int32)[None, :]
        ).astype(f32)
        mine = lax.dynamic_slice_in_dim(rel_bias, side * heads, heads, 1)
        line = lax.dot_general(
            mine, hot, (((0,), (1,)), ((), ())), precision=lax.Precision.HIGHEST
        )
        hot_back = (
            buckets[::-1][:, None] == jnp.arange(rel_bias.shape[0], dtype=jnp.int32)[None, :]
        ).astype(f32)
        line_back = lax.dot_general(
            mine, hot_back, (((0,), (1,)), ((), ())), precision=lax.Precision.HIGHEST
        )
        padded = jnp.pad(line, ((0, 8 - heads), (pad_lo, pad_hi)))
        backward = jnp.pad(line_back, ((0, 8 - heads), (pad_lo, pad_hi)))
        return (
            hot,
            lax.dynamic_slice_in_dim(padded, line_start, line_len, 1),
            lax.dynamic_slice_in_dim(backward, reverse_start, line_len, 1),
        )

    enc_hot, enc_line, enc_back = lines(enc_rel_bias, enc_buckets)
    dec_hot, dec_line, dec_back = lines(dec_rel_bias, dec_buckets)

    def bucket_grads(hot, grad_line):
        padded = jnp.zeros((heads, 2 * reach + pad_lo + pad_hi), f32)
        padded = lax.dynamic_update_slice_in_dim(padded, grad_line[:heads], line_start, 1)
        cropped = padded[:, pad_lo : pad_lo + 2 * reach]
        grads = lax.dot_general(
            hot, cropped, (((0,), (1,)), ((), ())), precision=lax.Precision.HIGHEST
        )
        whole = jnp.zeros((hot.shape[1], 2 * heads), f32)
        return lax.dynamic_update_slice_in_dim(whole, grads, side * heads, 1)

    def gather_start(value):
        return value, flip(value, 2)

    def gather_end(value, far):
        both = jnp.concatenate([value, far], axis=1)
        return jnp.concatenate([both, flip(both, 1)], axis=1)

    low = ctx_size // 8

    def route_start(*values):
        columns = values[0].shape[0] // ctx_size
        split = jnp.stack(values).reshape(len(values), low, 2, 2, 2, columns, -1)
        return pick(split, far_bit, 2), flip(pick(split, 1 - far_bit, 2), 2)

    def route_end(mine, other):
        half = jnp.concatenate([mine, other], axis=5)
        return jnp.concatenate(
            [pick(half, core_bit, 2), flip(pick(half, 1 - core_bit, 2), 1)], axis=4
        )

    def weight_part(selected, source):
        return dot(selected, source, selected.ndim - 1, 1)

    low_bits = (ctx_size // 8).bit_length() - 1
    low_bit = lax.rem(ctx // REACH_PAIRS, 2)

    def first_leaving(routed, source):
        split = routed.reshape((routed.shape[0], low // 2, 2) + routed.shape[2:])
        return weight_part(pick(split, 1 - low_bit, 2), source).astype(bf16)

    def after_first(routed, source, arrived):
        split = routed.reshape((routed.shape[0], low // 2, 2) + routed.shape[2:])
        return (weight_part(pick(split, low_bit, 2), source) + arrived.astype(f32)).astype(bf16)

    def after_low(part):
        for k in range(1, low_bits):
            step = REACH_PAIRS << k
            bit = lax.rem(ctx // step, 2)
            split = part.reshape((part.shape[0], part.shape[1] // 2, 2) + part.shape[2:])
            arrived = flip(pick(split, 1 - bit, 2), step)
            part = (pick(split, bit, 2).astype(f32) + arrived.astype(f32)).astype(bf16)
        return pick(part[:, 0], side, 1), pick(part[:, 0], 1 - side, 1)

    same_side = side == ctx // (ctx_size // 2)

    def last_start(staying, arrived):
        mine = jnp.where(same_side, staying, arrived)
        return mine, flip(jnp.where(same_side, arrived, staying), ctx_size // 2)

    def last_end(mine, arrived):
        total = mine.astype(f32) + arrived.astype(f32)
        return total.reshape(-1, total.shape[-1])

    def halve(part, step):
        bit = lax.rem(ctx // step, 2)
        half = part.shape[0] // 2
        arrived = flip(lax.dynamic_slice_in_dim(part, (1 - bit) * half, half, 0), step)
        return lax.dynamic_slice_in_dim(part, bit * half, half, 0), arrived

    def halved(staying, arrived):
        total = staying.astype(f32) + arrived.astype(f32)
        return total if total.shape[0] == 1 else total.astype(bf16)

    def halving(part, step):
        while step < ctx_size:
            part = halved(*halve(part, step))
            step *= 2
        return part[0]

    enc_in, dec_in = enc_input.T, dec_input.T
    enc_arrived = swap(enc_in)
    dec_arrived = swap(dec_in)
    enc_pair = ordered(enc_in, enc_arrived)
    dec_pair = ordered(dec_in, dec_arrived)
    enc_normed = root_norm(enc_pair, enc_norm_attn).astype(bf16)
    dec_normed = root_norm(dec_pair, dec_norm_self).astype(bf16)

    def project(normed, *weights):
        made = [dot(w, normed, 0, 0).astype(bf16) for w in weights]
        return made[0] if len(made) == 1 else jnp.concatenate(made, axis=0)

    enc_kv = project(enc_normed, enc_key, enc_value)
    dec_kv = project(dec_normed, dec_key, dec_value)
    teacher_low = jnp.pad(
        jnp.concatenate([teacher.T, valid_mask.astype(f32)[None]], axis=0), ((0, 7), (0, 0))
    )
    enc_kv, enc_line, enc_back, dec_line, dec_back, teacher_low = together(
        enc_kv, enc_line, enc_back, dec_line, dec_back, teacher_low
    )
    enc_window, dec_window, enc_out_other = window_gather(
        1, [(enc_kv, BOTH), (dec_kv, BELOW)], [enc_out_proj]
    )
    enc_q = project(enc_normed, enc_query)
    dec_q = project(dec_normed, dec_query)

    enc_o, enc_att, enc_logs = attend(enc_q, enc_window, bounds_both, doc_lo, doc_hi, enc_line)
    enc_att_other = swap(enc_att)
    enc_att, dec_q = together(enc_att, dec_q)
    dec_o, dec_att, dec_logs = attend(dec_q, dec_window, bounds_below, doc_lo, positions, dec_line)
    dec_att_other = swap(dec_att)
    enc_att_other, dec_att, dec_out_here = together(enc_att_other, dec_att, dec_out_proj)
    dec_out_other = swap(dec_out_here)
    enc_mid = (
        enc_pair + dot(enc_out_proj, enc_att, 0, 0) + dot(enc_out_other, enc_att_other, 0, 0)
    )
    enc_ffn_in = root_norm(enc_mid, enc_norm_ff).astype(bf16)
    enc_weights = (enc_gate, enc_up, enc_down.T)
    partial, low_part, enc_hidden, enc_d1, enc_d2 = feed_forward(enc_ffn_in, enc_weights)
    low_part, dec_att, enc_hidden = together(low_part, dec_att, enc_hidden)
    branch = swap(low_part).astype(f32)

    enc_hidden_route = route_start(enc_hidden)
    dec_mid = (
        dec_pair + dot(dec_out_proj, dec_att, 0, 0) + dot(dec_out_other, dec_att_other, 0, 0)
    )
    cross_normed = root_norm(dec_mid, dec_norm_cross).astype(bf16)
    cross_q = project(cross_normed, cross_query)
    branch, cross_q = together(branch, cross_q)
    memory = (enc_mid + partial + branch).astype(bf16)
    cross_kv = project(memory, cross_key, cross_value)
    valid_count = jnp.broadcast_to(jnp.sum(valid_mask.astype(f32)), (8, 128))
    cross_window, cross_out_other, valid_tile = window_gather(
        2, [(cross_kv, BOTH)], [cross_out_proj], valid_count
    )
    cross_window, enc_ffn_in = together(cross_window, enc_ffn_in)
    enc_ffn_gather = gather_start(enc_ffn_in)
    valid_total = valid_tile[0, 0]
    scale = (rows * ctx_size) / valid_total
    cross_o, cross_att, cross_logs = attend(
        cross_q, cross_window, bounds_both, doc_lo, doc_hi, None
    )
    cross_att_other = swap(cross_att)
    cross_att, enc_hidden_route, teacher_low = together(cross_att, enc_hidden_route, teacher_low)
    teacher_other = swap(teacher_low)
    enc_hidden_routed = route_end(*enc_hidden_route)
    cross_att_other, enc_hidden_routed = together(cross_att_other, enc_hidden_routed)
    dec_cross = (
        dec_mid + dot(cross_out_proj, cross_att, 0, 0) + dot(cross_out_other, cross_att_other, 0, 0)
    )
    dec_ffn_in = root_norm(dec_cross, dec_norm_ff).astype(bf16)
    dec_ffn_gather = gather_start(dec_ffn_in)
    dec_weights = (dec_gate, dec_up, dec_down.T)
    partial, low_part, dec_hidden, dec_d1, dec_d2 = feed_forward(dec_ffn_in, dec_weights)
    low_part, dec_hidden, teacher_other, enc_ffn_gather = together(
        low_part, dec_hidden, teacher_other, enc_ffn_gather
    )
    mask_pair = ordered(valid_mask.astype(f32)[None], teacher_other[D : D + 1])
    branch = swap(low_part).astype(f32)
    dec_hidden_route = route_start(dec_hidden)
    teacher_pair = ordered(teacher.T, teacher_other[:D])
    before = dec_cross + partial - teacher_pair
    enc_ffn_all = gather_end(*enc_ffn_gather)
    branch, before, enc_ffn_all = together(branch, before, enc_ffn_all)

    difference = before + branch
    grad_seed = difference * (mask_pair * scale)

    dec_branch = grad_seed.astype(bf16)
    cross_key_here, dec_branch = together(cross_key, dec_branch)
    cross_key_other = swap(cross_key_here.T)
    partial, low_part, grad_gating, grad_upward = feed_backward(
        dec_branch, dec_weights, dec_d1, dec_d2
    )
    low_part, grad_gating, grad_upward, dec_hidden_route, dec_ffn_gather = together(
        low_part, grad_gating, grad_upward, dec_hidden_route, dec_ffn_gather
    )
    branch = swap(low_part).astype(f32)
    dec_gu_route = route_start(grad_gating, grad_upward)
    dec_hidden_routed = route_end(*dec_hidden_route)
    dec_ffn_all = gather_end(*dec_ffn_gather)
    dec_output = own(difference) + teacher.T
    branch, dec_hidden_routed, dec_ffn_all, dec_output = together(
        branch, dec_hidden_routed, dec_ffn_all, dec_output
    )
    part, g_dec_norm_ff = norm_backward(dec_cross, dec_norm_ff, partial + branch)
    grad_cross = grad_seed + part

    cross_branch = grad_cross.astype(bf16)
    qd, stats, cross_wide = prepare(cross_branch, cross_out_proj, cross_q, cross_o, cross_logs)
    qd_window, stat_window, cross_value_other = window_gather(
        3, [(qd, BOTH), (stats, BOTH)], [cross_value.T]
    )
    qd_window, dec_gu_route, dec_branch = together(qd_window, dec_gu_route, dec_branch)
    dec_branch_gather = gather_start(dec_branch)
    dec_gu_routed = route_end(*dec_gu_route)
    dec_gu_leaving = first_leaving(dec_gu_routed, dec_ffn_all)
    qd_window, dec_gu_leaving = together(qd_window, dec_gu_leaving)
    dec_gu_arrived = flip(dec_gu_leaving, REACH_PAIRS)
    cross_dkv = attend_keys(
        cross_kv, qd_window, stat_window, bounds_both, doc_lo, doc_hi, None
    )
    dkv_other = swap(cross_dkv)
    cross_dkv, qd, cross_query_here = together(cross_dkv, qd, cross_query)
    cross_query_other = swap(cross_query_here.T)
    (cross_dq,) = attend_queries(
        qd, cross_window, bounds_both, doc_lo, doc_hi, cross_wide, None
    )
    grad_memory = dot(cross_key, cross_dkv[:width]) + dot(cross_value, cross_dkv[width:])
    dkv_other, cross_dq, grad_memory = together(dkv_other, cross_dq, grad_memory)
    dq_other = swap(cross_dq)
    grad_memory = (
        grad_memory
        + dot(cross_key_other, dkv_other[:width], 0, 0)
        + dot(cross_value_other, dkv_other[width:], 0, 0)
    )

    memory_branch = grad_memory.astype(bf16)
    enc_branch_gather = gather_start(memory_branch)
    partial, low_part, grad_gating, grad_upward = feed_backward(
        memory_branch, enc_weights, enc_d1, enc_d2
    )
    low_part, grad_gating, grad_upward, dec_branch_gather, dq_other, cross_query_other = together(
        low_part, grad_gating, grad_upward, dec_branch_gather, dq_other, cross_query_other
    )
    branch = swap(low_part).astype(f32)
    enc_gu_route = route_start(grad_gating, grad_upward)

    dec_branch_all = gather_end(*dec_branch_gather)
    dec_down_leaving = first_leaving(dec_hidden_routed, dec_branch_all)
    grad_normed = dot(cross_query, cross_dq) + dot(cross_query_other, dq_other, 0, 0)
    part, g_dec_norm_cross = norm_backward(dec_mid, dec_norm_cross, grad_normed)
    grad_mid = grad_cross + part
    self_branch = grad_mid.astype(bf16)
    self_qd, self_stats, self_wide = prepare(self_branch, dec_out_proj, dec_q, dec_o, dec_logs)
    self_qd, dec_down_leaving, dec_gu_arrived = together(self_qd, dec_down_leaving, dec_gu_arrived)
    dec_down_arrived = flip(dec_down_leaving, REACH_PAIRS)
    dec_gu_kept, dec_gu_sent = after_low(after_first(dec_gu_routed, dec_ffn_all, dec_gu_arrived))
    cross_part = small_parts(
        ctx_size,
        width,
        side,
        [
            (
                [cross_dq, cross_dkv, cross_att],
                [dq_other, dkv_other, cross_att_other],
                [((0, 0), cross_normed), ((1, 2), memory), ((3, 3), cross_branch)],
            )
        ],
    )
    branch, dec_gu_sent, dec_gu_kept, cross_part = together(
        branch, dec_gu_sent, dec_gu_kept, cross_part
    )
    cross_half = halve(cross_part, 1)
    part, g_enc_norm_ff = norm_backward(enc_mid, enc_norm_ff, partial + branch)
    grad_enc_mid = grad_memory + part

    enc_branch = grad_enc_mid.astype(bf16)
    enc_qd, enc_stats, enc_wide = prepare(enc_branch, enc_out_proj, enc_q, enc_o, enc_logs)
    enc_qd_window, enc_stat_window, self_qd_window, self_stat_window, dec_gu_sent = window_gather(
        4,
        [(enc_qd, BOTH), (enc_stats, BOTH), (self_qd, ABOVE), (self_stats, ABOVE)],
        [dec_gu_sent],
    )
    dec_gu_last = last_start(dec_gu_kept, dec_gu_sent)
    enc_qd_window, enc_gu_route, dec_gu_mine, cross_half, dec_down_arrived = together(
        enc_qd_window, enc_gu_route, dec_gu_last[0], cross_half, dec_down_arrived
    )
    enc_gu_routed = route_end(*enc_gu_route)
    enc_gu_leaving = first_leaving(enc_gu_routed, enc_ffn_all)
    enc_qd_window, enc_gu_leaving = together(enc_qd_window, enc_gu_leaving)
    enc_gu_arrived = flip(enc_gu_leaving, REACH_PAIRS)
    enc_dkv = attend_keys(
        enc_kv, enc_qd_window, enc_stat_window, bounds_both, doc_lo, doc_hi, enc_back
    )
    enc_dkv, enc_qd = together(enc_dkv, enc_qd)
    enc_dq, enc_grad_line = attend_queries(
        enc_qd, enc_window, bounds_both, doc_lo, doc_hi, enc_wide, enc_line
    )
    enc_dq, self_qd_window = together(enc_dq, self_qd_window)
    self_dkv = attend_keys(
        dec_kv, self_qd_window, self_stat_window, bounds_above, positions, doc_hi, dec_back
    )
    self_dkv, self_qd = together(self_dkv, self_qd)
    self_dq, dec_grad_line = attend_queries(
        self_qd, dec_window, bounds_below, doc_lo, positions, self_wide, dec_line
    )
    (
        enc_dq, enc_dkv, self_dq, self_dkv, dec_gu_end, enc_gu_arrived, enc_branch_gather,
        cross_half,
    ) = together(
        enc_dq, enc_dkv, self_dq, self_dkv, dec_gu_last[1], enc_gu_arrived, enc_branch_gather,
        cross_half,
    )
    grads = jnp.concatenate([enc_dq, enc_dkv, self_dq, self_dkv], axis=0)
    grads_other = swap(grads)
    cross_half = halve(halved(*cross_half), 2)
    kinds_wide = (KINDS - 1) * width
    enc_partial = (
        dot(enc_query, enc_dq) + dot(enc_key, enc_dkv[:width]) + dot(enc_value, enc_dkv[width:])
    )
    self_partial = (
        dot(dec_query, self_dq) + dot(dec_key, self_dkv[:width]) + dot(dec_value, self_dkv[width:])
    )
    low_others = jnp.concatenate([others(enc_partial), others(self_partial)], axis=0).astype(bf16)
    grads, low_others, enc_gu_arrived, enc_branch_gather = together(
        grads, low_others, enc_gu_arrived, enc_branch_gather
    )
    low_arrived = swap(low_others)

    enc_gu_sum = after_first(enc_gu_routed, enc_ffn_all, enc_gu_arrived)
    dec_down_sum = after_first(dec_hidden_routed, dec_branch_all, dec_down_arrived)
    enc_branch_all = gather_end(*enc_branch_gather)
    enc_down_leaving = first_leaving(enc_hidden_routed, enc_branch_all)
    low_half = enc_hidden_routed.reshape((1, low // 2, 2) + enc_hidden_routed.shape[2:])
    enc_down_staying = weight_part(pick(low_half, low_bit, 2), enc_branch_all)
    dec_gu = last_end(dec_gu_mine, dec_gu_end)
    (
        grads, grads_other, enc_down_leaving, enc_down_staying, enc_gu_sum, dec_down_sum,
        dec_gu, cross_kept, cross_arrived,
    ) = together(
        grads, grads_other, enc_down_leaving, enc_down_staying, enc_gu_sum, dec_down_sum,
        dec_gu, cross_half[0], cross_half[1],
    )
    cross_half = halve(halved(cross_kept, cross_arrived), 4)
    attention_parts = [
        (
            [grads[:kinds_wide], enc_att],
            [grads_other[:kinds_wide], enc_att_other],
            [((0, 2), enc_normed), ((3, 3), enc_branch)],
        ),
        (
            [grads[kinds_wide:], dec_att],
            [grads_other[kinds_wide:], dec_att_other],
            [((0, 2), dec_normed), ((3, 3), self_branch)],
        ),
    ]
    if ctx_size == 16:
        both_part = small_parts(ctx_size, width, side, attention_parts)
        both_part, low_arrived, cross_kept, cross_arrived = together(
            both_part, low_arrived, cross_half[0], cross_half[1]
        )
        cross_half = halve(halved(cross_kept, cross_arrived), 8)
    partial_others = low_arrived.astype(f32)
    part, g_enc_norm_attn = norm_backward(
        enc_in, enc_norm_attn, own(enc_partial) + partial_others[:D]
    )
    grad_enc_input = own(grad_enc_mid) + part
    part, g_dec_norm_self = norm_backward(
        dec_in, dec_norm_self, own(self_partial) + partial_others[D:]
    )
    grad_dec_input = own(grad_mid) + part
    loss_part = jnp.sum(own(difference * difference * mask_pair))

    enc_bias_part = bucket_grads(enc_hot, enc_grad_line)
    dec_bias_part = bucket_grads(dec_hot, dec_grad_line)
    gains = jnp.concatenate(
        [
            g_enc_norm_attn,
            0.5 * g_enc_norm_ff,
            g_dec_norm_self,
            0.5 * g_dec_norm_cross,
            0.5 * g_dec_norm_ff,
        ]
    )
    small = jnp.concatenate(
        [
            gains,
            enc_bias_part.reshape(-1),
            dec_bias_part.reshape(-1),
            loss_part[None],
        ]
    )
    if ctx_size == 16:
        count = small.shape[0]
        padded = -(-count // 1024) * 1024
        small = jnp.pad(small, (0, padded - count)).reshape(8, padded // 8)
        columns = enc_down_leaving.shape[-2]
        both_part, small, cross_kept = together(both_part, small, cross_half[0])
        both_shard, enc_gu, enc_down_rows, dec_down_rows, small = last_exchanges(
            6,
            both_part,
            enc_gu_sum[:, 0].transpose(1, 0, 2, 3).reshape(2, 2 * columns, D),
            enc_down_leaving.reshape(2, columns, D),
            enc_down_staying.reshape(2, columns, D),
            dec_down_sum.reshape(2, columns, D),
            small,
        )
        small, cross_arrived = together(small, cross_half[1])
        small = small.reshape(-1)[:count]
        cross_shard = halved(cross_kept, cross_arrived)[0]
        enc_shard, self_shard = jnp.split(both_shard, 2, axis=0)
    else:
        small = total_over_devices(small, 7, ctx_size)
        enc_shard, self_shard = [
            halving(small_parts(ctx_size, width, side, [part]), 1) for part in attention_parts
        ]
        cross_shard = halving(halved(*cross_half), 8)

        def finished(part):
            kept, sent = after_low(part)
            return last_end(*last_start(kept, swap(sent)))

        enc_gu, dec_down_rows = finished(enc_gu_sum), finished(dec_down_sum)
        enc_down_first = flip(enc_down_leaving, REACH_PAIRS).astype(f32)
        enc_down_rows = finished((enc_down_staying + enc_down_first).astype(bf16))
    teacher_loss = small[-1] / (D * valid_total)
    gain = [small[i * D : (i + 1) * D] for i in range(5)]
    bias_size = enc_bias_part.size
    bias = [
        small[5 * D + i * bias_size : 5 * D + (i + 1) * bias_size].reshape(enc_bias_part.shape)
        for i in range(2)
    ]

    def pieces(shard, kinds):
        each = shard.shape[0] // len(kinds)
        made = []
        for i, transposed in enumerate(kinds):
            piece = shard[i * each : (i + 1) * each].astype(f32)
            made.append(piece.T if transposed else piece)
        return made

    dec_gate_up = pieces(dec_gu, (True, True))
    dec_down_g = pieces(dec_down_rows, (False,))
    enc_gate_up = pieces(enc_gu, (True, True))
    enc_down_g = pieces(enc_down_rows, (False,))
    kinds = (True, True, True, False)
    enc_attn = pieces(enc_shard, kinds)
    dec_attn = pieces(self_shard, kinds) + pieces(cross_shard, kinds)
    return (
        teacher_loss,
        dec_output.T,
        grad_enc_input.T,
        grad_dec_input.T,
        gain[0],
        *enc_attn,
        gain[1],
        *enc_gate_up,
        *enc_down_g,
        bias[0],
        gain[2],
        *dec_attn[:4],
        gain[3],
        *dec_attn[4:],
        gain[4],
        *dec_gate_up,
        *dec_down_g,
        bias[1],
    )


def solution(mesh):
    rows = P(("ctx", "fsdp"), None)
    split_columns = P(None, "fsdp")
    split_rows = P("fsdp", None)
    attention_in = (split_columns,) * 3 + (split_rows,)
    feed_in = (split_columns,) * 2 + (split_rows,)
    in_specs = (
        (rows,) * 3
        + (P(("ctx", "fsdp")), P(), P(), P())
        + (P(),)
        + attention_in
        + (P(),)
        + feed_in
        + (P(), P())
        + attention_in
        + (P(),)
        + attention_in
        + (P(),)
        + feed_in
        + (P(),)
    )
    columns = P(None, ("ctx", "fsdp"))
    attention_out = (columns,) * 3 + (rows,)
    feed_out = (columns,) * 2 + (rows,)
    out_specs = (
        (P(),)
        + (rows,) * 3
        + (P(),)
        + attention_out
        + (P(),)
        + feed_out
        + (P(), P())
        + attention_out
        + (P(),)
        + attention_out
        + (P(),)
        + feed_out
        + (P(),)
    )
    return jax.shard_map(body, mesh=mesh, in_specs=in_specs, out_specs=out_specs, check_vma=False)
```

```python
import functools

import jax
import jax.numpy as jnp
from jax import lax
from jax.experimental import pallas as pl
from jax.experimental.pallas import tpu as pltpu
from jax.sharding import PartitionSpec as P

D = 1472
HEAD = 64
REACH_PAIRS = 4
WIN = 3 * REACH_PAIRS
epsilon = 1e-06
far_below = -1e30
bf16 = jnp.bfloat16
f32 = jnp.float32
MESH = pl.DeviceIdType.MESH
FEED_LIMIT = 16 * 1024 * 1024
SMALL_COST = pl.CostEstimate(flops=0, bytes_accessed=500_000, transcendentals=0)


def dot(left, right, left_dim=1, right_dim=0):
    return lax.dot_general(
        left, right, (((left_dim,), (right_dim,)), ((), ())), preferred_element_type=f32
    )


def swap(value):
    return lax.ppermute(value, "fsdp", [(0, 1), (1, 0)])


def flipped(index, bit):
    return index + bit - 2 * bit * lax.rem(index // bit, 2)


def window_kernel(flags, swaps, summed, *refs):
    arrays = len(flags)
    total = arrays + swaps
    given = total + (1 if summed else 0)
    ins, outs = refs[:given], refs[given : 2 * given]
    local_sem, send_sem, recv_sem, swap_send, swap_recv = refs[2 * given : 2 * given + 5]
    rounds = lax.axis_size("ctx").bit_length() if summed else 0
    if summed:
        sum_mine, sum_theirs, sum_send, sum_recv = refs[2 * given + 5 :]
    R = REACH_PAIRS
    ctx = lax.axis_index("ctx")
    fsdp = lax.axis_index("fsdp")
    groups = lax.axis_size("ctx") // R
    group = ctx // R
    place = lax.rem(ctx, R)
    near, far = flipped(place, 1), flipped(place, 2)
    dev_near, dev_far = group * R + near, group * R + far
    dev_up, dev_down = ctx + R, ctx - R
    has_up, has_down = group < groups - 1, group > 0
    barrier = pltpu.get_barrier_semaphore()

    def greet(device):
        pl.semaphore_signal(barrier, inc=1, device_id=(device, fsdp), device_id_type=MESH)

    greet(dev_near)
    greet(dev_far)
    if swaps:
        pl.semaphore_signal(barrier, inc=1, device_id=(ctx, 1 - fsdp), device_id_type=MESH)

    @pl.when(has_up)
    def _():
        greet(dev_up)

    @pl.when(has_down)
    def _():
        greet(dev_down)

    for k in range(2, rounds - 1):
        greet(flipped(ctx, 1 << k))

    greeted = 2 + (1 if swaps else 0) + max(rounds - 3, 0)
    pl.semaphore_wait(barrier, greeted + has_up.astype(jnp.int32) + has_down.astype(jnp.int32))

    def copies(number, source_slot, slot, device, use=lambda f: True, part=None):
        made = []
        for k, (below, above, split) in enumerate(flags):
            if not use(flags[k]):
                continue
            rows = ins[k].shape[0]
            cut = rows if not split else (rows // 2 if not (below and above) else 3 * rows // 8)
            where = {None: (0, rows), 0: (0, cut), 1: (cut, rows)}[part]
            if where[0] == where[1]:
                continue
            span = pl.ds(where[0], where[1] - where[0])
            source = ins[k] if source_slot is None else outs[k].at[source_slot, span]
            made.append(
                pltpu.make_async_remote_copy(
                    src_ref=source,
                    dst_ref=outs[k].at[slot, span],
                    send_sem=send_sem.at[k, number],
                    recv_sem=recv_sem.at[k, number],
                    device_id=(device, fsdp),
                    device_id_type=MESH,
                )
            )
        return made

    def start(made):
        for copy in made:
            copy.start()

    sums = [
        pltpu.make_async_remote_copy(
            src_ref=sum_mine.at[k],
            dst_ref=sum_theirs.at[k],
            send_sem=sum_send.at[k],
            recv_sem=sum_recv.at[k],
            device_id=(ctx, 1 - fsdp) if k == 0 else (flipped(ctx, 1 << (k - 1)), fsdp),
            device_id_type=MESH,
        )
        for k in range(rounds)
    ]

    def sum_step(k):
        if k == 0:
            sum_mine[0] = ins[total][...]
        else:
            sums[k - 1].wait_recv()
            added = sum_mine[k - 1] + sum_theirs[k - 1]
            if k == rounds:
                outs[total][...] = added
            else:
                sum_mine[k] = added
        if k < rounds:
            sums[k].start()

    def arrived(made):
        for copy in made:
            copy.wait_recv()

    def left(made):
        for copy in made:
            copy.wait_send()

    below = lambda flag: flag[0]
    above = lambda flag: flag[1]
    to_up = copies(0, None, place, dev_up, below)
    to_down = copies(1, None, 2 * R + place, dev_down, above)
    to_far = copies(2, None, R + place, dev_far)
    to_near = copies(3, None, R + place, dev_near)
    far_low = copies(4, place, place, dev_far, below, 0)
    far_high = copies(5, 2 * R + place, 2 * R + place, dev_far, above, 0)
    up_far = copies(6, R + far, far, dev_up, below, 1)
    down_far = copies(7, R + far, 2 * R + far, dev_down, above, 1)
    near_low = copies(8, place, place, dev_near, below)
    near_high = copies(9, 2 * R + place, 2 * R + place, dev_near, above)
    near_far = copies(10, R + far, R + far, dev_near)
    near_far_low = copies(11, far, far, dev_near, below)
    near_far_high = copies(12, 2 * R + far, 2 * R + far, dev_near, above)
    own = [
        pltpu.make_async_copy(ins[k], outs[k].at[R + place], local_sem.at[k])
        for k in range(arrays)
    ]

    across = [
        pltpu.make_async_remote_copy(
            src_ref=ins[arrays + k],
            dst_ref=outs[arrays + k],
            send_sem=swap_send.at[k],
            recv_sem=swap_recv.at[k],
            device_id=(ctx, 1 - fsdp),
            device_id_type=MESH,
        )
        for k in range(swaps)
    ]

    @pl.when(has_up)
    def _():
        start(to_up)

    @pl.when(has_down)
    def _():
        start(to_down)

    if summed:
        sum_step(0)
    start(to_far)
    start(to_near)
    start(across)
    start(own)
    if summed:
        sum_step(1)
    arrived(to_far)
    if summed:
        sum_step(2)

    @pl.when(has_up)
    def _():
        start(up_far)

    @pl.when(has_down)
    def _():
        start(down_far)

    start(near_far)

    @pl.when(has_down)
    def _():
        arrived(to_up)
        start(far_low)
        start(near_low)

    @pl.when(has_up)
    def _():
        arrived(to_down)
        start(far_high)
        start(near_high)

    if summed:
        sum_step(3)

    @pl.when(has_down)
    def _():
        arrived(far_low)
        arrived(up_far)
        start(near_far_low)

    @pl.when(has_up)
    def _():
        arrived(far_high)
        arrived(down_far)
        start(near_far_high)

    arrived(to_near)
    arrived(near_far)

    @pl.when(has_down)
    def _():
        arrived(near_low)
        arrived(near_far_low)
        left(far_low)
        left(near_low)
        left(near_far_low)
        left(to_down)
        left(down_far)

    @pl.when(has_up)
    def _():
        arrived(near_high)
        arrived(near_far_high)
        left(far_high)
        left(near_high)
        left(near_far_high)
        left(to_up)
        left(up_far)

    left(to_far)
    left(to_near)
    left(near_far)
    for copy in own + across:
        copy.wait()
    if summed:
        for k in range(4, rounds + 1):
            sum_step(k)
        left(sums)


BOTH, BELOW, ABOVE = (True, True), (True, False), (False, True)


def window_gather(number, pairs, swapped=(), summand=None):
    values = [value for value, _ in pairs]
    flags = tuple(
        sides + (value.dtype == bf16 and value.shape[0] % 128 == 0,) for value, sides in pairs
    )
    count, swaps = len(values), len(swapped)
    vmem = pl.BlockSpec(memory_space=pltpu.VMEM)
    specs = [vmem] * count + [pl.BlockSpec(memory_space=pl.ANY)] * swaps
    extra, sum_scratch = [], []
    if summand is not None:
        specs = specs + [vmem]
        extra = [summand]
        rounds = lax.axis_size("ctx").bit_length()
        sum_scratch = [pltpu.VMEM((rounds,) + summand.shape, f32)] * 2 + [
            pltpu.SemaphoreType.DMA((rounds,))
        ] * 2
    return pl.pallas_call(
        functools.partial(window_kernel, flags, swaps, summand is not None),
        out_shape=[jax.ShapeDtypeStruct((WIN,) + v.shape, v.dtype) for v in values]
        + [jax.ShapeDtypeStruct(v.shape, v.dtype) for v in [*swapped, *extra]],
        in_specs=specs,
        out_specs=specs,
        scratch_shapes=[
            pltpu.SemaphoreType.DMA((count,)),
            pltpu.SemaphoreType.DMA((count, 13)),
            pltpu.SemaphoreType.DMA((count, 13)),
            pltpu.SemaphoreType.DMA((max(swaps, 1),)),
            pltpu.SemaphoreType.DMA((max(swaps, 1),)),
        ]
        + sum_scratch,
        compiler_params=pltpu.CompilerParams(
            collective_id=number, has_side_effects=True, vmem_limit_bytes=4 << 20
        ),
        cost_estimate=SMALL_COST,
        name="window_gather",
    )(*values, *swapped, *extra)


def total_kernel(rounds, sides, x_ref, o_ref, mine, theirs, send_sem, recv_sem):
    ctx = lax.axis_index("ctx")
    fsdp = lax.axis_index("fsdp")
    partners = [(flipped(ctx, 1 << k), fsdp) for k in range(rounds - sides)]
    partners += [(ctx, 1 - fsdp)] * sides
    barrier = pltpu.get_barrier_semaphore()
    for partner in partners:
        pl.semaphore_signal(barrier, inc=1, device_id=partner, device_id_type=MESH)
    pl.semaphore_wait(barrier, rounds)
    mine[0] = x_ref[...]
    for k, partner in enumerate(partners):
        copy = pltpu.make_async_remote_copy(
            src_ref=mine.at[k],
            dst_ref=theirs.at[k],
            send_sem=send_sem.at[k],
            recv_sem=recv_sem.at[k],
            device_id=partner,
            device_id_type=MESH,
        )
        copy.start()
        copy.wait()
        added = mine[k] + theirs[k]
        if k + 1 < rounds:
            mine[k + 1] = added
        else:
            o_ref[...] = added


def total_over_devices(value, number, ctx_size, sides=1):
    rounds = ctx_size.bit_length() - 1 + sides
    padded = -(-value.shape[0] // 1024) * 1024
    wide = jnp.pad(value, (0, padded - value.shape[0])).reshape(8, padded // 8)
    vmem = pl.BlockSpec(memory_space=pltpu.VMEM)
    made = pl.pallas_call(
        functools.partial(total_kernel, rounds, sides),
        out_shape=jax.ShapeDtypeStruct(wide.shape, f32),
        in_specs=[vmem],
        out_specs=vmem,
        scratch_shapes=[
            pltpu.VMEM((rounds,) + wide.shape, f32),
            pltpu.VMEM((rounds,) + wide.shape, f32),
            pltpu.SemaphoreType.DMA((rounds,)),
            pltpu.SemaphoreType.DMA((rounds,)),
        ],
        compiler_params=pltpu.CompilerParams(collective_id=number, has_side_effects=True),
        cost_estimate=SMALL_COST,
        name="total_over_devices",
    )(wide)
    return made.reshape(-1)[: value.shape[0]]


def head_rows(width):
    rows = lax.broadcasted_iota(jnp.int32, (width, 1), 0)
    return [(rows >= h * HEAD) & (rows < (h + 1) * HEAD) for h in range(width // HEAD)]


def head_lanes(width):
    lanes = lax.broadcasted_iota(jnp.int32, (1, width), 1)
    return [(lanes >= h * HEAD) & (lanes < (h + 1) * HEAD) for h in range(width // HEAD)]


def only(value, mask):
    return jnp.where(mask, value, jnp.zeros_like(value))


def by_token(value):
    width, rows = value.shape
    full = -(-width // 128) * 128
    return jnp.concatenate([value, jnp.zeros((full - width, rows), value.dtype)], axis=0).T[:, :width]


def toeplitz(line_ref, head, block, rows):
    start = pl.multiple_of(block * rows, rows)
    segment = line_ref[pl.ds(head, 1), pl.ds(start, 2 * rows)]
    spread = jnp.broadcast_to(segment, (rows, 2 * rows))
    return pltpu.roll(spread, rows + 1, 1, stride=1, stride_axis=0)[:, :rows]


def halves(value, op):
    half = value.shape[1] // 2
    return op(value[:, :half], value[:, half:])


def forward_kernel(biased, bounds, q_ref, kv_ref, lo_ref, hi_ref, *rest):
    if biased:
        line_ref, rest = rest[0], rest[1:]
    o_ref, att_ref, l_ref, s_ref, m_ref, sum_ref, acc_ref, rest_ref = rest
    width, rows = q_ref.shape
    heads = width // HEAD
    lanes, bands = head_lanes(width), head_rows(width)
    first, last, key_base = bounds[0], bounds[1], bounds[2]
    lo, hi = lo_ref[...], hi_ref[...]
    m_ref[...] = jnp.full_like(m_ref, far_below)
    sum_ref[...] = jnp.zeros_like(sum_ref)
    acc_ref[...] = jnp.zeros_like(acc_ref)
    q = by_token(q_ref[...])

    def scores(block, carry):
        keys = kv_ref[block, :width]
        key_pos = key_base + block * rows + lax.broadcasted_iota(jnp.int32, (rows, rows), 1)
        allowed = (key_pos >= lo) & (key_pos <= hi)
        for h in range(heads):
            s = dot(only(q, lanes[h]), keys)
            if biased:
                s = s + toeplitz(line_ref, h, block, rows)
            s = jnp.where(allowed, s, far_below)
            s_ref[block, h] = s
            m_ref[h] = jnp.maximum(m_ref[h], halves(s, jnp.maximum))
        return carry

    lax.fori_loop(first, last + 1, scores, 0)
    tops = [jnp.max(m_ref[h], axis=1, keepdims=True) for h in range(heads)]

    def weigh(block, carry):
        for h in range(heads):
            p = jnp.exp(s_ref[block, h] - tops[h])
            s_ref[block, h] = p
            sum_ref[h] += halves(p, jnp.add)
        return carry

    lax.fori_loop(first, last + 1, weigh, 0)
    totals = [jnp.sum(sum_ref[h], axis=1, keepdims=True) for h in range(heads)]
    shares = [1.0 / total for total in totals]
    rest_ref[...] = jnp.zeros_like(rest_ref)

    def mix(block, carry):
        values = kv_ref[block, width:]
        total, left = None, None
        for h in range(heads):
            p = s_ref[block, h] * shares[h]
            low_p = p.astype(bf16)
            band = only(values, bands[h])
            part = dot(band, low_p, 1, 1)
            rest_part = dot(band, (p - low_p.astype(f32)).astype(bf16), 1, 1)
            total = part if total is None else total + part
            left = rest_part if left is None else left + rest_part
        acc_ref[...] += total
        rest_ref[...] += left
        return carry

    lax.fori_loop(first, last + 1, mix, 0)
    column = lax.broadcasted_iota(jnp.int32, (rows, 128), 1)
    logs = jnp.zeros((rows, 128), f32)
    for h in range(heads):
        logs = jnp.where(column == h, tops[h] + jnp.log(totals[h]), logs)
    o_ref[...] = acc_ref[...] + rest_ref[...]
    att_ref[...] = acc_ref[...].astype(bf16)
    l_ref[...] = logs.T[:8]


def query_kernel(biased, bounds, qd_ref, kv_ref, lo_ref, hi_ref, stat_ref, *rest):
    if biased:
        line_ref, dq_ref, gline_ref, acc_ref = rest
        gline_ref[...] = jnp.zeros_like(gline_ref)
    else:
        dq_ref, acc_ref = rest
    width, rows = qd_ref.shape[0] // 2, qd_ref.shape[1]
    heads = width // HEAD
    lanes, bands = head_lanes(width), head_rows(width)
    first, last, key_base = bounds[0], bounds[1], bounds[2]
    lo, hi = lo_ref[...], hi_ref[...]
    acc_ref[...] = jnp.zeros_like(acc_ref)
    q, da = by_token(qd_ref[:width]), by_token(qd_ref[width:])
    logs = [stat_ref[:, h : h + 1] for h in range(heads)]
    deltas = [stat_ref[:, heads + h : heads + h + 1] for h in range(heads)]

    def step(block, carry):
        keys = kv_ref[block, :width]
        values = kv_ref[block, width:]
        key_pos = key_base + block * rows + lax.broadcasted_iota(jnp.int32, (rows, rows), 1)
        allowed = (key_pos >= lo) & (key_pos <= hi)
        total = None
        for h in range(heads):
            s = dot(only(q, lanes[h]), keys)
            if biased:
                s = s + toeplitz(line_ref, h, block, rows)
            p = jnp.exp(jnp.where(allowed, s - logs[h], far_below))
            dp = dot(only(da, lanes[h]), values)
            ds = (p * (dp - deltas[h])).astype(bf16)
            part = dot(only(keys, bands[h]), ds, 1, 1)
            total = part if total is None else total + part
            if biased:
                folded = jnp.concatenate([ds.astype(f32), jnp.zeros((rows, rows), f32)], axis=1)
                half = rows // 2
                while half >= 1:
                    folded = pltpu.roll(folded[:half], half, 1) + folded[half:]
                    half //= 2
                start = pl.multiple_of(block * rows, rows)
                gline_ref[pl.ds(h, 1), pl.ds(start, 2 * rows)] += folded
        acc_ref[...] += total
        return carry

    lax.fori_loop(first, last + 1, step, 0)
    dq_ref[...] = acc_ref[...].astype(bf16)


def key_kernel(biased, bounds, kv_ref, qd_ref, stat_ref, lo_ref, hi_ref, *rest):
    if biased:
        line_ref, rest = rest[0], rest[1:]
    dkv_ref, dk_acc, dv_acc = rest
    width, rows = kv_ref.shape[0] // 2, kv_ref.shape[1]
    heads = width // HEAD
    lanes, bands = head_lanes(width), head_rows(width)
    first, last, query_base = bounds[0], bounds[1], bounds[2]
    lo, hi = lo_ref[...], hi_ref[...]
    dk_acc[...] = jnp.zeros_like(dk_acc)
    dv_acc[...] = jnp.zeros_like(dv_acc)
    keys, values = by_token(kv_ref[:width]), by_token(kv_ref[width:])

    def step(block, carry):
        q = qd_ref[block, :width]
        da = qd_ref[block, width:]
        query_pos = query_base + block * rows + lax.broadcasted_iota(jnp.int32, (rows, rows), 1)
        allowed = (query_pos >= lo) & (query_pos <= hi)
        total_k = None
        total_v = None
        for h in range(heads):
            s = dot(only(keys, lanes[h]), q)
            if biased:
                s = s + toeplitz(line_ref, h, block, rows)
            p = jnp.exp(jnp.where(allowed, s - stat_ref[block, h : h + 1, :], far_below))
            dp = dot(only(values, lanes[h]), da)
            ds = (p * (dp - stat_ref[block, heads + h : heads + h + 1, :])).astype(bf16)
            part_k = dot(only(q, bands[h]), ds, 1, 1)
            part_v = dot(only(da, bands[h]), p.astype(bf16), 1, 1)
            total_k = part_k if total_k is None else total_k + part_k
            total_v = part_v if total_v is None else total_v + part_v
        dk_acc[...] += total_k
        dv_acc[...] += total_v
        return carry

    lax.fori_loop(first, last + 1, step, 0)
    dkv_ref[:width] = dk_acc[...].astype(bf16)
    dkv_ref[width:] = dv_acc[...].astype(bf16)


def local_call(kernel, out_shape, scratch, name, limit, bounds, *values):
    vmem = pl.BlockSpec(memory_space=pltpu.VMEM)
    smem = pl.BlockSpec(memory_space=pltpu.SMEM)
    return pl.pallas_call(
        kernel,
        out_shape=out_shape,
        in_specs=[smem] + [vmem] * len(values),
        out_specs=jax.tree.map(lambda _: vmem, out_shape),
        scratch_shapes=scratch,
        compiler_params=pltpu.CompilerParams(vmem_limit_bytes=limit << 20),
        cost_estimate=SMALL_COST,
        name=name,
    )(bounds, *values)


def attend(q, kv_window, bounds, lo, hi, line):
    width, rows = q.shape
    heads = width // HEAD
    biased = line is not None
    return local_call(
        functools.partial(forward_kernel, biased),
        [
            jax.ShapeDtypeStruct((width, rows), f32),
            jax.ShapeDtypeStruct((width, rows), bf16),
            jax.ShapeDtypeStruct((8, rows), f32),
        ],
        [
            pltpu.VMEM((WIN, heads, rows, rows), f32),
            pltpu.VMEM((heads, rows, rows // 2), f32),
            pltpu.VMEM((heads, rows, rows // 2), f32),
            pltpu.VMEM((width, rows), f32),
            pltpu.VMEM((width, rows), f32),
        ],
        "attend_forward",
        16,
        bounds,
        q,
        kv_window,
        lo,
        hi,
        *([line] if biased else []),
    )


def attend_queries(qd, kv_window, bounds, lo, hi, stats, line):
    width, rows = qd.shape[0] // 2, qd.shape[1]
    biased = line is not None
    shapes = [jax.ShapeDtypeStruct((width, rows), bf16)]
    if biased:
        shapes.append(jax.ShapeDtypeStruct(line.shape, f32))
    return local_call(
        functools.partial(query_kernel, biased),
        shapes,
        [pltpu.VMEM((width, rows), f32)],
        "attend_queries",
        10,
        bounds,
        qd,
        kv_window,
        lo,
        hi,
        stats,
        *([line] if biased else []),
    )


def attend_keys(kv, qd_window, stat_window, bounds, lo, hi, line):
    width, rows = kv.shape[0] // 2, kv.shape[1]
    biased = line is not None
    return local_call(
        functools.partial(key_kernel, biased),
        jax.ShapeDtypeStruct((2 * width, rows), bf16),
        [pltpu.VMEM((width, rows), f32)] * 2,
        "attend_keys",
        10,
        bounds,
        kv,
        qd_window,
        stat_window,
        lo,
        hi,
        *([line] if biased else []),
    )


def prepare_kernel(grad_ref, w_ref, q_ref, o_ref, log_ref, qd_ref, row_ref, wide_ref):
    width, rows = q_ref.shape
    heads = width // HEAD
    da = dot(w_ref[...], grad_ref[...]).astype(bf16)
    qd_ref[:width] = q_ref[...]
    qd_ref[width:] = da
    product = da.astype(f32) * o_ref[...]
    row = lax.broadcasted_iota(jnp.int32, (128, rows), 0)
    stats = jnp.concatenate([log_ref[...], jnp.zeros((120, rows), f32)], axis=0)
    for h, mask in enumerate(head_rows(width)):
        delta = jnp.sum(only(product, mask), axis=0, keepdims=True)
        stats = jnp.where(row == heads + h, delta, stats)
    row_ref[...] = stats[:8]
    wide_ref[...] = stats.T


def prepare(grad, w_out, q, out, log_rows):
    width, rows = q.shape
    vmem = pl.BlockSpec(memory_space=pltpu.VMEM)
    return pl.pallas_call(
        prepare_kernel,
        out_shape=[
            jax.ShapeDtypeStruct((2 * width, rows), bf16),
            jax.ShapeDtypeStruct((8, rows), f32),
            jax.ShapeDtypeStruct((rows, 128), f32),
        ],
        in_specs=[vmem] * 5,
        out_specs=[vmem] * 3,
        compiler_params=pltpu.CompilerParams(vmem_limit_bytes=10 << 20),
        cost_estimate=SMALL_COST,
        name="attention_prepare",
    )(grad, w_out, q, out, log_rows)


KINDS = 4


def small_kernel(blocks, width, layout, place, *refs):
    out_ref = refs[-1]
    columns = width // blocks
    side = place[0]
    row = lax.broadcasted_iota(jnp.int32, (blocks * KINDS * columns, 1), 0)
    left, block = row // (KINDS * columns), jnp.zeros_like(row)
    for _ in range(blocks.bit_length() - 1):
        block = 2 * block + lax.rem(left, 2)
        left = left // 2
    kind = lax.rem(row // columns, KINDS)
    column = columns * (2 * block + side) + lax.rem(row, columns)
    away = jnp.where(column // width == side, 0, 1)
    wanted = away * (KINDS * width) + kind * width + lax.rem(column, width)
    used = 0
    for number, (counted, kinds) in enumerate(layout):
        values = jnp.concatenate([ref[...] for ref in refs[used : used + counted]], axis=0)
        sources = refs[used + counted : used + counted + len(kinds)]
        used += counted + len(kinds)
        spot = lax.broadcasted_iota(jnp.int32, (1, values.shape[0]), 1)
        onehot = jnp.where(wanted == spot, 1.0, 0.0).astype(bf16)
        chosen = dot(onehot, values).astype(bf16)
        total = None
        for (first, last), source in zip(kinds, sources):
            part = dot(only(chosen, (kind >= first) & (kind <= last)), source[...], 1, 1)
            total = part if total is None else total + part
        total = total.astype(bf16)
        depth = KINDS * columns
        for index in range(blocks):
            out_ref[index, number * depth : (number + 1) * depth] = total[
                index * depth : (index + 1) * depth
            ]


def small_parts(blocks, width, side, parts):
    vmem = pl.BlockSpec(memory_space=pltpu.VMEM)
    smem = pl.BlockSpec(memory_space=pltpu.SMEM)
    layout, values = [], []
    for own, other, sources in parts:
        layout.append((len(own) + len(other), tuple(span for span, _ in sources)))
        values += [*own, *other, *[source for _, source in sources]]
    depth = parts[0][2][0][1].shape[0]
    rows = len(parts) * KINDS * (width // blocks)
    return pl.pallas_call(
        functools.partial(small_kernel, blocks, width, tuple(layout)),
        out_shape=jax.ShapeDtypeStruct((blocks, rows, depth), bf16),
        in_specs=[smem] + [vmem] * len(values),
        out_specs=vmem,
        compiler_params=pltpu.CompilerParams(vmem_limit_bytes=22 << 20),
        cost_estimate=SMALL_COST,
        name="attention_weight_part",
    )(jnp.stack([side]), *values)


CHUNK = 256
GELU_RATE = 0.7978845608028654
GELU_CUBE = 0.044715


def feed_kernel(x_ref, gate_ref, up_ref, down_ref, sum_ref, low_ref, hidden_ref, d1_ref, d2_ref):
    x = x_ref[...].T
    for start in range(0, gate_ref.shape[1], CHUNK):
        span = slice(start, start + CHUNK)
        gating = dot(x, gate_ref[:, span]).T
        upward = dot(x, up_ref[:, span]).T
        square = gating * gating
        t = jnp.tanh(GELU_RATE * gating * (1.0 + GELU_CUBE * square))
        half = 0.5 * (1.0 + t)
        unit = gating * half
        slope = half + 0.5 * gating * (1.0 - t * t) * (
            GELU_RATE * (1.0 + 3.0 * GELU_CUBE * square)
        )
        hidden_ref[span, :] = (unit * upward).astype(bf16)
        d1_ref[span, :] = slope * upward
        d2_ref[span, :] = unit
    total = dot(down_ref[...], hidden_ref[...])
    sum_ref[...] = total
    low_ref[...] = total.astype(bf16)


def feed_back_kernel(e_ref, gate_ref, up_ref, down_ref, d1_ref, d2_ref, sum_ref, low_ref, gg_ref, gu_ref):
    e = e_ref[...].T
    for start in range(0, gate_ref.shape[1], CHUNK):
        span = slice(start, start + CHUNK)
        grad_hidden = dot(e, down_ref[:, span]).astype(bf16).astype(f32).T
        gg_ref[span, :] = (grad_hidden * d1_ref[span, :]).astype(bf16)
        gu_ref[span, :] = (grad_hidden * d2_ref[span, :]).astype(bf16)
    total = dot(gate_ref[...], gg_ref[...]) + dot(up_ref[...], gu_ref[...])
    sum_ref[...] = total
    low_ref[...] = total.astype(bf16)


def feed_call(kernel, name, source, weights, chunked, outs):
    depth, rows = source.shape
    columns = weights[0].shape[1]
    vmem = pl.BlockSpec(memory_space=pltpu.VMEM)
    return pl.pallas_call(
        kernel,
        out_shape=[
            jax.ShapeDtypeStruct((depth, rows), f32),
            jax.ShapeDtypeStruct((depth, rows), bf16),
        ]
        + [jax.ShapeDtypeStruct((columns, rows), kind) for kind in outs],
        in_specs=[vmem] * (4 + len(chunked)),
        out_specs=[vmem] * (2 + len(outs)),
        compiler_params=pltpu.CompilerParams(vmem_limit_bytes=FEED_LIMIT),
        cost_estimate=SMALL_COST,
        name=name,
    )(source, *weights, *chunked)


def feed_forward(source, weights):
    return feed_call(feed_kernel, "feed_forward", source, weights, (), (bf16, f32, f32))


def feed_backward(grad, weights, d1, d2):
    return feed_call(feed_back_kernel, "feed_backward", grad, weights, (d1, d2), (bf16, bf16))


def last_kernel(
    part_ref, gu_ref, leave_ref, stay_ref, dec_ref, small_ref,
    both_out, gu_out, down_out, dec_out, small_out,
    near_r, near_s, far_r, far_s, z_r, z_s, top_r,
    gu_x, gu_send, gu_top, down_z, down_sum, down_x, down_send, down_top,
    dec_x, dec_send, dec_top, mine, theirs, send_sem, recv_sem,
):
    ctx = lax.axis_index("ctx")
    side = lax.axis_index("fsdp")
    bits = [lax.rem(ctx // step, 2) for step in (1, 2, 4, 8)]
    across = (ctx, 1 - side)
    partners = [(flipped(ctx, step), side) for step in (1, 2, 4, 8)]
    same = side == bits[3]
    barrier = pltpu.get_barrier_semaphore()
    for device in [across] + partners:
        pl.semaphore_signal(barrier, inc=1, device_id=device, device_id_type=MESH)
    pl.semaphore_wait(barrier, 5)

    def copy(number, source, target, device):
        made = pltpu.make_async_remote_copy(
            src_ref=source,
            dst_ref=target,
            send_sem=send_sem.at[number],
            recv_sem=recv_sem.at[number],
            device_id=device,
            device_id_type=MESH,
        )
        made.start()
        return made

    def added(kept, arrived):
        return kept.astype(f32) + arrived.astype(f32)

    def small_copy(k, device):
        return copy(9 if k == 4 else 12 + k, mine.at[k], theirs.at[k], device)

    def small_sum(k, made):
        made.wait_recv()
        total = mine[k] + theirs[k]
        if k < 4:
            mine[k + 1] = total
        else:
            small_out[...] = total

    near = copy(0, part_ref.at[pl.ds((1 - bits[0]) * 8, 8)], near_r, partners[0])
    mine[0] = small_ref[...]
    small_top = small_copy(0, partners[3])
    dec_across = copy(1, dec_ref.at[1 - side], dec_x, across)
    gu_across = copy(2, gu_ref.at[1 - side], gu_x, across)
    small_sum(0, small_top)
    small_z = small_copy(1, partners[2])
    down_first = copy(3, leave_ref, down_z, partners[2])

    near.wait_recv()
    near_s[...] = added(part_ref[pl.ds(bits[0] * 8, 8)], near_r[...]).astype(bf16)
    small_sum(1, small_z)
    small_far = small_copy(2, partners[1])
    far = copy(4, near_s.at[pl.ds((1 - bits[1]) * 4, 4)], far_r, partners[1])
    small_sum(2, small_far)
    small_near = small_copy(3, partners[0])

    dec_across.wait_recv()
    dec_send[...] = jnp.where(same, dec_x[...], dec_ref[side])
    dec_last = copy(5, dec_send, dec_top, partners[3])
    gu_across.wait_recv()
    gu_send[...] = jnp.where(same, gu_x[...], gu_ref[side])
    gu_last = copy(6, gu_send, gu_top, partners[3])
    small_sum(3, small_near)
    small_across = small_copy(4, across)
    down_first.wait_recv()
    down_sum[...] = added(stay_ref[...], down_z[...]).astype(bf16)
    down_across = copy(7, down_sum.at[1 - side], down_x, across)
    down_across.wait_recv()
    down_send[...] = jnp.where(same, down_x[...], down_sum[side])
    down_last = copy(8, down_send, down_top, partners[3])
    small_sum(4, small_across)

    far.wait_recv()
    far_s[...] = added(near_s[pl.ds(bits[1] * 4, 4)], far_r[...]).astype(bf16)
    z = copy(10, far_s.at[pl.ds((1 - bits[2]) * 2, 2)], z_r, partners[2])
    dec_last.wait_recv()
    dec_out[...] = added(jnp.where(same, dec_ref[side], dec_x[...]), dec_top[...])
    z.wait_recv()
    z_s[...] = added(far_s[pl.ds(bits[2] * 2, 2)], z_r[...]).astype(bf16)
    top = copy(11, z_s.at[1 - bits[3]], top_r, partners[3])
    gu_last.wait_recv()
    gu_out[...] = added(jnp.where(same, gu_ref[side], gu_x[...]), gu_top[...])
    down_last.wait_recv()
    down_out[...] = added(jnp.where(same, down_sum[side], down_x[...]), down_top[...])
    top.wait_recv()
    both_out[...] = added(z_s[bits[3]], top_r[...])
    for made in (
        near, dec_across, gu_across, down_first, far, dec_last, gu_last,
        down_across, down_last, z, top, small_top, small_z, small_far, small_near, small_across,
    ):
        made.wait_send()


def last_exchanges(number, part, gu, leave, stay, dec, small):
    blocks, rows, depth = part.shape
    vmem = pl.BlockSpec(memory_space=pltpu.VMEM)
    wide, narrow = gu.shape[1], dec.shape[1]
    return pl.pallas_call(
        last_kernel,
        out_shape=[
            jax.ShapeDtypeStruct((rows, depth), f32),
            jax.ShapeDtypeStruct((wide, depth), f32),
            jax.ShapeDtypeStruct((narrow, depth), f32),
            jax.ShapeDtypeStruct((narrow, depth), f32),
            jax.ShapeDtypeStruct(small.shape, f32),
        ],
        in_specs=[vmem] * 6,
        out_specs=[vmem] * 5,
        scratch_shapes=[
            pltpu.VMEM((size, rows, depth), bf16)
            for size in (blocks // 2, blocks // 2, blocks // 4, blocks // 4, blocks // 8, blocks // 8)
        ]
        + [pltpu.VMEM((rows, depth), bf16)]
        + [pltpu.VMEM((wide, depth), bf16)] * 3
        + [pltpu.VMEM((2, narrow, depth), bf16)] * 2
        + [pltpu.VMEM((narrow, depth), bf16)] * 6
        + [pltpu.VMEM((5,) + small.shape, f32)] * 2
        + [pltpu.SemaphoreType.DMA((16,)), pltpu.SemaphoreType.DMA((16,))],
        compiler_params=pltpu.CompilerParams(
            collective_id=number, has_side_effects=True, vmem_limit_bytes=20 << 20
        ),
        cost_estimate=SMALL_COST,
        name="last_exchanges",
    )(part, gu, leave, stay, dec, small)


def inverse_root(inputs):
    return lax.rsqrt(jnp.mean(inputs * inputs, axis=0, keepdims=True) + epsilon)


def root_norm(inputs, gain):
    return inputs * inverse_root(inputs) * gain[:, None]


def norm_backward(inputs, gain, grad):
    inverse = inverse_root(inputs)
    scaled = grad * gain[:, None]
    along = jnp.mean(inputs * scaled, axis=0, keepdims=True)
    grad_inputs = inverse * scaled - inputs * (inverse * inverse * inverse) * along
    return grad_inputs, jnp.sum(grad * inputs * inverse, axis=1)


def body(
    enc_input,
    dec_input,
    teacher,
    valid_mask,
    doc_lengths,
    enc_buckets,
    dec_buckets,
    enc_norm_attn,
    enc_query,
    enc_key,
    enc_value,
    enc_out_proj,
    enc_norm_ff,
    enc_gate,
    enc_up,
    enc_down,
    enc_rel_bias,
    dec_norm_self,
    dec_query,
    dec_key,
    dec_value,
    dec_out_proj,
    dec_norm_cross,
    cross_query,
    cross_key,
    cross_value,
    cross_out_proj,
    dec_norm_ff,
    dec_gate,
    dec_up,
    dec_down,
    dec_rel_bias,
):
    ctx = lax.axis_index("ctx")
    side = lax.axis_index("fsdp")
    ctx_size = lax.axis_size("ctx")
    own_rows = enc_input.shape[0]
    rows = 2 * own_rows
    width = enc_query.shape[1]
    heads = width // HEAD
    place = lax.rem(ctx, REACH_PAIRS)
    core_bit, far_bit = lax.rem(place, 2), place // 2

    def ordered(mine, other, axis=1):
        first = side == 0
        return jnp.concatenate(
            [jnp.where(first, mine, other), jnp.where(first, other, mine)], axis=axis
        )

    def pick(value, index, axis):
        return lax.dynamic_index_in_dim(value, index, axis, keepdims=False)

    def flip(value, bit):
        return lax.ppermute(value, "ctx", [(i, i ^ bit) for i in range(ctx_size)])

    def own(value):
        return lax.dynamic_slice_in_dim(value, side * own_rows, own_rows, 1)

    def others(value):
        return lax.dynamic_slice_in_dim(value, (1 - side) * own_rows, own_rows, 1)

    def together(*values):
        return lax.optimization_barrier(values)

    count = doc_lengths.shape[0]
    order = jnp.arange(count, dtype=jnp.int32)
    starts = jnp.sum(
        jnp.where(order[None, :] < order[:, None], doc_lengths[None, :], 0), axis=1
    )
    ends = starts + doc_lengths
    positions = ctx * rows + jnp.arange(rows, dtype=jnp.int32)[:, None]
    doc_lo = jnp.max(jnp.where(starts[None, :] <= positions, starts[None, :], 0), axis=1, keepdims=True)
    doc_hi = (
        jnp.min(
            jnp.where(ends[None, :] > positions, ends[None, :], ctx_size * rows),
            axis=1,
            keepdims=True,
        )
        - 1
    )
    base_block = ctx - place - REACH_PAIRS
    first_block = doc_lo[0, 0] // rows - base_block
    last_block = doc_hi[rows - 1, 0] // rows - base_block
    own_block = REACH_PAIRS + place
    base_pos = base_block * rows
    bounds_both = jnp.stack([first_block, last_block, base_pos])
    bounds_below = jnp.stack([first_block, own_block, base_pos])
    bounds_above = jnp.stack([own_block, last_block, base_pos])

    reach = enc_buckets.shape[0] // 2
    line_len = (WIN + 1) * rows
    pad_lo, pad_hi = reach, reach + rows
    line_start = (reach + 1 - rows) + pad_lo - rows * (REACH_PAIRS + place)
    reverse_start = (reach - rows) + pad_lo - rows * (REACH_PAIRS + place)

    def lines(rel_bias, buckets):
        hot = (
            buckets[:, None] == jnp.arange(rel_bias.shape[0], dtype=jnp.int32)[None, :]
        ).astype(f32)
        mine = lax.dynamic_slice_in_dim(rel_bias, side * heads, heads, 1)
        line = lax.dot_general(
            mine, hot, (((0,), (1,)), ((), ())), precision=lax.Precision.HIGHEST
        )
        hot_back = (
            buckets[::-1][:, None] == jnp.arange(rel_bias.shape[0], dtype=jnp.int32)[None, :]
        ).astype(f32)
        line_back = lax.dot_general(
            mine, hot_back, (((0,), (1,)), ((), ())), precision=lax.Precision.HIGHEST
        )
        padded = jnp.pad(line, ((0, 8 - heads), (pad_lo, pad_hi)))
        backward = jnp.pad(line_back, ((0, 8 - heads), (pad_lo, pad_hi)))
        return (
            hot,
            lax.dynamic_slice_in_dim(padded, line_start, line_len, 1),
            lax.dynamic_slice_in_dim(backward, reverse_start, line_len, 1),
        )

    enc_hot, enc_line, enc_back = lines(enc_rel_bias, enc_buckets)
    dec_hot, dec_line, dec_back = lines(dec_rel_bias, dec_buckets)

    def bucket_grads(hot, grad_line):
        padded = jnp.zeros((heads, 2 * reach + pad_lo + pad_hi), f32)
        padded = lax.dynamic_update_slice_in_dim(padded, grad_line[:heads], line_start, 1)
        cropped = padded[:, pad_lo : pad_lo + 2 * reach]
        grads = lax.dot_general(
            hot, cropped, (((0,), (1,)), ((), ())), precision=lax.Precision.HIGHEST
        )
        whole = jnp.zeros((hot.shape[1], 2 * heads), f32)
        return lax.dynamic_update_slice_in_dim(whole, grads, side * heads, 1)

    def gather_start(value):
        return value, flip(value, 2)

    def gather_end(value, far):
        both = jnp.concatenate([value, far], axis=1)
        return jnp.concatenate([both, flip(both, 1)], axis=1)

    low = ctx_size // 8

    def route_start(*values):
        columns = values[0].shape[0] // ctx_size
        split = jnp.stack(values).reshape(len(values), low, 2, 2, 2, columns, -1)
        return pick(split, far_bit, 2), flip(pick(split, 1 - far_bit, 2), 2)

    def route_end(mine, other):
        half = jnp.concatenate([mine, other], axis=5)
        return jnp.concatenate(
            [pick(half, core_bit, 2), flip(pick(half, 1 - core_bit, 2), 1)], axis=4
        )

    def weight_part(selected, source):
        return dot(selected, source, selected.ndim - 1, 1)

    low_bits = (ctx_size // 8).bit_length() - 1
    low_bit = lax.rem(ctx // REACH_PAIRS, 2)

    def first_leaving(routed, source):
        split = routed.reshape((routed.shape[0], low // 2, 2) + routed.shape[2:])
        return weight_part(pick(split, 1 - low_bit, 2), source).astype(bf16)

    def after_first(routed, source, arrived):
        split = routed.reshape((routed.shape[0], low // 2, 2) + routed.shape[2:])
        return (weight_part(pick(split, low_bit, 2), source) + arrived.astype(f32)).astype(bf16)

    def after_low(part):
        for k in range(1, low_bits):
            step = REACH_PAIRS << k
            bit = lax.rem(ctx // step, 2)
            split = part.reshape((part.shape[0], part.shape[1] // 2, 2) + part.shape[2:])
            arrived = flip(pick(split, 1 - bit, 2), step)
            part = (pick(split, bit, 2).astype(f32) + arrived.astype(f32)).astype(bf16)
        return pick(part[:, 0], side, 1), pick(part[:, 0], 1 - side, 1)

    same_side = side == ctx // (ctx_size // 2)

    def last_start(staying, arrived):
        mine = jnp.where(same_side, staying, arrived)
        return mine, flip(jnp.where(same_side, arrived, staying), ctx_size // 2)

    def last_end(mine, arrived):
        total = mine.astype(f32) + arrived.astype(f32)
        return total.reshape(-1, total.shape[-1])

    def halve(part, step):
        bit = lax.rem(ctx // step, 2)
        half = part.shape[0] // 2
        arrived = flip(lax.dynamic_slice_in_dim(part, (1 - bit) * half, half, 0), step)
        return lax.dynamic_slice_in_dim(part, bit * half, half, 0), arrived

    def halved(staying, arrived):
        total = staying.astype(f32) + arrived.astype(f32)
        return total if total.shape[0] == 1 else total.astype(bf16)

    def halving(part, step):
        while step < ctx_size:
            part = halved(*halve(part, step))
            step *= 2
        return part[0]

    enc_in, dec_in = enc_input.T, dec_input.T
    enc_arrived = swap(enc_in)
    dec_arrived = swap(dec_in)
    enc_pair = ordered(enc_in, enc_arrived)
    dec_pair = ordered(dec_in, dec_arrived)
    enc_normed = root_norm(enc_pair, enc_norm_attn).astype(bf16)
    dec_normed = root_norm(dec_pair, dec_norm_self).astype(bf16)

    def project(normed, *weights):
        made = [dot(w, normed, 0, 0).astype(bf16) for w in weights]
        return made[0] if len(made) == 1 else jnp.concatenate(made, axis=0)

    enc_kv = project(enc_normed, enc_key, enc_value)
    dec_kv = project(dec_normed, dec_key, dec_value)
    teacher_low = jnp.pad(
        jnp.concatenate([teacher.T, valid_mask.astype(f32)[None]], axis=0), ((0, 7), (0, 0))
    )
    enc_kv, enc_line, enc_back, dec_line, dec_back, teacher_low = together(
        enc_kv, enc_line, enc_back, dec_line, dec_back, teacher_low
    )
    enc_window, dec_window, enc_out_other = window_gather(
        1, [(enc_kv, BOTH), (dec_kv, BELOW)], [enc_out_proj]
    )
    enc_q = project(enc_normed, enc_query)
    dec_q = project(dec_normed, dec_query)

    enc_o, enc_att, enc_logs = attend(enc_q, enc_window, bounds_both, doc_lo, doc_hi, enc_line)
    enc_att_other = swap(enc_att)
    enc_att, dec_q = together(enc_att, dec_q)
    dec_o, dec_att, dec_logs = attend(dec_q, dec_window, bounds_below, doc_lo, positions, dec_line)
    dec_att_other = swap(dec_att)
    enc_att_other, dec_att, dec_out_here = together(enc_att_other, dec_att, dec_out_proj)
    dec_out_other = swap(dec_out_here)
    enc_mid = (
        enc_pair + dot(enc_out_proj, enc_att, 0, 0) + dot(enc_out_other, enc_att_other, 0, 0)
    )
    enc_ffn_in = root_norm(enc_mid, enc_norm_ff).astype(bf16)
    enc_weights = (enc_gate, enc_up, enc_down.T)
    partial, low_part, enc_hidden, enc_d1, enc_d2 = feed_forward(enc_ffn_in, enc_weights)
    low_part, dec_att, enc_hidden = together(low_part, dec_att, enc_hidden)
    branch = swap(low_part).astype(f32)

    enc_hidden_route = route_start(enc_hidden)
    dec_mid = (
        dec_pair + dot(dec_out_proj, dec_att, 0, 0) + dot(dec_out_other, dec_att_other, 0, 0)
    )
    cross_normed = root_norm(dec_mid, dec_norm_cross).astype(bf16)
    cross_q = project(cross_normed, cross_query)
    branch, cross_q = together(branch, cross_q)
    memory = (enc_mid + partial + branch).astype(bf16)
    cross_kv = project(memory, cross_key, cross_value)
    valid_count = jnp.broadcast_to(jnp.sum(valid_mask.astype(f32)), (8, 128))
    cross_window, cross_out_other, valid_tile = window_gather(
        2, [(cross_kv, BOTH)], [cross_out_proj], valid_count
    )
    cross_window, enc_ffn_in = together(cross_window, enc_ffn_in)
    enc_ffn_gather = gather_start(enc_ffn_in)
    valid_total = valid_tile[0, 0]
    scale = (rows * ctx_size) / valid_total
    cross_o, cross_att, cross_logs = attend(
        cross_q, cross_window, bounds_both, doc_lo, doc_hi, None
    )
    cross_att_other = swap(cross_att)
    cross_att, enc_hidden_route, teacher_low = together(cross_att, enc_hidden_route, teacher_low)
    teacher_other = swap(teacher_low)
    enc_hidden_routed = route_end(*enc_hidden_route)
    cross_att_other, enc_hidden_routed = together(cross_att_other, enc_hidden_routed)
    dec_cross = (
        dec_mid + dot(cross_out_proj, cross_att, 0, 0) + dot(cross_out_other, cross_att_other, 0, 0)
    )
    dec_ffn_in = root_norm(dec_cross, dec_norm_ff).astype(bf16)
    dec_ffn_gather = gather_start(dec_ffn_in)
    dec_weights = (dec_gate, dec_up, dec_down.T)
    partial, low_part, dec_hidden, dec_d1, dec_d2 = feed_forward(dec_ffn_in, dec_weights)
    low_part, dec_hidden, teacher_other, enc_ffn_gather = together(
        low_part, dec_hidden, teacher_other, enc_ffn_gather
    )
    mask_pair = ordered(valid_mask.astype(f32)[None], teacher_other[D : D + 1])
    branch = swap(low_part).astype(f32)
    dec_hidden_route = route_start(dec_hidden)
    teacher_pair = ordered(teacher.T, teacher_other[:D])
    before = dec_cross + partial - teacher_pair
    enc_ffn_all = gather_end(*enc_ffn_gather)
    branch, before, enc_ffn_all = together(branch, before, enc_ffn_all)

    difference = before + branch
    grad_seed = difference * (mask_pair * scale)

    dec_branch = grad_seed.astype(bf16)
    cross_key_here, dec_branch = together(cross_key, dec_branch)
    cross_key_other = swap(cross_key_here.T)
    partial, low_part, grad_gating, grad_upward = feed_backward(
        dec_branch, dec_weights, dec_d1, dec_d2
    )
    (
        low_part,
        grad_gating,
        grad_upward,
        dec_hidden_route,
        dec_ffn_gather,
        cross_key_other,
    ) = together(
        low_part, grad_gating, grad_upward, dec_hidden_route, dec_ffn_gather, cross_key_other
    )
    branch = swap(low_part).astype(f32)
    dec_gu_route = route_start(grad_gating, grad_upward)
    dec_hidden_routed = route_end(*dec_hidden_route)
    dec_ffn_all = gather_end(*dec_ffn_gather)
    dec_output = own(difference) + teacher.T
    branch, dec_hidden_routed, dec_ffn_all, dec_output = together(
        branch, dec_hidden_routed, dec_ffn_all, dec_output
    )
    part, g_dec_norm_ff = norm_backward(dec_cross, dec_norm_ff, partial + branch)
    grad_cross = grad_seed + part

    cross_branch = grad_cross.astype(bf16)
    qd, stats, cross_wide = prepare(cross_branch, cross_out_proj, cross_q, cross_o, cross_logs)
    qd_window, stat_window, cross_value_other = window_gather(
        3, [(qd, BOTH), (stats, BOTH)], [cross_value.T]
    )
    qd_window, dec_gu_route, dec_branch = together(qd_window, dec_gu_route, dec_branch)
    dec_branch_gather = gather_start(dec_branch)
    dec_gu_routed = route_end(*dec_gu_route)
    dec_gu_leaving = first_leaving(dec_gu_routed, dec_ffn_all)
    qd_window, dec_gu_leaving = together(qd_window, dec_gu_leaving)
    dec_gu_arrived = flip(dec_gu_leaving, REACH_PAIRS)
    cross_dkv = attend_keys(
        cross_kv, qd_window, stat_window, bounds_both, doc_lo, doc_hi, None
    )
    dkv_other = swap(cross_dkv)
    cross_dkv, qd, cross_query_here = together(cross_dkv, qd, cross_query)
    cross_query_other = swap(cross_query_here.T)
    (cross_dq,) = attend_queries(
        qd, cross_window, bounds_both, doc_lo, doc_hi, cross_wide, None
    )
    grad_memory = dot(cross_key, cross_dkv[:width]) + dot(cross_value, cross_dkv[width:])
    dkv_other, cross_dq, grad_memory = together(dkv_other, cross_dq, grad_memory)
    dq_other = swap(cross_dq)
    grad_memory = (
        grad_memory
        + dot(cross_key_other, dkv_other[:width], 0, 0)
        + dot(cross_value_other, dkv_other[width:], 0, 0)
    )

    memory_branch = grad_memory.astype(bf16)
    enc_branch_gather = gather_start(memory_branch)
    partial, low_part, grad_gating, grad_upward = feed_backward(
        memory_branch, enc_weights, enc_d1, enc_d2
    )
    low_part, grad_gating, grad_upward, dec_branch_gather, dq_other, cross_query_other = together(
        low_part, grad_gating, grad_upward, dec_branch_gather, dq_other, cross_query_other
    )
    branch = swap(low_part).astype(f32)
    enc_gu_route = route_start(grad_gating, grad_upward)

    dec_branch_all = gather_end(*dec_branch_gather)
    dec_down_leaving = first_leaving(dec_hidden_routed, dec_branch_all)
    grad_normed = dot(cross_query, cross_dq) + dot(cross_query_other, dq_other, 0, 0)
    part, g_dec_norm_cross = norm_backward(dec_mid, dec_norm_cross, grad_normed)
    grad_mid = grad_cross + part
    self_branch = grad_mid.astype(bf16)
    self_qd, self_stats, self_wide = prepare(self_branch, dec_out_proj, dec_q, dec_o, dec_logs)
    self_qd, dec_down_leaving, dec_gu_arrived = together(self_qd, dec_down_leaving, dec_gu_arrived)
    dec_down_arrived = flip(dec_down_leaving, REACH_PAIRS)
    dec_gu_kept, dec_gu_sent = after_low(after_first(dec_gu_routed, dec_ffn_all, dec_gu_arrived))
    cross_part = small_parts(
        ctx_size,
        width,
        side,
        [
            (
                [cross_dq, cross_dkv, cross_att],
                [dq_other, dkv_other, cross_att_other],
                [((0, 0), cross_normed), ((1, 2), memory), ((3, 3), cross_branch)],
            )
        ],
    )
    branch, dec_gu_sent, dec_gu_kept, cross_part = together(
        branch, dec_gu_sent, dec_gu_kept, cross_part
    )
    cross_half = halve(cross_part, 1)
    part, g_enc_norm_ff = norm_backward(enc_mid, enc_norm_ff, partial + branch)
    grad_enc_mid = grad_memory + part

    enc_branch = grad_enc_mid.astype(bf16)
    enc_qd, enc_stats, enc_wide = prepare(enc_branch, enc_out_proj, enc_q, enc_o, enc_logs)
    enc_qd_window, enc_stat_window, self_qd_window, self_stat_window, dec_gu_sent = window_gather(
        4,
        [(enc_qd, BOTH), (enc_stats, BOTH), (self_qd, ABOVE), (self_stats, ABOVE)],
        [dec_gu_sent],
    )
    dec_gu_last = last_start(dec_gu_kept, dec_gu_sent)
    enc_qd_window, enc_gu_route, dec_gu_mine, cross_half, dec_down_arrived = together(
        enc_qd_window, enc_gu_route, dec_gu_last[0], cross_half, dec_down_arrived
    )
    enc_gu_routed = route_end(*enc_gu_route)
    enc_gu_leaving = first_leaving(enc_gu_routed, enc_ffn_all)
    enc_qd_window, enc_gu_leaving = together(enc_qd_window, enc_gu_leaving)
    enc_gu_arrived = flip(enc_gu_leaving, REACH_PAIRS)
    enc_dkv = attend_keys(
        enc_kv, enc_qd_window, enc_stat_window, bounds_both, doc_lo, doc_hi, enc_back
    )
    enc_dkv, enc_qd = together(enc_dkv, enc_qd)
    enc_dq, enc_grad_line = attend_queries(
        enc_qd, enc_window, bounds_both, doc_lo, doc_hi, enc_wide, enc_line
    )
    enc_dq, self_qd_window = together(enc_dq, self_qd_window)
    self_dkv = attend_keys(
        dec_kv, self_qd_window, self_stat_window, bounds_above, positions, doc_hi, dec_back
    )
    self_dkv, self_qd = together(self_dkv, self_qd)
    self_dq, dec_grad_line = attend_queries(
        self_qd, dec_window, bounds_below, doc_lo, positions, self_wide, dec_line
    )
    (
        enc_dq, enc_dkv, self_dq, self_dkv, dec_gu_end, enc_gu_arrived, enc_branch_gather,
        cross_half,
    ) = together(
        enc_dq, enc_dkv, self_dq, self_dkv, dec_gu_last[1], enc_gu_arrived, enc_branch_gather,
        cross_half,
    )
    grads = jnp.concatenate([enc_dq, enc_dkv, self_dq, self_dkv], axis=0)
    grads_other = swap(grads)
    cross_half = halve(halved(*cross_half), 2)
    kinds_wide = (KINDS - 1) * width
    enc_partial = (
        dot(enc_query, enc_dq) + dot(enc_key, enc_dkv[:width]) + dot(enc_value, enc_dkv[width:])
    )
    self_partial = (
        dot(dec_query, self_dq) + dot(dec_key, self_dkv[:width]) + dot(dec_value, self_dkv[width:])
    )
    low_others = jnp.concatenate([others(enc_partial), others(self_partial)], axis=0).astype(bf16)
    grads, low_others, enc_gu_arrived, enc_branch_gather = together(
        grads, low_others, enc_gu_arrived, enc_branch_gather
    )
    low_arrived = swap(low_others)

    enc_gu_sum = after_first(enc_gu_routed, enc_ffn_all, enc_gu_arrived)
    dec_down_sum = after_first(dec_hidden_routed, dec_branch_all, dec_down_arrived)
    enc_branch_all = gather_end(*enc_branch_gather)
    enc_down_leaving = first_leaving(enc_hidden_routed, enc_branch_all)
    low_half = enc_hidden_routed.reshape((1, low // 2, 2) + enc_hidden_routed.shape[2:])
    enc_down_staying = weight_part(pick(low_half, low_bit, 2), enc_branch_all)
    dec_gu = last_end(dec_gu_mine, dec_gu_end)
    (
        grads, grads_other, enc_down_leaving, enc_down_staying, enc_gu_sum, dec_down_sum,
        dec_gu, cross_kept, cross_arrived,
    ) = together(
        grads, grads_other, enc_down_leaving, enc_down_staying, enc_gu_sum, dec_down_sum,
        dec_gu, cross_half[0], cross_half[1],
    )
    cross_half = halve(halved(cross_kept, cross_arrived), 4)
    attention_parts = [
        (
            [grads[:kinds_wide], enc_att],
            [grads_other[:kinds_wide], enc_att_other],
            [((0, 2), enc_normed), ((3, 3), enc_branch)],
        ),
        (
            [grads[kinds_wide:], dec_att],
            [grads_other[kinds_wide:], dec_att_other],
            [((0, 2), dec_normed), ((3, 3), self_branch)],
        ),
    ]
    if ctx_size == 16:
        both_part = small_parts(ctx_size, width, side, attention_parts)
        both_part, low_arrived, cross_kept, cross_arrived = together(
            both_part, low_arrived, cross_half[0], cross_half[1]
        )
        cross_half = halve(halved(cross_kept, cross_arrived), 8)
    partial_others = low_arrived.astype(f32)
    part, g_enc_norm_attn = norm_backward(
        enc_in, enc_norm_attn, own(enc_partial) + partial_others[:D]
    )
    grad_enc_input = own(grad_enc_mid) + part
    part, g_dec_norm_self = norm_backward(
        dec_in, dec_norm_self, own(self_partial) + partial_others[D:]
    )
    grad_dec_input = own(grad_mid) + part
    loss_part = jnp.sum(own(difference * difference * mask_pair))

    enc_bias_part = bucket_grads(enc_hot, enc_grad_line)
    dec_bias_part = bucket_grads(dec_hot, dec_grad_line)
    gains = jnp.concatenate(
        [
            g_enc_norm_attn,
            0.5 * g_enc_norm_ff,
            g_dec_norm_self,
            0.5 * g_dec_norm_cross,
            0.5 * g_dec_norm_ff,
        ]
    )
    small = jnp.concatenate(
        [
            gains,
            enc_bias_part.reshape(-1),
            dec_bias_part.reshape(-1),
            loss_part[None],
        ]
    )
    if ctx_size == 16:
        count = small.shape[0]
        padded = -(-count // 1024) * 1024
        small = jnp.pad(small, (0, padded - count)).reshape(8, padded // 8)
        columns = enc_down_leaving.shape[-2]
        both_part, small, cross_kept = together(both_part, small, cross_half[0])
        both_shard, enc_gu, enc_down_rows, dec_down_rows, small = last_exchanges(
            6,
            both_part,
            enc_gu_sum[:, 0].transpose(1, 0, 2, 3).reshape(2, 2 * columns, D),
            enc_down_leaving.reshape(2, columns, D),
            enc_down_staying.reshape(2, columns, D),
            dec_down_sum.reshape(2, columns, D),
            small,
        )
        small, cross_arrived = together(small, cross_half[1])
        small = small.reshape(-1)[:count]
        cross_shard = halved(cross_kept, cross_arrived)[0]
        enc_shard, self_shard = jnp.split(both_shard, 2, axis=0)
    else:
        small = total_over_devices(small, 7, ctx_size)
        enc_shard, self_shard = [
            halving(small_parts(ctx_size, width, side, [part]), 1) for part in attention_parts
        ]
        cross_shard = halving(halved(*cross_half), 8)

        def finished(part):
            kept, sent = after_low(part)
            return last_end(*last_start(kept, swap(sent)))

        enc_gu, dec_down_rows = finished(enc_gu_sum), finished(dec_down_sum)
        enc_down_first = flip(enc_down_leaving, REACH_PAIRS).astype(f32)
        enc_down_rows = finished((enc_down_staying + enc_down_first).astype(bf16))
    teacher_loss = small[-1] / (D * valid_total)
    gain = [small[i * D : (i + 1) * D] for i in range(5)]
    bias_size = enc_bias_part.size
    bias = [
        small[5 * D + i * bias_size : 5 * D + (i + 1) * bias_size].reshape(enc_bias_part.shape)
        for i in range(2)
    ]

    def pieces(shard, kinds):
        each = shard.shape[0] // len(kinds)
        made = []
        for i, transposed in enumerate(kinds):
            piece = shard[i * each : (i + 1) * each].astype(f32)
            made.append(piece.T if transposed else piece)
        return made

    dec_gate_up = pieces(dec_gu, (True, True))
    dec_down_g = pieces(dec_down_rows, (False,))
    enc_gate_up = pieces(enc_gu, (True, True))
    enc_down_g = pieces(enc_down_rows, (False,))
    kinds = (True, True, True, False)
    enc_attn = pieces(enc_shard, kinds)
    dec_attn = pieces(self_shard, kinds) + pieces(cross_shard, kinds)
    return (
        teacher_loss,
        dec_output.T,
        grad_enc_input.T,
        grad_dec_input.T,
        gain[0],
        *enc_attn,
        gain[1],
        *enc_gate_up,
        *enc_down_g,
        bias[0],
        gain[2],
        *dec_attn[:4],
        gain[3],
        *dec_attn[4:],
        gain[4],
        *dec_gate_up,
        *dec_down_g,
        bias[1],
    )


def solution(mesh):
    rows = P(("ctx", "fsdp"), None)
    split_columns = P(None, "fsdp")
    split_rows = P("fsdp", None)
    attention_in = (split_columns,) * 3 + (split_rows,)
    feed_in = (split_columns,) * 2 + (split_rows,)
    in_specs = (
        (rows,) * 3
        + (P(("ctx", "fsdp")), P(), P(), P())
        + (P(),)
        + attention_in
        + (P(),)
        + feed_in
        + (P(), P())
        + attention_in
        + (P(),)
        + attention_in
        + (P(),)
        + feed_in
        + (P(),)
    )
    columns = P(None, ("ctx", "fsdp"))
    attention_out = (columns,) * 3 + (rows,)
    feed_out = (columns,) * 2 + (rows,)
    out_specs = (
        (P(),)
        + (rows,) * 3
        + (P(),)
        + attention_out
        + (P(),)
        + feed_out
        + (P(), P())
        + attention_out
        + (P(),)
        + attention_out
        + (P(),)
        + feed_out
        + (P(),)
    )
    return jax.shard_map(body, mesh=mesh, in_specs=in_specs, out_specs=out_specs, check_vma=False)
```
